32 devices in a mesh: dp: 4 (over y, core), seq: 8 (over z, x).
Axes of the slice: x: 2, y: 2, z: 4, core: 2. Of those that a mesh axis runs over, the one named last changes fastest.
Arguments:
- tokens: bfloat16 [4, 8, 128, 1152], P('dp', 'seq'), may hold values from -6 to 6
- cond: float32 [4, 6, 1152], P('dp'), may hold values from -4 to 4
- d_out: bfloat16 [4, 8, 128, 1152], P('dp', 'seq'), may hold values from -6 to 6
- attn_in: bfloat16 [2, 3981312], P(None, ('dp', 'seq')), may hold values from -0.1875 to 0.1875
- attn_out: bfloat16 [2, 1327104], P(None, ('dp', 'seq')), may hold values from -0.375 to 0.375
- mlp_in: bfloat16 [2, 5308416], P(None, ('dp', 'seq')), may hold values from -0.1875 to 0.1875
- mlp_out: bfloat16 [2, 5308416], P(None, ('dp', 'seq')), may hold values from -0.09375 to 0.09375
- vectors: bfloat16 [2, 16128], P(None, ('dp', 'seq')), may hold values from -2 to 2
Outputs:
- output: float32 [4, 8, 128, 1152], P('dp', 'seq')
- d_tokens: float32 [4, 8, 128, 1152], P('dp', 'seq')
- d_cond: float32 [4, 6, 1152], P('dp')
- d_attn_in: float32 [2, 3981312], P(None, ('dp', 'seq'))
- d_attn_out: float32 [2, 1327104], P(None, ('dp', 'seq'))
- d_mlp_in: float32 [2, 5308416], P(None, ('dp', 'seq'))
- d_mlp_out: float32 [2, 5308416], P(None, ('dp', 'seq'))
- d_vectors: float32 [2, 16128], P(None, ('dp', 'seq'))
The draws below stay inside these ranges and needn't reach their ends.
All inputs are finite; a program needn't handle non-finite values.
Results may differ from the reference program's by a relative error of at most 0.025.
Values may be sent and summed in bfloat16 or wider, within the bound.
No kernel may reach another device: no remote copies, remote signals or barrier semaphores. Data moves between devices by JAX's collectives and lax.ppermute only.
A program may use at most 768 MiB of HBM per device.

```python
import jax
import jax.numpy as jnp
from jax import lax

D = 1152
HEADS = 16
HEAD_DIM = 72
FF = 4608
PLACES = 128
LAYERS = 2
FRAMES = 8
CLIPS = 4


def shard_levels(key, shape, split, smallest, high):
    loudness, own = 1.0, jax.random.fold_in(key, 6)
    for position, parts in split:
        draws = jnp.exp(jax.random.uniform(jax.random.fold_in(own, position), (parts,), jnp.float32, smallest / len(split), high / len(split)))
        loudness = loudness * jnp.repeat(draws, shape[position] // parts).reshape([-1 if axis == position else 1 for axis in range(len(shape))])
    return loudness


def gaussian(own_key, dims, spread, limit, split=(), held_as=jnp.bfloat16):
    values = spread * jax.random.normal(own_key, dims, jnp.float32)
    if split:
        values = values * shard_levels(own_key, dims, split, -0.22, 0.18)
    return jnp.clip(values, -limit, limit).astype(held_as)


def setup_inputs(seed: int = 0) -> dict:
    seeds = jax.random.split(jax.random.key(seed), 9)
    tokens = gaussian(seeds[0], (CLIPS, FRAMES, PLACES, D), 1.0, 6.0, ((0, 4), (1, 8)))
    cond = gaussian(seeds[1], (CLIPS, 6, D), 0.5, 4.0, ((0, 4),), jnp.float32)
    d_out = gaussian(seeds[2], (CLIPS, FRAMES, PLACES, D), 1.0, 6.0, ((0, 4), (1, 8)))
    attn_in = gaussian(seeds[3], (LAYERS, 3 * D * D), D ** -0.5, 0.1875, ((1, 32),))
    attn_out = gaussian(seeds[4], (LAYERS, D * D), (D // 4) ** -0.5, 0.375, ((1, 32),))
    mlp_in = gaussian(seeds[5], (LAYERS, D * FF), D ** -0.5, 0.1875, ((1, 32),))
    mlp_out = gaussian(seeds[6], (LAYERS, FF * D), FF ** -0.5, 0.09375, ((1, 32),))
    vectors = gaussian(seeds[7], (LAYERS, 10 * D + FF), 0.3, 2.0, ((1, 32),))
    return dict(tokens=tokens, cond=cond, d_out=d_out, attn_in=attn_in, attn_out=attn_out, mlp_in=mlp_in, mlp_out=mlp_out, vectors=vectors)


@jax.custom_vjp
def low(v):
    return lax.optimization_barrier(v.astype(jnp.bfloat16)).astype(jnp.float32)

@jax.custom_vjp
def low_back(v):
    return v

def low_keep(v):
    return (low(v), None)

def low_pass(kept, grad):
    return (grad,)

def back_keep(v):
    return (v, None)

def back_low(kept, grad):
    return (low(grad),)
low.defvjp(low_keep, low_pass)
low_back.defvjp(back_keep, back_low)

def matmul(former, latter):
    return jnp.dot(former, latter, precision=lax.Precision.HIGHEST, preferred_element_type=jnp.float32)

def modulate(tokens, scale, shift):
    average = lax.optimization_barrier(jnp.mean(tokens, axis=-1, keepdims=True))
    centred = tokens - average
    variance = lax.optimization_barrier(jnp.mean(centred * centred, axis=-1, keepdims=True))
    return centred * lax.rsqrt(variance + 1e-06) * (1.0 + scale) + shift

def attend(queries, key_heads, values, temporal):
    if temporal:
        score_form, mix_form = ('aibhe,ajbhe->abhij', 'abhij,ajbhe->aibhe')
    else:
        score_form, mix_form = ('abihe,abjhe->abhij', 'abhij,abjhe->abihe')
    scores = jnp.einsum(score_form, queries, key_heads, precision=lax.Precision.HIGHEST) * HEAD_DIM ** (-0.5)
    scores = low_back(scores)
    weights_soft = low(jax.nn.softmax(scores, axis=-1))
    return jnp.einsum(mix_form, weights_soft, values, precision=lax.Precision.HIGHEST)

def latte_block(tokens, cond, attn_in, attn_out, mlp_in, mlp_out, vector, temporal):
    w_qkv = attn_in.reshape(D, 3 * D)
    w_out = attn_out.reshape(D, D)
    w_one = mlp_in.reshape(D, FF)
    w_two = mlp_out.reshape(FF, D)
    bias_q = vector[0:D]
    bias_v = vector[D:2 * D]
    bias_o = vector[2 * D:3 * D]
    bias_one = vector[3 * D:3 * D + FF]
    bias_two = vector[3 * D + FF:4 * D + FF]
    modulation = vector[4 * D + FF:].reshape(6, D) + cond
    leading = tokens.shape[:-1]
    head_shape = leading + (HEADS, HEAD_DIM)
    hidden = low(modulate(tokens, modulation[1], modulation[0])).reshape(-1, D)
    packed = matmul(hidden, w_qkv)
    queries = low(low_back(packed[:, :D] + bias_q)).reshape(head_shape)
    key_heads = low(low_back(packed[:, D:2 * D])).reshape(head_shape)
    values = low(low_back(packed[:, 2 * D:] + bias_v)).reshape(head_shape)
    attended = low(low_back(attend(queries, key_heads, values, temporal))).reshape(-1, D)
    branch_one = low_back(matmul(attended, w_out) + bias_o).reshape(leading + (D,))
    middle = tokens + modulation[2] * branch_one
    hidden_two = low(modulate(middle, modulation[4], modulation[3])).reshape(-1, D)
    inner_sum = low_back(matmul(hidden_two, w_one) + bias_one)
    active = low(jax.nn.gelu(inner_sum, approximate=True))
    branch_two = low_back(matmul(active, w_two) + bias_two).reshape(leading + (D,))
    return middle + modulation[5] * branch_two

def forward(tokens, cond, attn_in, attn_out, mlp_in, mlp_out, vectors):
    for layer_index in range(LAYERS):
        tokens = latte_block(tokens, cond, attn_in[layer_index], attn_out[layer_index], mlp_in[layer_index], mlp_out[layer_index], vectors[layer_index], layer_index % 2 == 1)
    return tokens

def reference(tokens, cond, d_out, attn_in, attn_out, mlp_in, mlp_out, vectors):
    weight_list = tuple((member.astype(jnp.float32) for member in (attn_in, attn_out, mlp_in, mlp_out, vectors)))

    def one_clip(totals, inputs):
        clip_tokens, clip_cond, clip_grad = inputs
        result, backward = jax.vjp(forward, clip_tokens.astype(jnp.float32)[None], clip_cond, *weight_list)
        gradients = backward(clip_grad.astype(jnp.float32)[None])
        totals = tuple((former + latter for former, latter in zip(totals, gradients[2:])))
        return (totals, (result[0], gradients[0][0], gradients[1]))
    zero_sums = tuple((jnp.zeros_like(member) for member in weight_list))
    totals, stacked = lax.scan(one_clip, zero_sums, (tokens, cond, d_out))
    return (stacked[0], stacked[1], stacked[2], totals[0], totals[1], totals[2], totals[3], totals[4])
```

```python
import functools

import jax
import jax.numpy as jnp
from jax import lax
from jax.experimental import pallas as pl
from jax.experimental.pallas import tpu as pltpu
from jax.sharding import PartitionSpec as P

D = 1152
HEADS = 16
HEAD_DIM = 72
FF = 4608


EPSILON = 1e-06


def as_sent(x):

    def short(part):
        return part.astype(jnp.bfloat16) if part.dtype == jnp.float32 else part

    return jax.tree.map(short, x)


def modulate(tokens, scale, shift):
    average = jnp.mean(tokens, axis=-1, keepdims=True)
    centred = tokens - average
    variance = jnp.mean(centred * centred, axis=-1, keepdims=True)
    return centred * lax.rsqrt(variance + EPSILON) * (1.0 + scale) + shift


def plain_dot(former, latter):
    return jnp.dot(former, latter, preferred_element_type=jnp.float32)


def left_dot(former, latter):
    return lax.dot_general(
        former, latter, (((0,), (0,)), ((), ())), preferred_element_type=jnp.float32
    )


def right_dot(former, latter):
    return lax.dot_general(
        former, latter, (((1,), (1,)), ((), ())), preferred_element_type=jnp.float32
    )


def contract(form, former, latter):
    return jnp.einsum(form, former, latter, preferred_element_type=jnp.float32)


def einsum_forms(temporal):
    if temporal:
        return ("aibhe,ajbhe->abhij", "abhij,ajbhe->aibhe", "abhij,aibhe->ajbhe")
    return ("abihe,abjhe->abhij", "abhij,abjhe->abihe", "abhij,abihe->abjhe")


def unpack(pieces):
    attn_in, attn_out, mlp_in, mlp_out, vector = pieces
    vector = vector.astype(jnp.float32)
    return (
        attn_in.reshape(D, 3 * D),
        attn_out.reshape(D, D),
        mlp_in.reshape(D, FF),
        mlp_out.reshape(FF, D),
        vector[0:D],
        vector[D : 2 * D],
        vector[2 * D : 3 * D],
        vector[3 * D : 3 * D + FF],
        vector[3 * D + FF : 4 * D + FF],
        vector[4 * D + FF :].reshape(6, D),
    )


def tuple_of(shards, layer_index):
    return (
        shards[0][layer_index],
        shards[1][layer_index],
        shards[2][layer_index],
        shards[3][layer_index],
        shards[4][layer_index],
    )


def fetch_forward(shards, layer_index):
    return lax.all_gather(as_sent(tuple_of(shards, layer_index)), ("dp", "seq"), axis=0, tiled=True)


def piece_of(left, right):
    product = left_dot(left, right).reshape(-1)
    return product


def reduce_grads(factors, widths):
    (
        hidden,
        d_packed,
        attended,
        d_branch_one,
        hidden_two,
        d_inner,
        active,
        d_branch_two,
        d_vector,
    ) = factors
    pairs = (
        (hidden, d_packed),
        (attended, d_branch_one),
        (hidden_two, d_inner),
        (active, d_branch_two),
    )
    block = sum(widths)
    blocks_here = lax.axis_size(("dp", "seq")) * block // block
    members = []
    for (left, right), term_width in zip(pairs, widths[:4]):
        piece = piece_of(left, right)
        members.append(piece.reshape(blocks_here, term_width))
    members.append(d_vector.reshape(blocks_here, widths[4]))
    owned = lax.psum_scatter(
        jnp.concatenate(members, axis=1).reshape(-1), ("dp", "seq"), scatter_dimension=0, tiled=True
    )
    results = []
    position = 0
    for width in widths:
        results.append(owned[position : position + width])
        position = position + width
    return tuple(results)


def mod_rows(modulation):
    return [modulation[:, number][:, None, None, :] for number in range(6)]


def layer_forward(tokens, cond, weight_set, temporal):
    w_qkv, w_out, w_one, w_two, bias_q, bias_v, bias_o, bias_one, bias_two, table = weight_set
    modulation = table[None] + cond
    rows_mod = mod_rows(modulation)
    leading = tokens.shape[:-1]
    head_shape = leading + (HEADS, HEAD_DIM)
    hidden = modulate(tokens, rows_mod[1], rows_mod[0]).astype(jnp.bfloat16).reshape(-1, D)
    packed = plain_dot(hidden, w_qkv)
    queries = (packed[:, :D] + bias_q).astype(jnp.bfloat16).reshape(head_shape)
    key_heads = packed[:, D : 2 * D].astype(jnp.bfloat16).reshape(head_shape)
    values = (packed[:, 2 * D :] + bias_v).astype(jnp.bfloat16).reshape(head_shape)
    score_form, mix_form, back_form = einsum_forms(temporal)
    scores = contract(score_form, queries, key_heads) * HEAD_DIM ** (-0.5)
    row_peak = jnp.max(scores, axis=-1, keepdims=True)
    exponent = jnp.exp(scores - row_peak)
    row_total = jnp.sum(exponent, axis=-1, keepdims=True)
    weights_soft = exponent / row_total
    log_total = row_peak + jnp.log(row_total)
    attended = (
        contract(mix_form, weights_soft.astype(jnp.bfloat16), values)
        .astype(jnp.bfloat16)
        .reshape(-1, D)
    )
    branch_one = (plain_dot(attended, w_out) + bias_o).reshape(leading + (D,))
    middle = tokens + rows_mod[2] * branch_one
    hidden_two = modulate(middle, rows_mod[4], rows_mod[3]).astype(jnp.bfloat16).reshape(-1, D)
    inner_sum = plain_dot(hidden_two, w_one) + bias_one
    active = jax.nn.gelu(inner_sum, approximate=True).astype(jnp.bfloat16)
    branch_two = (plain_dot(active, w_two) + bias_two).reshape(leading + (D,))
    result = middle + rows_mod[5] * branch_two
    stored = (
        tokens,
        modulation,
        hidden,
        queries,
        key_heads,
        values,
        log_total,
        attended,
        branch_one,
        middle,
        hidden_two,
        inner_sum,
        active,
        branch_two,
    )
    return (result, stored)


def layer_backward(grad_out, stored, weight_set, temporal):
    w_qkv, w_out, w_one, w_two = (weight_set[0], weight_set[1], weight_set[2], weight_set[3])
    (
        tokens,
        modulation,
        hidden,
        queries,
        key_heads,
        values,
        log_total,
        attended,
        branch_one,
        middle,
        hidden_two,
        inner_sum,
        active,
        branch_two,
    ) = stored
    rows_mod = mod_rows(modulation)
    leading = tokens.shape[:-1]
    clips_here = tokens.shape[0]
    d_gate_two = jnp.sum(grad_out * branch_two, axis=(1, 2))
    d_branch_two = (rows_mod[5] * grad_out).astype(jnp.bfloat16).reshape(-1, D)
    d_bias_two = jnp.sum(d_branch_two, axis=0, dtype=jnp.float32)
    d_active = right_dot(d_branch_two, w_two)
    unused_gelu, gelu_back = jax.vjp(
        lambda entries: jax.nn.gelu(entries, approximate=True), inner_sum
    )
    d_inner = gelu_back(d_active)[0].astype(jnp.bfloat16)
    d_bias_one = jnp.sum(d_inner, axis=0, dtype=jnp.float32)
    d_hidden_two = right_dot(d_inner, w_one).reshape(leading + (D,))
    unused_norm, norm_back = jax.vjp(modulate, middle, rows_mod[4], rows_mod[3])
    d_middle, d_scale_two, d_shift_two = norm_back(d_hidden_two)
    grad_mid = grad_out + d_middle
    d_gate_one = jnp.sum(grad_mid * branch_one, axis=(1, 2))
    d_branch_one = (rows_mod[2] * grad_mid).astype(jnp.bfloat16).reshape(-1, D)
    d_bias_o = jnp.sum(d_branch_one, axis=0, dtype=jnp.float32)
    d_attended = (
        right_dot(d_branch_one, w_out).astype(jnp.bfloat16).reshape(leading + (HEADS, HEAD_DIM))
    )
    score_form, mix_form, back_form = einsum_forms(temporal)
    scale_qk = HEAD_DIM ** (-0.5)
    scores = contract(score_form, queries, key_heads) * scale_qk
    weights_soft = jnp.exp(scores - log_total)
    d_values = contract(back_form, weights_soft.astype(jnp.bfloat16), d_attended)
    d_probs = contract(score_form, d_attended, values)
    d_scores = weights_soft * (d_probs - jnp.sum(weights_soft * d_probs, axis=-1, keepdims=True))
    d_scores = d_scores.astype(jnp.bfloat16)
    d_queries = contract(mix_form, d_scores, key_heads) * scale_qk
    d_keys = contract(back_form, d_scores, queries) * scale_qk
    d_packed = jnp.concatenate(
        [
            d_queries.reshape(-1, D).astype(jnp.bfloat16),
            d_keys.reshape(-1, D).astype(jnp.bfloat16),
            d_values.reshape(-1, D).astype(jnp.bfloat16),
        ],
        axis=1,
    )
    d_bias_q = jnp.sum(d_packed[:, :D], axis=0, dtype=jnp.float32)
    d_bias_v = jnp.sum(d_packed[:, 2 * D :], axis=0, dtype=jnp.float32)
    d_hidden = right_dot(d_packed, w_qkv).reshape(leading + (D,))
    unused_first, first_back = jax.vjp(modulate, tokens, rows_mod[1], rows_mod[0])
    d_input, d_scale_one, d_shift_one = first_back(d_hidden)
    d_input = grad_mid + d_input
    d_modulation = jnp.stack(
        [
            d_shift_one.reshape(clips_here, D),
            d_scale_one.reshape(clips_here, D),
            d_gate_one,
            d_shift_two.reshape(clips_here, D),
            d_scale_two.reshape(clips_here, D),
            d_gate_two,
        ],
        axis=1,
    )
    d_vector = jnp.concatenate(
        [
            d_bias_q,
            d_bias_v,
            d_bias_o,
            d_bias_one,
            d_bias_two,
            jnp.sum(d_modulation, axis=0).reshape(-1),
        ]
    )
    factors = (
        hidden,
        d_packed,
        attended,
        d_branch_one,
        hidden_two,
        d_inner,
        active,
        d_branch_two,
        d_vector,
    )
    return (d_input, factors, d_modulation)


def swap_dp(x, k):
    return lax.ppermute(x, "dp", [(i, i ^ k) for i in range(4)])


def gather_dp(x):
    far = swap_dp(x, 2)
    return jnp.concatenate([x, swap_dp(x, 1), far, swap_dp(far, 1)], axis=0)


def scatter_dp(partial):
    quarters = partial.reshape((4, -1) + partial.shape[1:])
    sent = jnp.stack([quarters[1], quarters[3]]).astype(jnp.bfloat16)
    got = swap_dp(sent, 1).astype(jnp.float32)
    far = swap_dp((quarters[2] + got[1]).astype(jnp.bfloat16), 2)
    return quarters[0] + got[0] + far.astype(jnp.float32)


def fetch_columns(shard, groups, n_dp):
    rows = D // (n_dp * lax.axis_size("seq"))
    parts = shard.reshape(rows, groups, n_dp, -1).transpose(2, 0, 1, 3).reshape(n_dp, rows, -1)
    mine = lax.all_to_all(parts, "dp", split_axis=0, concat_axis=0, tiled=True)
    return lax.all_gather(mine, "seq", axis=1).reshape(D, -1)


def fetch_rows(shard):
    return lax.all_gather(shard.reshape(-1, D), "seq", axis=0, tiled=True)


def pick(x, index):
    return lax.dynamic_index_in_dim(x, index, 0, keepdims=False)


def scatter_seq(blocks):
    n_seq = blocks.shape[0]
    n_z = n_seq // 2
    here = lax.axis_index("seq")
    z, x = here // 2, here % 2
    blocks = blocks.reshape((n_z, 2) + blocks.shape[1:])
    mine = lax.dynamic_index_in_dim(blocks, x, 1, keepdims=False)
    other = lax.dynamic_index_in_dim(blocks, 1 - x, 1, keepdims=False)
    got = lax.ppermute(other, "seq", [(i, i ^ 1) for i in range(n_seq)])
    pair = (mine.astype(jnp.float32) + got.astype(jnp.float32)).astype(jnp.bfloat16)
    total = pick(pair, z).astype(jnp.float32)
    for k in range(1, n_z):
        to = [(i, (i + 2 * k) % n_seq) for i in range(n_seq)]
        arrived = lax.ppermute(pick(pair, (z + k) % n_z), "seq", to)
        total = total + arrived.astype(jnp.float32)
    return total


def return_columns(grad, groups, n_dp):
    n_seq = lax.axis_size("seq")
    blocks = grad.astype(jnp.bfloat16).reshape(n_dp, n_seq, -1, grad.shape[1])
    mine = scatter_seq(blocks.transpose(1, 0, 2, 3)).astype(jnp.bfloat16)
    parts = lax.all_to_all(mine, "dp", split_axis=0, concat_axis=0, tiled=True)
    rows = parts.shape[1]
    parts = parts.astype(jnp.float32).reshape(n_dp, rows, groups, -1)
    return parts.transpose(1, 2, 0, 3).reshape(-1)


def return_rows(grad):
    n_seq = lax.axis_size("seq")
    return scatter_seq(grad.astype(jnp.bfloat16).reshape(n_seq, -1, D)).reshape(-1)


def softmax_of(scores, period):
    if period:
        row = lax.broadcasted_iota(jnp.int32, scores.shape, 0) % period
        column = lax.broadcasted_iota(jnp.int32, scores.shape, 1) % period
        scores = jnp.where(row == column, scores, -1e30)
    exponent = jnp.exp(scores - jnp.max(scores, axis=-1, keepdims=True))
    return exponent / jnp.sum(exponent, axis=-1, keepdims=True)


def attend_kernel(period, heads, packed_ref, mixed_ref):
    width = heads * HEAD_DIM
    queries = packed_ref[:, 0:width]
    key_heads = packed_ref[:, width : 2 * width]
    values = packed_ref[:, 2 * width : 3 * width]
    owner = lax.broadcasted_iota(jnp.int32, (1, width), 1) // HEAD_DIM
    mixed = jnp.zeros(queries.shape, jnp.float32)
    for head in range(heads):
        mine = owner == head
        scores = right_dot(jnp.where(mine, queries, 0), key_heads) * HEAD_DIM ** (-0.5)
        weights_soft = softmax_of(scores, period).astype(jnp.bfloat16)
        mixed = jnp.where(mine, plain_dot(weights_soft, values), mixed)
    mixed_ref[...] = mixed.astype(jnp.bfloat16)


def attend_back_kernel(period, heads, packed_ref, d_mixed_ref, d_packed_ref):
    width = heads * HEAD_DIM
    queries = packed_ref[:, 0:width]
    key_heads = packed_ref[:, width : 2 * width]
    values = packed_ref[:, 2 * width : 3 * width]
    d_mixed = d_mixed_ref[...]
    owner = lax.broadcasted_iota(jnp.int32, (1, width), 1) // HEAD_DIM
    scale = HEAD_DIM ** (-0.5)
    d_queries = jnp.zeros(queries.shape, jnp.float32)
    d_keys = d_queries
    d_values = d_queries
    for head in range(heads):
        mine = owner == head
        scores = right_dot(jnp.where(mine, queries, 0), key_heads) * scale
        weights_soft = softmax_of(scores, period)
        d_values = jnp.where(mine, left_dot(weights_soft.astype(jnp.bfloat16), d_mixed), d_values)
        d_probs = right_dot(jnp.where(mine, d_mixed, 0), values)
        inner = jnp.sum(weights_soft * d_probs, axis=-1, keepdims=True)
        d_scores = (weights_soft * (d_probs - inner)).astype(jnp.bfloat16)
        d_queries = jnp.where(mine, plain_dot(d_scores, key_heads), d_queries)
        d_keys = jnp.where(mine, left_dot(d_scores, queries), d_keys)
    d_packed_ref[...] = jnp.concatenate(
        [d_queries * scale, d_keys * scale, d_values], axis=1
    ).astype(jnp.bfloat16)


def attend(packed, period, heads, group):
    width = heads * HEAD_DIM
    count = packed.shape[0] // group
    return pl.pallas_call(
        functools.partial(attend_kernel, period, heads),
        out_shape=jax.ShapeDtypeStruct((packed.shape[0], width), jnp.bfloat16),
        grid=(count,),
        in_specs=[pl.BlockSpec((group, 3 * width), lambda i: (i, 0))],
        out_specs=pl.BlockSpec((group, width), lambda i: (i, 0)),
        cost_estimate=pl.CostEstimate(
            flops=4 * count * heads * group * group * width,
            bytes_accessed=packed.size * 3,
            transcendentals=count * heads * group * group,
        ),
    )(packed)


def attend_back(packed, d_mixed, period, heads, group):
    width = heads * HEAD_DIM
    count = packed.shape[0] // group
    return pl.pallas_call(
        functools.partial(attend_back_kernel, period, heads),
        out_shape=jax.ShapeDtypeStruct(packed.shape, jnp.bfloat16),
        grid=(count,),
        in_specs=[
            pl.BlockSpec((group, 3 * width), lambda i: (i, 0)),
            pl.BlockSpec((group, width), lambda i: (i, 0)),
        ],
        out_specs=pl.BlockSpec((group, 3 * width), lambda i: (i, 0)),
        cost_estimate=pl.CostEstimate(
            flops=10 * count * heads * group * group * width,
            bytes_accessed=packed.size * 6,
            transcendentals=count * heads * group * group,
        ),
    )(packed, d_mixed)


def gelu(entries):
    return jax.nn.gelu(entries, approximate=True)


def block_forward(tokens, modulation, weight_set, period, heads):
    w_qkv, w_out, w_one, w_two, bias_qkv, bias_o, bias_one, bias_two = weight_set
    hidden = modulate(tokens, modulation[1], modulation[0]).astype(jnp.bfloat16)
    hidden = gather_dp(hidden)
    packed = (plain_dot(hidden, w_qkv) + bias_qkv).astype(jnp.bfloat16)
    attended = attend(packed, period, heads, tokens.shape[0])
    branch_one = scatter_dp(plain_dot(attended, w_out)) + bias_o
    middle = tokens + modulation[2] * branch_one
    hidden_two = modulate(middle, modulation[4], modulation[3]).astype(jnp.bfloat16)
    hidden_two = gather_dp(hidden_two)
    inner_sum = plain_dot(hidden_two, w_one) + bias_one
    active = gelu(inner_sum).astype(jnp.bfloat16)
    branch_two = scatter_dp(plain_dot(active, w_two)) + bias_two
    result = middle + modulation[5] * branch_two
    stored = (
        tokens,
        hidden,
        packed,
        attended,
        branch_one,
        middle,
        hidden_two,
        inner_sum,
        active,
        branch_two,
    )
    return result, stored


def column_sums(x):
    return jnp.sum(x, axis=0, dtype=jnp.float32)


def block_backward(grad_out, modulation, stored, weight_set, period, heads):
    w_qkv, w_out, w_one, w_two = weight_set[:4]
    (
        tokens,
        hidden,
        packed,
        attended,
        branch_one,
        middle,
        hidden_two,
        inner_sum,
        active,
        branch_two,
    ) = stored
    d_gate_two = column_sums(grad_out * branch_two)
    d_branch_two = (modulation[5] * grad_out).astype(jnp.bfloat16)
    d_bias_two = column_sums(d_branch_two)
    d_branch_two = gather_dp(d_branch_two)
    d_active = right_dot(d_branch_two, w_two)
    d_inner = jax.vjp(gelu, inner_sum)[1](d_active)[0].astype(jnp.bfloat16)
    d_bias_one = column_sums(d_inner)
    d_w_two = left_dot(active, d_branch_two)
    d_hidden_two = scatter_dp(right_dot(d_inner, w_one))
    d_w_one = left_dot(hidden_two, d_inner)
    norm_back = jax.vjp(modulate, middle, modulation[4], modulation[3])[1]
    d_middle, d_scale_two, d_shift_two = norm_back(d_hidden_two)
    grad_mid = grad_out + d_middle
    d_gate_one = column_sums(grad_mid * branch_one)
    d_branch_one = (modulation[2] * grad_mid).astype(jnp.bfloat16)
    d_bias_o = column_sums(d_branch_one)
    d_branch_one = gather_dp(d_branch_one)
    d_attended = right_dot(d_branch_one, w_out).astype(jnp.bfloat16)
    d_w_out = left_dot(attended, d_branch_one)
    d_packed = attend_back(packed, d_attended, period, heads, tokens.shape[0])
    d_bias_qkv = column_sums(d_packed)
    d_hidden = scatter_dp(right_dot(d_packed, w_qkv))
    d_w_qkv = left_dot(hidden, d_packed)
    first_back = jax.vjp(modulate, tokens, modulation[1], modulation[0])[1]
    d_input, d_scale_one, d_shift_one = first_back(d_hidden)
    d_input = grad_mid + d_input
    d_modulation = jnp.stack(
        [d_shift_one, d_scale_one, d_gate_one, d_shift_two, d_scale_two, d_gate_two]
    )
    d_vectors = (d_bias_qkv, d_bias_o, d_bias_one, d_bias_two, d_modulation)
    return d_input, (d_w_qkv, d_w_out, d_w_one, d_w_two), d_vectors


def slice_of(vector, n_dp):
    width = vector.shape[0] // n_dp
    return lax.dynamic_slice(vector, (lax.axis_index("dp") * width,), (width,))


def place_slice(piece, n_dp):
    zeros = jnp.zeros((piece.shape[0] * n_dp,), piece.dtype)
    return lax.dynamic_update_slice(zeros, piece, (lax.axis_index("dp") * piece.shape[0],))


def on_device_split(tokens, cond, d_out, attn_in, attn_out, mlp_in, mlp_out, vectors):
    n_dp = lax.axis_size("dp")
    n_seq = lax.axis_size("seq")
    heads = HEADS // n_dp
    width = heads * HEAD_DIM
    frames, places = tokens.shape[1] * n_seq, tokens.shape[2]
    period = places // n_seq
    everyone = lax.all_gather(vectors, ("dp", "seq"), axis=1, tiled=True).astype(jnp.float32)
    weight_sets, modulations = [], []
    for index in range(2):
        vector = everyone[index]
        bias_q = slice_of(vector[0:D], n_dp)
        bias_v = slice_of(vector[D : 2 * D], n_dp)
        weight_sets.append(
            (
                fetch_columns(attn_in[index], 3, n_dp),
                fetch_rows(attn_out[index]),
                fetch_columns(mlp_in[index], 1, n_dp),
                fetch_rows(mlp_out[index]),
                jnp.concatenate([bias_q, jnp.zeros_like(bias_q), bias_v]),
                vector[2 * D : 3 * D],
                slice_of(vector[3 * D : 3 * D + FF], n_dp),
                vector[3 * D + FF : 4 * D + FF],
            )
        )
        modulations.append(vector[4 * D + FF :].reshape(6, D) + cond[0])

    def to_places(x):
        x = x.reshape(1, frames // n_seq, places, D)
        x = lax.all_to_all(x, "seq", split_axis=2, concat_axis=1, tiled=True)
        return x.reshape(-1, D).astype(jnp.float32)

    def to_frames(x):
        x = x.astype(jnp.bfloat16).reshape(1, frames, period, D)
        x = lax.all_to_all(x, "seq", split_axis=1, concat_axis=2, tiled=True)
        return x.reshape(-1, D).astype(jnp.float32)

    grad_places = to_places(d_out)
    spatial_out, stored_zero = block_forward(
        tokens.reshape(-1, D).astype(jnp.float32), modulations[0], weight_sets[0], 0, heads
    )
    temporal_out, stored_one = block_forward(
        to_places(spatial_out.astype(jnp.bfloat16)), modulations[1], weight_sets[1], period, heads
    )
    output = to_frames(temporal_out)
    grad_mid, weight_grads_one, vector_grads_one = block_backward(
        grad_places, modulations[1], stored_one, weight_sets[1], period, heads
    )
    grad_frames = to_frames(grad_mid)
    d_tokens, weight_grads_zero, vector_grads_zero = block_backward(
        grad_frames, modulations[0], stored_zero, weight_sets[0], 0, heads
    )
    owned = []
    for weight_grads in (weight_grads_zero, weight_grads_one):
        owned.append(
            (
                return_columns(weight_grads[0], 3, n_dp),
                return_rows(weight_grads[1]),
                return_columns(weight_grads[2], 1, n_dp),
                return_rows(weight_grads[3]),
            )
        )
    vector_rows = []
    for d_bias_qkv, d_bias_o, d_bias_one, d_bias_two, d_modulation in (
        vector_grads_zero,
        vector_grads_one,
    ):
        vector_rows.append(
            jnp.concatenate(
                [
                    place_slice(d_bias_qkv[:width], n_dp),
                    place_slice(d_bias_qkv[2 * width :], n_dp),
                    d_bias_o,
                    place_slice(d_bias_one, n_dp),
                    d_bias_two,
                    d_modulation.reshape(-1),
                ]
            )
        )
    d_vectors = lax.psum_scatter(
        jnp.stack(vector_rows), ("dp", "seq"), scatter_dimension=1, tiled=True
    )
    d_cond = lax.psum(vector_grads_zero[4] + vector_grads_one[4], "seq")[None]
    stacked = tuple(jnp.stack(pair) for pair in zip(*owned))
    return (
        output.reshape(tokens.shape),
        d_tokens.reshape(tokens.shape),
        d_cond,
        *stacked,
        d_vectors,
    )


def on_device(tokens, cond, d_out, attn_in, attn_out, mlp_in, mlp_out, vectors):
    shards = (attn_in, attn_out, mlp_in, mlp_out, vectors)
    widths = (
        attn_in.shape[1],
        attn_out.shape[1],
        mlp_in.shape[1],
        mlp_out.shape[1],
        vectors.shape[1],
    )
    layer_zero = unpack(fetch_forward(shards, 0))
    spatial_out, stored_zero = layer_forward(tokens.astype(jnp.float32), cond, layer_zero, False)
    by_place = lax.all_to_all(
        spatial_out.astype(jnp.bfloat16), "seq", split_axis=2, concat_axis=1, tiled=True
    ).astype(spatial_out.dtype)
    layer_one = unpack(fetch_forward(shards, 1))
    temporal_out, stored_one = layer_forward(by_place, cond, layer_one, True)
    output = lax.all_to_all(
        temporal_out.astype(jnp.bfloat16), "seq", split_axis=1, concat_axis=2, tiled=True
    ).astype(temporal_out.dtype)
    grad_places = lax.all_to_all(d_out, "seq", split_axis=2, concat_axis=1, tiled=True).astype(
        jnp.float32
    )
    grad_mid, factors_one, modul_one = layer_backward(grad_places, stored_one, layer_one, True)
    owned_one = reduce_grads(factors_one, widths)
    grad_frames = lax.all_to_all(
        grad_mid.astype(jnp.bfloat16), "seq", split_axis=1, concat_axis=2, tiled=True
    ).astype(grad_mid.dtype)
    d_tokens, factors_zero, modul_zero = layer_backward(grad_frames, stored_zero, layer_zero, False)
    owned_zero = reduce_grads(factors_zero, widths)
    d_cond = lax.psum(modul_zero + modul_one, "seq")
    stacked = tuple((jnp.stack([former, latter]) for former, latter in zip(owned_zero, owned_one)))
    return (output, d_tokens, d_cond, stacked[0], stacked[1], stacked[2], stacked[3], stacked[4])


def solution(mesh):
    in_specs = (
        P("dp", "seq", None, None),
        P("dp", None, None),
        P("dp", "seq", None, None),
        P(None, ("dp", "seq")),
        P(None, ("dp", "seq")),
        P(None, ("dp", "seq")),
        P(None, ("dp", "seq")),
        P(None, ("dp", "seq")),
    )
    out_specs = (
        P("dp", "seq", None, None),
        P("dp", "seq", None, None),
        P("dp", None, None),
        P(None, ("dp", "seq")),
        P(None, ("dp", "seq")),
        P(None, ("dp", "seq")),
        P(None, ("dp", "seq")),
        P(None, ("dp", "seq")),
    )
    n_dp, n_seq = mesh.shape["dp"], mesh.shape["seq"]
    split = n_dp == 4 and n_seq == 8
    return jax.shard_map(
        on_device_split if split else on_device, mesh=mesh, in_specs=in_specs, out_specs=out_specs, check_vma=False
    )
```

```python
import functools

import jax
import jax.numpy as jnp
from jax import lax
from jax.experimental import pallas as pl
from jax.experimental.pallas import tpu as pltpu
from jax.sharding import PartitionSpec as P

D = 1152
HEADS = 16
HEAD_DIM = 72
FF = 4608


EPSILON = 1e-06


def as_sent(x):

    def short(part):
        return part.astype(jnp.bfloat16) if part.dtype == jnp.float32 else part

    return jax.tree.map(short, x)


def modulate(tokens, scale, shift):
    average = jnp.mean(tokens, axis=-1, keepdims=True)
    centred = tokens - average
    variance = jnp.mean(centred * centred, axis=-1, keepdims=True)
    return centred * lax.rsqrt(variance + EPSILON) * (1.0 + scale) + shift


def plain_dot(former, latter):
    return jnp.dot(former, latter, preferred_element_type=jnp.float32)


def left_dot(former, latter):
    return lax.dot_general(
        former, latter, (((0,), (0,)), ((), ())), preferred_element_type=jnp.float32
    )


def right_dot(former, latter):
    return lax.dot_general(
        former, latter, (((1,), (1,)), ((), ())), preferred_element_type=jnp.float32
    )


def contract(form, former, latter):
    return jnp.einsum(form, former, latter, preferred_element_type=jnp.float32)


def einsum_forms(temporal):
    if temporal:
        return ("aibhe,ajbhe->abhij", "abhij,ajbhe->aibhe", "abhij,aibhe->ajbhe")
    return ("abihe,abjhe->abhij", "abhij,abjhe->abihe", "abhij,abihe->abjhe")


def unpack(pieces):
    attn_in, attn_out, mlp_in, mlp_out, vector = pieces
    vector = vector.astype(jnp.float32)
    return (
        attn_in.reshape(D, 3 * D),
        attn_out.reshape(D, D),
        mlp_in.reshape(D, FF),
        mlp_out.reshape(FF, D),
        vector[0:D],
        vector[D : 2 * D],
        vector[2 * D : 3 * D],
        vector[3 * D : 3 * D + FF],
        vector[3 * D + FF : 4 * D + FF],
        vector[4 * D + FF :].reshape(6, D),
    )


def tuple_of(shards, layer_index):
    return (
        shards[0][layer_index],
        shards[1][layer_index],
        shards[2][layer_index],
        shards[3][layer_index],
        shards[4][layer_index],
    )


def fetch_forward(shards, layer_index):
    return lax.all_gather(as_sent(tuple_of(shards, layer_index)), ("dp", "seq"), axis=0, tiled=True)


def piece_of(left, right):
    product = left_dot(left, right).reshape(-1)
    return product


def reduce_grads(factors, widths):
    (
        hidden,
        d_packed,
        attended,
        d_branch_one,
        hidden_two,
        d_inner,
        active,
        d_branch_two,
        d_vector,
    ) = factors
    pairs = (
        (hidden, d_packed),
        (attended, d_branch_one),
        (hidden_two, d_inner),
        (active, d_branch_two),
    )
    block = sum(widths)
    blocks_here = lax.axis_size(("dp", "seq")) * block // block
    members = []
    for (left, right), term_width in zip(pairs, widths[:4]):
        piece = piece_of(left, right)
        members.append(piece.reshape(blocks_here, term_width))
    members.append(d_vector.reshape(blocks_here, widths[4]))
    owned = lax.psum_scatter(
        jnp.concatenate(members, axis=1).reshape(-1), ("dp", "seq"), scatter_dimension=0, tiled=True
    )
    results = []
    position = 0
    for width in widths:
        results.append(owned[position : position + width])
        position = position + width
    return tuple(results)


def mod_rows(modulation):
    return [modulation[:, number][:, None, None, :] for number in range(6)]


def layer_forward(tokens, cond, weight_set, temporal):
    w_qkv, w_out, w_one, w_two, bias_q, bias_v, bias_o, bias_one, bias_two, table = weight_set
    modulation = table[None] + cond
    rows_mod = mod_rows(modulation)
    leading = tokens.shape[:-1]
    head_shape = leading + (HEADS, HEAD_DIM)
    hidden = modulate(tokens, rows_mod[1], rows_mod[0]).astype(jnp.bfloat16).reshape(-1, D)
    packed = plain_dot(hidden, w_qkv)
    queries = (packed[:, :D] + bias_q).astype(jnp.bfloat16).reshape(head_shape)
    key_heads = packed[:, D : 2 * D].astype(jnp.bfloat16).reshape(head_shape)
    values = (packed[:, 2 * D :] + bias_v).astype(jnp.bfloat16).reshape(head_shape)
    score_form, mix_form, back_form = einsum_forms(temporal)
    scores = contract(score_form, queries, key_heads) * HEAD_DIM ** (-0.5)
    row_peak = jnp.max(scores, axis=-1, keepdims=True)
    exponent = jnp.exp(scores - row_peak)
    row_total = jnp.sum(exponent, axis=-1, keepdims=True)
    weights_soft = exponent / row_total
    log_total = row_peak + jnp.log(row_total)
    attended = (
        contract(mix_form, weights_soft.astype(jnp.bfloat16), values)
        .astype(jnp.bfloat16)
        .reshape(-1, D)
    )
    branch_one = (plain_dot(attended, w_out) + bias_o).reshape(leading + (D,))
    middle = tokens + rows_mod[2] * branch_one
    hidden_two = modulate(middle, rows_mod[4], rows_mod[3]).astype(jnp.bfloat16).reshape(-1, D)
    inner_sum = plain_dot(hidden_two, w_one) + bias_one
    active = jax.nn.gelu(inner_sum, approximate=True).astype(jnp.bfloat16)
    branch_two = (plain_dot(active, w_two) + bias_two).reshape(leading + (D,))
    result = middle + rows_mod[5] * branch_two
    stored = (
        tokens,
        modulation,
        hidden,
        queries,
        key_heads,
        values,
        log_total,
        attended,
        branch_one,
        middle,
        hidden_two,
        inner_sum,
        active,
        branch_two,
    )
    return (result, stored)


def layer_backward(grad_out, stored, weight_set, temporal):
    w_qkv, w_out, w_one, w_two = (weight_set[0], weight_set[1], weight_set[2], weight_set[3])
    (
        tokens,
        modulation,
        hidden,
        queries,
        key_heads,
        values,
        log_total,
        attended,
        branch_one,
        middle,
        hidden_two,
        inner_sum,
        active,
        branch_two,
    ) = stored
    rows_mod = mod_rows(modulation)
    leading = tokens.shape[:-1]
    clips_here = tokens.shape[0]
    d_gate_two = jnp.sum(grad_out * branch_two, axis=(1, 2))
    d_branch_two = (rows_mod[5] * grad_out).astype(jnp.bfloat16).reshape(-1, D)
    d_bias_two = jnp.sum(d_branch_two, axis=0, dtype=jnp.float32)
    d_active = right_dot(d_branch_two, w_two)
    unused_gelu, gelu_back = jax.vjp(
        lambda entries: jax.nn.gelu(entries, approximate=True), inner_sum
    )
    d_inner = gelu_back(d_active)[0].astype(jnp.bfloat16)
    d_bias_one = jnp.sum(d_inner, axis=0, dtype=jnp.float32)
    d_hidden_two = right_dot(d_inner, w_one).reshape(leading + (D,))
    unused_norm, norm_back = jax.vjp(modulate, middle, rows_mod[4], rows_mod[3])
    d_middle, d_scale_two, d_shift_two = norm_back(d_hidden_two)
    grad_mid = grad_out + d_middle
    d_gate_one = jnp.sum(grad_mid * branch_one, axis=(1, 2))
    d_branch_one = (rows_mod[2] * grad_mid).astype(jnp.bfloat16).reshape(-1, D)
    d_bias_o = jnp.sum(d_branch_one, axis=0, dtype=jnp.float32)
    d_attended = (
        right_dot(d_branch_one, w_out).astype(jnp.bfloat16).reshape(leading + (HEADS, HEAD_DIM))
    )
    score_form, mix_form, back_form = einsum_forms(temporal)
    scale_qk = HEAD_DIM ** (-0.5)
    scores = contract(score_form, queries, key_heads) * scale_qk
    weights_soft = jnp.exp(scores - log_total)
    d_values = contract(back_form, weights_soft.astype(jnp.bfloat16), d_attended)
    d_probs = contract(score_form, d_attended, values)
    d_scores = weights_soft * (d_probs - jnp.sum(weights_soft * d_probs, axis=-1, keepdims=True))
    d_scores = d_scores.astype(jnp.bfloat16)
    d_queries = contract(mix_form, d_scores, key_heads) * scale_qk
    d_keys = contract(back_form, d_scores, queries) * scale_qk
    d_packed = jnp.concatenate(
        [
            d_queries.reshape(-1, D).astype(jnp.bfloat16),
            d_keys.reshape(-1, D).astype(jnp.bfloat16),
            d_values.reshape(-1, D).astype(jnp.bfloat16),
        ],
        axis=1,
    )
    d_bias_q = jnp.sum(d_packed[:, :D], axis=0, dtype=jnp.float32)
    d_bias_v = jnp.sum(d_packed[:, 2 * D :], axis=0, dtype=jnp.float32)
    d_hidden = right_dot(d_packed, w_qkv).reshape(leading + (D,))
    unused_first, first_back = jax.vjp(modulate, tokens, rows_mod[1], rows_mod[0])
    d_input, d_scale_one, d_shift_one = first_back(d_hidden)
    d_input = grad_mid + d_input
    d_modulation = jnp.stack(
        [
            d_shift_one.reshape(clips_here, D),
            d_scale_one.reshape(clips_here, D),
            d_gate_one,
            d_shift_two.reshape(clips_here, D),
            d_scale_two.reshape(clips_here, D),
            d_gate_two,
        ],
        axis=1,
    )
    d_vector = jnp.concatenate(
        [
            d_bias_q,
            d_bias_v,
            d_bias_o,
            d_bias_one,
            d_bias_two,
            jnp.sum(d_modulation, axis=0).reshape(-1),
        ]
    )
    factors = (
        hidden,
        d_packed,
        attended,
        d_branch_one,
        hidden_two,
        d_inner,
        active,
        d_branch_two,
        d_vector,
    )
    return (d_input, factors, d_modulation)


SHIFTS = (1, 2, 3)
VMEM_BYTES = 50 * 2**20


def swap_dp(x, k):
    return lax.ppermute(x, "dp", [(i, i ^ k) for i in range(4)])


def shift_z(x, k):
    n = lax.axis_size("seq")
    return lax.ppermute(x, "seq", [(i, (i + 2 * k) % n) for i in range(n)])


def swap_x(x):
    n = lax.axis_size("seq")
    return lax.ppermute(x, "seq", [(i, i ^ 1) for i in range(n)])


def gather_dp(x):
    far = swap_dp(x, 2)
    return [x, swap_dp(x, 1), far, swap_dp(far, 1)]


def scatter_dp(kept, sent):
    got_near = swap_dp(sent[0], 1)
    got_far = swap_dp(sent[1], 1)
    far = (kept[1] + got_far.astype(jnp.float32)).astype(jnp.bfloat16)
    return kept[0], got_near, swap_dp(far, 2)


def gather_seq(x):
    column = [x] + [shift_z(x, k) for k in SHIFTS]
    return column + [swap_x(piece) for piece in column]


def scatter_seq(mine, other):
    got = [swap_x(piece) for piece in other]
    pair = [m.astype(jnp.float32) + g.astype(jnp.float32) for m, g in zip(mine, got)]
    total = pair[0]
    for k in SHIFTS:
        total = total + shift_z(pair[k].astype(jnp.bfloat16), k).astype(jnp.float32)
    return total


def source_of(number):
    here = lax.axis_index("seq")
    z, x = here // 2, here % 2
    return 2 * ((z - number % 4 + 4) % 4) + (x + number // 4) % 2


def target_of(number):
    here = lax.axis_index("seq")
    z, x = here // 2, here % 2
    return 2 * ((z + number % 4) % 4) + (x + number // 4) % 2


def padded(count, unit):
    return -(-count // unit) * unit


def whole():
    return pl.BlockSpec(memory_space=pltpu.VMEM)


def anywhere():
    return pl.BlockSpec(memory_space=pl.ANY)


def run(kernel, ins, outs, specs=None, scratch=(), flops=0, grid=(), out_specs=None):
    moved = sum(x.size * x.dtype.itemsize for x in list(ins) + list(outs))
    return pl.pallas_call(
        kernel,
        out_shape=tuple(outs),
        grid=grid,
        in_specs=specs or [whole()] * len(ins),
        out_specs=tuple(out_specs or [whole()] * len(outs)),
        scratch_shapes=list(scratch),
        compiler_params=pltpu.CompilerParams(vmem_limit_bytes=VMEM_BYTES),
        cost_estimate=pl.CostEstimate(flops=flops, bytes_accessed=moved, transcendentals=0),
    )(*ins)


def f32(*shape):
    return jax.ShapeDtypeStruct(shape, jnp.float32)


def bf16(*shape):
    return jax.ShapeDtypeStruct(shape, jnp.bfloat16)


def normal_parts(x):
    average = jnp.mean(x, axis=-1, keepdims=True)
    centred = x - average
    variance = jnp.mean(centred * centred, axis=-1, keepdims=True)
    inverse = lax.rsqrt(variance + EPSILON)
    return centred * inverse, inverse


def modulated(x, modulation, scale_row, order):
    normal, _ = normal_parts(x)
    scale = modulation[scale_row : scale_row + 1]
    shift = modulation[scale_row - 1 : scale_row]
    hidden = (normal * (1.0 + scale) + shift).astype(jnp.bfloat16)
    return plain_dot(hidden, order).astype(jnp.bfloat16)


def enter_kernel(x_ref, modulation_ref, order_ref, hidden_ref):
    x = x_ref[...].astype(jnp.float32)
    hidden_ref[...] = modulated(x, modulation_ref[...], 1, order_ref[...])


def middle_kernel(
    kept_ref, near_ref, far_ref, bias_ref, x_ref, modulation_ref, order_ref, branch_ref, middle_ref, hidden_ref
):
    branch = kept_ref[...] + near_ref[...].astype(jnp.float32) + far_ref[...].astype(jnp.float32) + bias_ref[...]
    modulation = modulation_ref[...]
    middle = x_ref[...].astype(jnp.float32) + modulation[2:3] * branch
    branch_ref[...] = branch
    middle_ref[...] = middle
    hidden_ref[...] = modulated(middle, modulation, 4, order_ref[...])


def leave_kernel(kept_ref, near_ref, far_ref, bias_ref, middle_ref, modulation_ref, branch_ref, result_ref):
    branch = kept_ref[...] + near_ref[...].astype(jnp.float32) + far_ref[...].astype(jnp.float32) + bias_ref[...]
    branch_ref[...] = branch
    result_ref[...] = (middle_ref[...] + modulation_ref[5:6] * branch).astype(jnp.bfloat16)


def start_pieces(pieces, buffer, sems, first):
    rows = pieces[0].shape[0]
    copies = []
    for number, piece in enumerate(pieces):
        at = pl.multiple_of(source_of(number) * rows, 16)
        copy = pltpu.make_async_copy(piece, buffer.at[pl.ds(at, rows)], sems.at[first + number])
        copy.start()
        copies.append(copy)
    return copies


def start_halves(pieces, split, upper, lower, sems):
    copies = []
    for number, piece in enumerate(pieces):
        source = source_of(number)
        rest = piece.shape[0] - split
        at = pl.multiple_of(source * split, 16)
        copy = pltpu.make_async_copy(
            piece.at[pl.ds(0, split)], upper.at[pl.ds(at, split)], sems.at[number]
        )
        copy.start()
        copies.append(copy)
    later = []
    for number, piece in enumerate(pieces):
        source = source_of(number)
        rest = piece.shape[0] - split
        at = pl.multiple_of(source * rest, 16)
        copy = pltpu.make_async_copy(
            piece.at[pl.ds(split, rest)], lower.at[pl.ds(at, rest)], sems.at[8 + number]
        )
        copy.start()
        later.append(copy)
    return copies, later


def wait_all(copies):
    for copy in copies:
        copy.wait()


def softmax_of(scores, period):
    if period:
        row = lax.broadcasted_iota(jnp.int32, scores.shape, 0) % period
        column = lax.broadcasted_iota(jnp.int32, scores.shape, 1) % period
        scores = jnp.where(row == column, scores, -1e30)
    exponent = jnp.exp(scores - jnp.max(scores, axis=-1, keepdims=True))
    return exponent / jnp.sum(exponent, axis=-1, keepdims=True)


def owners(width, per_head):
    return lax.broadcasted_iota(jnp.int32, (1, width), 1) // per_head


def attention_kernel(period, heads, *refs):
    hidden, w_qkv, w_out, bias_ref = refs[0:4], refs[4:12], refs[12:20], refs[20]
    packed_ref, mixed_ref, keep_zero, send_one, keep_two, send_three = refs[21:27]
    qkv, out, sems = refs[27:30]
    first = start_pieces(w_qkv, qkv, sems, 0)
    second = start_pieces(w_out, out, sems, 8)
    width, wide = heads * HEAD_DIM, out.shape[0]
    count = hidden[0].shape[0]
    narrow_owner, wide_owner = owners(width, HEAD_DIM), owners(wide, wide // heads)
    wait_all(first)
    for number in range(4):
        rows = pl.ds(number * count, count)
        packed = (plain_dot(hidden[number][...], qkv[...]) + bias_ref[...]).astype(jnp.bfloat16)
        packed_ref[rows, :] = packed
        values = packed[:, :wide]
        queries = packed[:, wide : wide + width]
        key_heads = packed[:, wide + width :]
        mixed = jnp.zeros((count, wide), jnp.float32)
        for head in range(heads):
            chosen = jnp.where(narrow_owner == head, queries, 0)
            scores = right_dot(chosen, key_heads) * HEAD_DIM ** (-0.5)
            weights_soft = softmax_of(scores, period).astype(jnp.bfloat16)
            mixed = jnp.where(wide_owner == head, plain_dot(weights_soft, values), mixed)
        mixed_ref[rows, :] = mixed.astype(jnp.bfloat16)
    wait_all(second)
    for number, ref in enumerate((keep_zero, send_one, keep_two, send_three)):
        partial = plain_dot(mixed_ref[pl.ds(number * count, count), :], out[...])
        ref[...] = partial.astype(ref.dtype)


def attention_back_kernel(period, heads, *refs):
    d_branch, w_out, w_qkv, packed_ref = refs[0:4], refs[4:12], refs[12:20], refs[20]
    d_packed_ref, sums_ref, keep_zero, send_one, keep_two, send_three = refs[21:27]
    qkv, out, sems = refs[27:30]
    second = start_pieces(w_out, out, sems, 8)
    first = start_pieces(w_qkv, qkv, sems, 0)
    width, wide = heads * HEAD_DIM, out.shape[0]
    count = d_branch[0].shape[0]
    scale = HEAD_DIM ** (-0.5)
    narrow_owner, wide_owner = owners(width, HEAD_DIM), owners(wide, wide // heads)
    sums = jnp.zeros((1, wide + 2 * width), jnp.float32)
    wait_all(second)
    for number in range(4):
        rows = pl.ds(number * count, count)
        d_mixed = right_dot(d_branch[number][...], out[...]).astype(jnp.bfloat16)
        packed = packed_ref[rows, :]
        values = packed[:, :wide]
        queries = packed[:, wide : wide + width]
        key_heads = packed[:, wide + width :]
        d_queries = jnp.zeros((count, width), jnp.float32)
        d_keys = d_queries
        d_values = jnp.zeros((count, wide), jnp.float32)
        for head in range(heads):
            chosen = jnp.where(narrow_owner == head, queries, 0)
            weights_soft = softmax_of(right_dot(chosen, key_heads) * scale, period)
            rounded = weights_soft.astype(jnp.bfloat16)
            d_values = jnp.where(wide_owner == head, left_dot(rounded, d_mixed), d_values)
            d_probs = right_dot(jnp.where(wide_owner == head, d_mixed, 0), values)
            inner = jnp.sum(weights_soft * d_probs, axis=-1, keepdims=True)
            d_scores = (weights_soft * (d_probs - inner)).astype(jnp.bfloat16)
            mine = narrow_owner == head
            d_queries = jnp.where(mine, plain_dot(d_scores, key_heads), d_queries)
            d_keys = jnp.where(mine, left_dot(d_scores, queries), d_keys)
        d_packed = jnp.concatenate([d_values, d_queries * scale, d_keys * scale], axis=1)
        d_packed = d_packed.astype(jnp.bfloat16)
        d_packed_ref[rows, :] = d_packed
        sums = sums + jnp.sum(d_packed.astype(jnp.float32), axis=0, keepdims=True)
    sums_ref[...] = sums
    wait_all(first)
    for number, ref in enumerate((keep_zero, send_one, keep_two, send_three)):
        partial = right_dot(d_packed_ref[pl.ds(number * count, count), :], qkv[...])
        ref[...] = partial.astype(ref.dtype)


def gelu_pair(u):
    inner = 0.7978845608028654 * (u + 0.044715 * u * u * u)
    bent = jnp.tanh(inner)
    value = 0.5 * u * (1.0 + bent)
    slope = 0.5 * (1.0 + bent) + 0.5 * u * (1.0 - bent * bent) * (
        0.7978845608028654 * (1.0 + 3 * 0.044715 * u * u)
    )
    return value, slope


def mlp_kernel(split, *refs):
    hidden, pieces, bias_ref = refs[0:4], refs[4:12], refs[12]
    active_ref, slope_ref, keep_zero, send_one, keep_two, send_three = refs[13:19]
    one, two, sems = refs[19:22]
    first, second = start_halves(pieces, split, one, two, sems)
    count = hidden[0].shape[0]
    wait_all(first)
    for number in range(4):
        rows = pl.ds(number * count, count)
        value, slope = gelu_pair(plain_dot(hidden[number][...], one[...]) + bias_ref[...])
        active_ref[rows, :] = value.astype(jnp.bfloat16)
        slope_ref[rows, :] = slope
    wait_all(second)
    for number, ref in enumerate((keep_zero, send_one, keep_two, send_three)):
        partial = plain_dot(active_ref[pl.ds(number * count, count), :], two[...])
        ref[...] = partial.astype(ref.dtype)


def mlp_back_kernel(split, *refs):
    d_branch, pieces, slope_ref = refs[0:4], refs[4:12], refs[12]
    d_inner_ref, sums_ref, keep_zero, send_one, keep_two, send_three = refs[13:19]
    one, two, sems = refs[19:22]
    first, second = start_halves(pieces, split, one, two, sems)
    count = d_branch[0].shape[0]
    wait_all(second)
    sums = jnp.zeros(sums_ref.shape, jnp.float32)
    for number in range(4):
        rows = pl.ds(number * count, count)
        d_active = right_dot(d_branch[number][...], two[...])
        d_inner = (d_active * slope_ref[rows, :]).astype(jnp.bfloat16)
        d_inner_ref[rows, :] = d_inner
        sums = sums + jnp.sum(d_inner.astype(jnp.float32), axis=0, keepdims=True)
    sums_ref[...] = sums
    wait_all(first)
    for number, ref in enumerate((keep_zero, send_one, keep_two, send_three)):
        partial = right_dot(d_inner_ref[pl.ds(number * count, count), :], one[...])
        ref[...] = partial.astype(ref.dtype)


def total_sums(ref, *members):
    rows = [jnp.sum(m.astype(jnp.float32), axis=0, keepdims=True) for m in members]
    ref[...] = jnp.concatenate(rows, axis=0)


def open_back_kernel(grad_ref, branch_ref, modulation_ref, d_branch_ref, sums_ref):
    grad = grad_ref[...].astype(jnp.float32)
    d_branch = (modulation_ref[5:6] * grad).astype(jnp.bfloat16)
    d_branch_ref[...] = d_branch
    total_sums(sums_ref, grad * branch_ref[...], d_branch)


def natural(total, order):
    high = total.astype(jnp.bfloat16)
    low = (total - high.astype(jnp.float32)).astype(jnp.bfloat16)
    return right_dot(high, order) + right_dot(low, order)


def norm_back(d_hidden, x, scale):
    normal, inverse = normal_parts(x)
    entry = d_hidden * (1.0 + scale)
    average = jnp.mean(entry, axis=-1, keepdims=True)
    along = jnp.mean(entry * normal, axis=-1, keepdims=True)
    return (entry - average - normal * along) * inverse, d_hidden * normal


def middle_back_kernel(
    kept_ref, near_ref, far_ref, grad_ref, x_ref, branch_ref, modulation_ref, order_ref, d_branch_ref, grad_mid_ref, sums_ref
):
    total = kept_ref[...] + near_ref[...].astype(jnp.float32) + far_ref[...].astype(jnp.float32)
    d_hidden = natural(total, order_ref[...])
    modulation = modulation_ref[...]
    d_x, d_scale = norm_back(d_hidden, x_ref[...], modulation[4:5])
    grad_mid = grad_ref[...].astype(jnp.float32) + d_x
    grad_mid_ref[...] = grad_mid
    d_branch = (modulation[2:3] * grad_mid).astype(jnp.bfloat16)
    d_branch_ref[...] = d_branch
    total_sums(sums_ref, d_hidden, d_scale, grad_mid * branch_ref[...], d_branch)


def close_back_kernel(kept_ref, near_ref, far_ref, grad_ref, x_ref, modulation_ref, order_ref, d_x_ref, sums_ref):
    total = kept_ref[...] + near_ref[...].astype(jnp.float32) + far_ref[...].astype(jnp.float32)
    d_hidden = natural(total, order_ref[...])
    d_x, d_scale = norm_back(d_hidden, x_ref[...].astype(jnp.float32), modulation_ref[1:2])
    d_x_ref[...] = (grad_ref[...] + d_x).astype(d_x_ref.dtype)
    total_sums(sums_ref, d_hidden, d_scale)


def factor(pairs, merged):
    ins, scratch, outs, flops = [], [], [], 0
    for left, right, height in pairs:
        ins += left + right
        count = sum(piece.shape[0] for piece in left)
        scratch.append(pltpu.VMEM((left[0].shape[1], count), jnp.bfloat16))
        if len(right) > 1:
            scratch.append(pltpu.VMEM((count, right[0].shape[1]), jnp.bfloat16))
        flops += 2 * count * left[0].shape[1] * right[0].shape[1]
    shapes = [bf16(height, right[0].shape[1]) for _, right, height in pairs]
    if merged:
        shapes = [bf16(sum(s.shape[0] for s in shapes), shapes[0].shape[1])]

    def kernel(*refs):
        refs = iter(refs)
        groups = []
        for left, right, height in pairs:
            groups.append(([next(refs) for _ in left], [next(refs) for _ in right], height))
        targets = [[next(refs) for _ in shapes] for _ in range(8)]
        ready = []
        for left, right, height in groups:
            flip = next(refs)
            at = 0
            for piece in left:
                flip[:, at : at + piece.shape[0]] = piece[...].T
                at += piece.shape[0]
            lay = right[0]
            if len(right) > 1:
                lay = next(refs)
                at = 0
                for piece in right:
                    lay[at : at + piece.shape[0], :] = piece[...]
                    at += piece.shape[0]
            ready.append((flip, lay, height))
        for number in range(8):
            target = target_of(number)
            at = 0
            for index, (flip, lay, height) in enumerate(ready):
                rows = pl.ds(pl.multiple_of(target * height, 16), height)
                product = plain_dot(flip[rows, :], lay[...]).astype(jnp.bfloat16)
                if merged:
                    targets[number][0][at : at + height, :] = product
                    at += height
                else:
                    targets[number][index][...] = product

    results = run(kernel, ins, shapes * 8, scratch=scratch, flops=flops)
    width = len(shapes)
    return [
        ([results[(number) * width + index] for number in range(4)],
         [results[(number + 4) * width + index] for number in range(4)])
        for index in range(width)
    ]


def order_matrix(n_dp, n_seq, rows, room):
    place = lax.broadcasted_iota(jnp.int32, (D, n_dp * n_seq * room), 1)
    feature = lax.broadcasted_iota(jnp.int32, (D, n_dp * n_seq * room), 0)
    block, inner = place // room, place % room
    owner = (block % n_dp) * n_seq + block // n_dp
    return ((feature == owner * rows + inner) & (inner < rows)).astype(jnp.bfloat16)


def grow(x, axis, size):
    pads = [(0, 0)] * x.ndim
    pads[axis] = (0, size - x.shape[axis])
    return jnp.pad(x, pads)


def exchange(parts):
    return lax.all_to_all(parts, "dp", split_axis=0, concat_axis=0, tiled=True)


def spread(values, n_seq, rows, room):
    lead = values.shape[:-1]
    return grow(values.reshape(lead + (n_seq, rows)), len(lead) + 1, room).reshape(lead + (-1,))


def ordered_vectors(everyone, n_dp, n_seq, count):
    chosen = owner_rows(n_dp, n_seq, -1)
    ordered = left_dot(chosen.astype(jnp.bfloat16), everyone)
    return ordered.reshape(n_dp * n_seq, 2, count).transpose(1, 0, 2).reshape(2, -1)


def owner_rows(n_dp, n_seq, sign):
    count = n_dp * n_seq
    relative = lax.broadcasted_iota(jnp.int32, (count, count), 0)
    owner = lax.broadcasted_iota(jnp.int32, (count, count), 1)
    dp, seq = lax.axis_index("dp"), lax.axis_index("seq")
    n_z = n_seq // 2
    z = (seq // 2 + sign * (relative // (2 * n_dp)) + n_z) % n_z
    x = (seq % 2) ^ ((relative // n_dp) % 2)
    source = (dp ^ (relative % n_dp)) * n_seq + 2 * z + x
    return (owner == source).astype(jnp.float32)


def scatter_vectors(sums, n_dp, n_seq):
    count = sums.shape[1] // (n_dp * n_seq)
    rows = sums.reshape(2, n_dp * n_seq, count).transpose(1, 0, 2).reshape(n_dp * n_seq, -1)
    chosen = owner_rows(n_dp, n_seq, 1)
    rows = jnp.dot(chosen, rows, precision=lax.Precision.HIGHEST)
    quarters = jnp.split(rows, n_seq // 2)
    total = quarters[0]
    for k in SHIFTS:
        total = total + shift_z(quarters[k], k)
    total = total[:n_dp] + swap_x(total[n_dp:])
    total = total[:2] + swap_dp(total[2:], 2)
    total = total[:1] + swap_dp(total[1:], 1)
    return total.reshape(2, count)


def sum_seq(x):
    x = x + swap_x(x)
    return x + sum(shift_z(x, k) for k in SHIFTS)


def slice_of(vector, n_dp):
    width = vector.shape[0] // n_dp
    return lax.dynamic_slice(vector, (lax.axis_index("dp") * width,), (width,))


def place_slice(piece, n_dp):
    zeros = jnp.zeros((piece.shape[0] * n_dp,), piece.dtype)
    return lax.dynamic_update_slice(zeros, piece, (lax.axis_index("dp") * piece.shape[0],))


class Gather:
    def __init__(self, pieces):
        self.column, self.across, self.sent, self.waiting = [pieces], [], 0, False

    def wants_x(self):
        return self.sent < len(self.column)

    def send_x(self):
        self.sent += 1
        return [swap_x(piece) for piece in self.column[self.sent - 1]]

    def got_x(self, pieces):
        self.across.append(pieces)

    def wants_z(self):
        return len(self.column) < 4 and not self.waiting

    def send_z(self):
        self.waiting = True
        return [shift_z(piece, 1) for piece in self.column[-1]]

    def got_z(self, pieces):
        self.waiting = False
        self.column.append(pieces)

    def finished(self):
        return len(self.across) == 4

    def pieces(self, index):
        return [piece[index] for piece in self.column + self.across]


class Reduce:
    def __init__(self, mine, other, finish):
        self.mine, self.other, self.finish = mine, other, finish
        self.sent, self.got, self.hops, self.carried, self.result = 3, {}, 3, None, None

    def wants_x(self):
        return self.sent >= 0

    def send_x(self):
        self.sent -= 1
        return [piece for piece in map(swap_x, self.other[self.sent + 1])]

    def got_x(self, pieces):
        self.got[3 - len(self.got)] = pieces

    def added(self, k):
        total = [m.astype(jnp.float32) + g.astype(jnp.float32) for m, g in zip(self.mine[k], self.got[k])]
        if k < 3:
            total = [t + c.astype(jnp.float32) for t, c in zip(total, self.carried)]
        return total

    def wants_z(self):
        ready = self.hops == 3 or self.carried is not None
        return self.hops > 0 and self.hops in self.got and ready

    def send_z(self):
        total = self.added(self.hops)
        self.hops -= 1
        self.carried = None
        return [shift_z(t.astype(jnp.bfloat16), 1) for t in total]

    def got_z(self, pieces):
        self.carried = pieces

    def finished(self):
        return self.hops == 0 and self.carried is not None and 0 in self.got


class Lane:
    def __init__(self):
        self.jobs, self.flight, self.extra = [], [], []

    def issue(self):
        for kind in ("x", "z"):
            for job in self.jobs:
                if getattr(job, "wants_" + kind)():
                    self.flight.append((job, kind, getattr(job, "send_" + kind)()))
                    break

    def close(self):
        for job in [job for job in self.jobs if job.finished()]:
            self.jobs.remove(job)
            if isinstance(job, Reduce):
                job.finish(job.added(0))

    def tick(self, values):
        values, arrived, extra = lax.optimization_barrier(
            (values, [pieces for _, _, pieces in self.flight], self.extra)
        )
        flight, self.flight, self.extra = self.flight, [], []
        for (job, kind, _), pieces in zip(flight, arrived):
            getattr(job, "got_" + kind)(pieces)
        self.close()
        self.issue()
        return values

    def until(self, job, values):
        while not job.finished():
            values = self.tick(values)
        return values


def on_device_split(tokens, cond, d_out, attn_in, attn_out, mlp_in, mlp_out, vectors):
    n_dp, n_seq = lax.axis_size("dp"), lax.axis_size("seq")
    heads = HEADS // n_dp
    width = heads * HEAD_DIM
    frames, places = tokens.shape[1] * n_seq, tokens.shape[2]
    periods = (0, places // n_seq)
    count = tokens.shape[1] * places
    everyone_count = n_dp * count
    rows = D // (n_dp * n_seq)
    room = padded(rows, 8)
    out_room = padded(rows, 16)
    deep, wide = n_dp * n_seq * room, n_seq * out_room
    packed_width = wide + 2 * width
    inner = FF // n_dp
    split = n_dp * room
    order = order_matrix(n_dp, n_seq, rows, room)

    def qkv_parts(flat):
        parts = flat.reshape(rows, 3, n_dp, width)
        values = spread(parts[:, 2], n_seq, rows, out_room)
        joined = jnp.concatenate([values, parts[:, 0], parts[:, 1]], axis=2)
        return grow(joined.transpose(1, 0, 2), 1, room)

    def one_parts(flat):
        return grow(flat.reshape(rows, n_dp, inner).transpose(1, 0, 2), 1, room)

    def qkv_piece(index):
        return exchange(qkv_parts(attn_in[index])).reshape(-1, packed_width)

    def out_piece(index):
        return grow(attn_out[index].reshape(rows, D), 0, out_room)

    def mlp_piece(index):
        one = exchange(one_parts(mlp_in[index])).reshape(-1, inner)
        return jnp.concatenate([one, mlp_out[index].reshape(-1, D)])

    weights, biases, modulations = [], [], []
    lane = Lane()
    first = [qkv_piece(0), out_piece(0)]
    mine = vectors.reshape(1, -1)
    near = jnp.concatenate([mine, swap_dp(mine, 1)])
    clips = jnp.concatenate([near, swap_dp(near, 2)])
    clips, first = lax.optimization_barrier((clips, first))
    attention_jobs, mlp_jobs = [Gather(first)], []
    lane.jobs.append(attention_jobs[0])
    lane.issue()
    pair = lane.tick(jnp.concatenate([clips, swap_x(clips)]))
    pieces = [mlp_piece(0)]
    lane.extra.append(pieces)
    everyone = lane.tick(jnp.concatenate([pair] + [shift_z(pair, k) for k in SHIFTS]))
    mlp_jobs.append(Gather(pieces))
    lane.jobs.append(mlp_jobs[0])
    vector = ordered_vectors(everyone, n_dp, n_seq, vectors.shape[1])
    for index in range(2):
        v = vector[index]
        bias_q, bias_v = slice_of(v[0:D], n_dp), slice_of(v[D : 2 * D], n_dp)
        bias_v = spread(bias_v, n_seq, rows, out_room)
        biases.append(
            (
                jnp.concatenate([bias_v, bias_q, jnp.zeros_like(bias_q)])[None],
                v[None, 2 * D : 3 * D],
                slice_of(v[3 * D : 3 * D + FF], n_dp)[None],
                v[None, 3 * D + FF : 4 * D + FF],
            )
        )
        modulations.append(v[4 * D + FF :].reshape(6, D) + cond[0])

    def to_places(x):
        x = x.reshape(1, frames // n_seq, places, D)
        x = lax.all_to_all(x, "seq", split_axis=2, concat_axis=1, tiled=True)
        return x.reshape(-1, D)

    def to_frames(x):
        x = x.reshape(1, frames, places // n_seq, D)
        x = lax.all_to_all(x, "seq", split_axis=1, concat_axis=2, tiled=True)
        return x.reshape(-1, D)

    sems = pltpu.SemaphoreType.DMA((16,))
    attention_scratch = [
        pltpu.VMEM((deep, packed_width), jnp.bfloat16),
        pltpu.VMEM((wide, D), jnp.bfloat16),
        sems,
    ]
    mlp_scratch = [
        pltpu.VMEM((deep, inner), jnp.bfloat16),
        pltpu.VMEM((inner, D), jnp.bfloat16),
        sems,
    ]
    in_attention = [whole()] * 4 + [anywhere()] * 16 + [whole()]
    in_mlp = [whole()] * 4 + [anywhere()] * 8 + [whole()]

    def quarters(size):
        return [f32(count, size), bf16(count, size), f32(count, size), bf16(count, size)]

    def forward(index, x):
        bias_qkv, bias_o, bias_one, bias_two = biases[index]
        modulation = modulations[index]
        (hidden,) = run(enter_kernel, [x, modulation, order], [bf16(count, deep)])
        if index == 0:
            hidden = lane.tick(hidden)
        hidden = lane.until(attention_jobs[index], lane.tick(gather_dp(hidden)))
        qkv, out = attention_jobs[index].pieces(0), attention_jobs[index].pieces(1)
        packed, mixed, *partial = run(
            functools.partial(attention_kernel, periods[index], heads),
            hidden + qkv + out + [bias_qkv],
            [bf16(everyone_count, packed_width), bf16(everyone_count, wide)] + quarters(D),
            specs=in_attention,
            scratch=attention_scratch,
            flops=2 * everyone_count * (deep * packed_width + wide * D) * 2,
        )
        if index == 0:
            pieces = [qkv_piece(1), out_piece(1)]
            lane.extra.append(pieces)
            attention_jobs.append(Gather(pieces))
        partial = lane.tick(partial)
        lane.jobs += attention_jobs[1:] * (index == 0)
        if index == 0:
            pieces = [mlp_piece(1)]
            lane.extra.append(pieces)
            mlp_jobs.append(Gather(pieces))
        own = lane.tick(scatter_dp(partial[0::2], partial[1::2]))
        lane.jobs += mlp_jobs[1:] * (index == 0)
        branch_one, middle, hidden_two = run(
            middle_kernel,
            list(own) + [bias_o, x, modulation, order],
            [f32(count, D), f32(count, D), bf16(count, deep)],
        )
        hidden_two = lane.until(mlp_jobs[index], lane.tick(gather_dp(hidden_two)))
        mlp = mlp_jobs[index].pieces(0)
        active, slope, *partial = run(
            functools.partial(mlp_kernel, split),
            hidden_two + mlp + [bias_one],
            [bf16(everyone_count, inner), f32(everyone_count, inner)] + quarters(D),
            specs=in_mlp,
            scratch=mlp_scratch,
            flops=2 * everyone_count * (deep + D) * inner,
        )
        partial = lane.tick(partial)
        own = lane.tick(scatter_dp(partial[0::2], partial[1::2]))
        branch_two, result = run(
            leave_kernel, list(own) + [bias_two, middle, modulation], [f32(count, D), bf16(count, D)]
        )
        stored = (x, hidden, packed, mixed, branch_one, middle, hidden_two, active, slope, branch_two)
        weights.append((qkv, out, mlp))
        return result, stored

    owned = {}

    def keep(key, value):
        owned[key] = value
        lane.extra.append(value)

    def finish_mlp(index):
        def finish(totals):
            (total,) = totals
            one = exchange(total[:split].astype(jnp.bfloat16).reshape(n_dp, room, -1))[:, :rows]
            keep(("one", index), one.transpose(1, 0, 2).astype(jnp.float32).reshape(-1))
            keep(("two", index), total[split:].reshape(-1))

        return finish

    def finish_attention(index):
        def finish(totals):
            qkv, out = totals
            qkv = exchange(qkv.astype(jnp.bfloat16).reshape(n_dp, room, -1))[:, :rows]
            values = qkv[:, :, :wide].reshape(n_dp, rows, n_seq, out_room)[..., :rows]
            values = values.reshape(n_dp, rows, width)
            joined = jnp.stack([qkv[:, :, wide : wide + width], qkv[:, :, wide + width :], values])
            keep(("qkv", index), joined.transpose(2, 0, 1, 3).astype(jnp.float32).reshape(-1))
            keep(("out", index), out[:rows].reshape(-1))

        return finish

    def backward(index, grad, stored, out_type):
        qkv, out, mlp = weights[index]
        modulation = modulations[index]
        x, hidden, packed, mixed, branch_one, middle, hidden_two, active, slope, branch_two = stored
        d_branch_two, sums_two = run(
            open_back_kernel, [grad, branch_two, modulation], [bf16(count, D), f32(2, D)]
        )
        d_branch_two = lane.tick(gather_dp(d_branch_two))
        d_inner, d_bias_one, *partial = run(
            functools.partial(mlp_back_kernel, split),
            d_branch_two + mlp + [slope],
            [bf16(everyone_count, inner), f32(1, inner)] + quarters(deep),
            specs=in_mlp,
            scratch=mlp_scratch,
            flops=2 * everyone_count * (deep + D) * inner,
        )
        partial = lane.tick(partial)
        own = scatter_dp(partial[0::2], partial[1::2])
        ((mlp_mine, mlp_other),) = factor(
            [(hidden_two, [d_inner], split), ([active], d_branch_two, inner // n_seq)], True
        )
        lane.jobs.append(Reduce([[m] for m in mlp_mine], [[m] for m in mlp_other], finish_mlp(index)))
        lane.extra.append((mlp_mine, mlp_other))
        own = lane.tick(own)
        d_branch_one, grad_mid, sums_mid = run(
            middle_back_kernel,
            list(own) + [grad, middle, branch_one, modulation, order],
            [bf16(count, D), f32(count, D), f32(4, D)],
        )
        d_branch_one = lane.tick(gather_dp(d_branch_one))
        d_packed, d_bias_qkv, *partial = run(
            functools.partial(attention_back_kernel, periods[index], heads),
            d_branch_one + out + qkv + [packed],
            [bf16(everyone_count, packed_width), f32(1, packed_width)] + quarters(deep),
            specs=in_attention,
            scratch=attention_scratch,
            flops=2 * everyone_count * (deep * packed_width + wide * D) * 2,
        )
        partial = lane.tick(partial)
        own = scatter_dp(partial[0::2], partial[1::2])
        (qkv_mine, qkv_other), (out_mine, out_other) = factor(
            [(hidden, [d_packed], split), ([mixed], d_branch_one, out_room)], False
        )
        lane.jobs.append(
            Reduce(list(zip(qkv_mine, out_mine)), list(zip(qkv_other, out_other)), finish_attention(index))
        )
        lane.extra.append((qkv_mine, qkv_other, out_mine, out_other))
        own = lane.tick(own)
        d_x, sums_one = run(
            close_back_kernel,
            list(own) + [grad_mid, x, modulation, order],
            [jax.ShapeDtypeStruct((count, D), out_type), f32(2, D)],
        )
        d_modulation = jnp.stack(
            [sums_one[0], sums_one[1], sums_mid[2], sums_mid[0], sums_mid[1], sums_two[0]]
        )
        bias_values = d_bias_qkv[0, :wide].reshape(n_seq, out_room)[:, :rows].reshape(-1)
        d_vector = jnp.concatenate(
            [
                place_slice(d_bias_qkv[0, wide : wide + width], n_dp),
                place_slice(bias_values, n_dp),
                sums_mid[3],
                place_slice(d_bias_one[0], n_dp),
                sums_two[1],
                d_modulation.reshape(-1),
            ]
        )
        return d_x, d_vector, d_modulation

    grad_places = to_places(d_out)
    spatial_out, stored_zero = forward(0, tokens.reshape(-1, D))
    temporal_out, stored_one = forward(1, lane.tick(to_places(spatial_out)))
    output = to_frames(temporal_out).astype(jnp.float32)
    grad_mid, vector_one, modulation_one = backward(1, grad_places, stored_one, jnp.bfloat16)
    d_tokens, vector_zero, modulation_zero = backward(
        0, lane.tick(to_frames(grad_mid)), stored_zero, jnp.float32
    )
    lane.extra.append(output)
    sums = (jnp.stack([vector_zero, vector_one]), modulation_zero + modulation_one)
    d_vectors = scatter_vectors(sums[0], n_dp, n_seq)
    d_cond = sum_seq(sums[1])[None]
    while lane.jobs:
        lane.tick(())
    stacked = tuple(
        jnp.stack([owned[name, 0], owned[name, 1]]) for name in ("qkv", "out", "one", "two")
    )
    return (
        output.reshape(tokens.shape),
        d_tokens.reshape(tokens.shape),
        d_cond,
        *stacked,
        d_vectors,
    )


def on_device(tokens, cond, d_out, attn_in, attn_out, mlp_in, mlp_out, vectors):
    shards = (attn_in, attn_out, mlp_in, mlp_out, vectors)
    widths = (
        attn_in.shape[1],
        attn_out.shape[1],
        mlp_in.shape[1],
        mlp_out.shape[1],
        vectors.shape[1],
    )
    layer_zero = unpack(fetch_forward(shards, 0))
    spatial_out, stored_zero = layer_forward(tokens.astype(jnp.float32), cond, layer_zero, False)
    by_place = lax.all_to_all(
        spatial_out.astype(jnp.bfloat16), "seq", split_axis=2, concat_axis=1, tiled=True
    ).astype(spatial_out.dtype)
    layer_one = unpack(fetch_forward(shards, 1))
    temporal_out, stored_one = layer_forward(by_place, cond, layer_one, True)
    output = lax.all_to_all(
        temporal_out.astype(jnp.bfloat16), "seq", split_axis=1, concat_axis=2, tiled=True
    ).astype(temporal_out.dtype)
    grad_places = lax.all_to_all(d_out, "seq", split_axis=2, concat_axis=1, tiled=True).astype(
        jnp.float32
    )
    grad_mid, factors_one, modul_one = layer_backward(grad_places, stored_one, layer_one, True)
    owned_one = reduce_grads(factors_one, widths)
    grad_frames = lax.all_to_all(
        grad_mid.astype(jnp.bfloat16), "seq", split_axis=1, concat_axis=2, tiled=True
    ).astype(grad_mid.dtype)
    d_tokens, factors_zero, modul_zero = layer_backward(grad_frames, stored_zero, layer_zero, False)
    owned_zero = reduce_grads(factors_zero, widths)
    d_cond = lax.psum(modul_zero + modul_one, "seq")
    stacked = tuple((jnp.stack([former, latter]) for former, latter in zip(owned_zero, owned_one)))
    return (output, d_tokens, d_cond, stacked[0], stacked[1], stacked[2], stacked[3], stacked[4])


def solution(mesh):
    in_specs = (
        P("dp", "seq", None, None),
        P("dp", None, None),
        P("dp", "seq", None, None),
        P(None, ("dp", "seq")),
        P(None, ("dp", "seq")),
        P(None, ("dp", "seq")),
        P(None, ("dp", "seq")),
        P(None, ("dp", "seq")),
    )
    out_specs = (
        P("dp", "seq", None, None),
        P("dp", "seq", None, None),
        P("dp", None, None),
        P(None, ("dp", "seq")),
        P(None, ("dp", "seq")),
        P(None, ("dp", "seq")),
        P(None, ("dp", "seq")),
        P(None, ("dp", "seq")),
    )
    split = mesh.shape["dp"] == 4 and mesh.shape["seq"] == 8
    return jax.shard_map(
        on_device_split if split else on_device, mesh=mesh, in_specs=in_specs, out_specs=out_specs, check_vma=False
    )
```

```python
import functools

import jax
import jax.numpy as jnp
from jax import lax
from jax.experimental import pallas as pl
from jax.experimental.pallas import tpu as pltpu
from jax.sharding import PartitionSpec as P

D = 1152
HEADS = 16
HEAD_DIM = 72
FF = 4608


EPSILON = 1e-06


def as_sent(x):

    def short(part):
        return part.astype(jnp.bfloat16) if part.dtype == jnp.float32 else part

    return jax.tree.map(short, x)


def modulate(tokens, scale, shift):
    average = jnp.mean(tokens, axis=-1, keepdims=True)
    centred = tokens - average
    variance = jnp.mean(centred * centred, axis=-1, keepdims=True)
    return centred * lax.rsqrt(variance + EPSILON) * (1.0 + scale) + shift


def plain_dot(former, latter):
    return jnp.dot(former, latter, preferred_element_type=jnp.float32)


def left_dot(former, latter):
    return lax.dot_general(
        former, latter, (((0,), (0,)), ((), ())), preferred_element_type=jnp.float32
    )


def right_dot(former, latter):
    return lax.dot_general(
        former, latter, (((1,), (1,)), ((), ())), preferred_element_type=jnp.float32
    )


def contract(form, former, latter):
    return jnp.einsum(form, former, latter, preferred_element_type=jnp.float32)


def einsum_forms(temporal):
    if temporal:
        return ("aibhe,ajbhe->abhij", "abhij,ajbhe->aibhe", "abhij,aibhe->ajbhe")
    return ("abihe,abjhe->abhij", "abhij,abjhe->abihe", "abhij,abihe->abjhe")


def unpack(pieces):
    attn_in, attn_out, mlp_in, mlp_out, vector = pieces
    vector = vector.astype(jnp.float32)
    return (
        attn_in.reshape(D, 3 * D),
        attn_out.reshape(D, D),
        mlp_in.reshape(D, FF),
        mlp_out.reshape(FF, D),
        vector[0:D],
        vector[D : 2 * D],
        vector[2 * D : 3 * D],
        vector[3 * D : 3 * D + FF],
        vector[3 * D + FF : 4 * D + FF],
        vector[4 * D + FF :].reshape(6, D),
    )


def tuple_of(shards, layer_index):
    return (
        shards[0][layer_index],
        shards[1][layer_index],
        shards[2][layer_index],
        shards[3][layer_index],
        shards[4][layer_index],
    )


def fetch_forward(shards, layer_index):
    return lax.all_gather(as_sent(tuple_of(shards, layer_index)), ("dp", "seq"), axis=0, tiled=True)


def piece_of(left, right):
    product = left_dot(left, right).reshape(-1)
    return product


def reduce_grads(factors, widths):
    (
        hidden,
        d_packed,
        attended,
        d_branch_one,
        hidden_two,
        d_inner,
        active,
        d_branch_two,
        d_vector,
    ) = factors
    pairs = (
        (hidden, d_packed),
        (attended, d_branch_one),
        (hidden_two, d_inner),
        (active, d_branch_two),
    )
    block = sum(widths)
    blocks_here = lax.axis_size(("dp", "seq")) * block // block
    members = []
    for (left, right), term_width in zip(pairs, widths[:4]):
        piece = piece_of(left, right)
        members.append(piece.reshape(blocks_here, term_width))
    members.append(d_vector.reshape(blocks_here, widths[4]))
    owned = lax.psum_scatter(
        jnp.concatenate(members, axis=1).reshape(-1), ("dp", "seq"), scatter_dimension=0, tiled=True
    )
    results = []
    position = 0
    for width in widths:
        results.append(owned[position : position + width])
        position = position + width
    return tuple(results)


def mod_rows(modulation):
    return [modulation[:, number][:, None, None, :] for number in range(6)]


def layer_forward(tokens, cond, weight_set, temporal):
    w_qkv, w_out, w_one, w_two, bias_q, bias_v, bias_o, bias_one, bias_two, table = weight_set
    modulation = table[None] + cond
    rows_mod = mod_rows(modulation)
    leading = tokens.shape[:-1]
    head_shape = leading + (HEADS, HEAD_DIM)
    hidden = modulate(tokens, rows_mod[1], rows_mod[0]).astype(jnp.bfloat16).reshape(-1, D)
    packed = plain_dot(hidden, w_qkv)
    queries = (packed[:, :D] + bias_q).astype(jnp.bfloat16).reshape(head_shape)
    key_heads = packed[:, D : 2 * D].astype(jnp.bfloat16).reshape(head_shape)
    values = (packed[:, 2 * D :] + bias_v).astype(jnp.bfloat16).reshape(head_shape)
    score_form, mix_form, back_form = einsum_forms(temporal)
    scores = contract(score_form, queries, key_heads) * HEAD_DIM ** (-0.5)
    row_peak = jnp.max(scores, axis=-1, keepdims=True)
    exponent = jnp.exp(scores - row_peak)
    row_total = jnp.sum(exponent, axis=-1, keepdims=True)
    weights_soft = exponent / row_total
    log_total = row_peak + jnp.log(row_total)
    attended = (
        contract(mix_form, weights_soft.astype(jnp.bfloat16), values)
        .astype(jnp.bfloat16)
        .reshape(-1, D)
    )
    branch_one = (plain_dot(attended, w_out) + bias_o).reshape(leading + (D,))
    middle = tokens + rows_mod[2] * branch_one
    hidden_two = modulate(middle, rows_mod[4], rows_mod[3]).astype(jnp.bfloat16).reshape(-1, D)
    inner_sum = plain_dot(hidden_two, w_one) + bias_one
    active = jax.nn.gelu(inner_sum, approximate=True).astype(jnp.bfloat16)
    branch_two = (plain_dot(active, w_two) + bias_two).reshape(leading + (D,))
    result = middle + rows_mod[5] * branch_two
    stored = (
        tokens,
        modulation,
        hidden,
        queries,
        key_heads,
        values,
        log_total,
        attended,
        branch_one,
        middle,
        hidden_two,
        inner_sum,
        active,
        branch_two,
    )
    return (result, stored)


def layer_backward(grad_out, stored, weight_set, temporal):
    w_qkv, w_out, w_one, w_two = (weight_set[0], weight_set[1], weight_set[2], weight_set[3])
    (
        tokens,
        modulation,
        hidden,
        queries,
        key_heads,
        values,
        log_total,
        attended,
        branch_one,
        middle,
        hidden_two,
        inner_sum,
        active,
        branch_two,
    ) = stored
    rows_mod = mod_rows(modulation)
    leading = tokens.shape[:-1]
    clips_here = tokens.shape[0]
    d_gate_two = jnp.sum(grad_out * branch_two, axis=(1, 2))
    d_branch_two = (rows_mod[5] * grad_out).astype(jnp.bfloat16).reshape(-1, D)
    d_bias_two = jnp.sum(d_branch_two, axis=0, dtype=jnp.float32)
    d_active = right_dot(d_branch_two, w_two)
    unused_gelu, gelu_back = jax.vjp(
        lambda entries: jax.nn.gelu(entries, approximate=True), inner_sum
    )
    d_inner = gelu_back(d_active)[0].astype(jnp.bfloat16)
    d_bias_one = jnp.sum(d_inner, axis=0, dtype=jnp.float32)
    d_hidden_two = right_dot(d_inner, w_one).reshape(leading + (D,))
    unused_norm, norm_back = jax.vjp(modulate, middle, rows_mod[4], rows_mod[3])
    d_middle, d_scale_two, d_shift_two = norm_back(d_hidden_two)
    grad_mid = grad_out + d_middle
    d_gate_one = jnp.sum(grad_mid * branch_one, axis=(1, 2))
    d_branch_one = (rows_mod[2] * grad_mid).astype(jnp.bfloat16).reshape(-1, D)
    d_bias_o = jnp.sum(d_branch_one, axis=0, dtype=jnp.float32)
    d_attended = (
        right_dot(d_branch_one, w_out).astype(jnp.bfloat16).reshape(leading + (HEADS, HEAD_DIM))
    )
    score_form, mix_form, back_form = einsum_forms(temporal)
    scale_qk = HEAD_DIM ** (-0.5)
    scores = contract(score_form, queries, key_heads) * scale_qk
    weights_soft = jnp.exp(scores - log_total)
    d_values = contract(back_form, weights_soft.astype(jnp.bfloat16), d_attended)
    d_probs = contract(score_form, d_attended, values)
    d_scores = weights_soft * (d_probs - jnp.sum(weights_soft * d_probs, axis=-1, keepdims=True))
    d_scores = d_scores.astype(jnp.bfloat16)
    d_queries = contract(mix_form, d_scores, key_heads) * scale_qk
    d_keys = contract(back_form, d_scores, queries) * scale_qk
    d_packed = jnp.concatenate(
        [
            d_queries.reshape(-1, D).astype(jnp.bfloat16),
            d_keys.reshape(-1, D).astype(jnp.bfloat16),
            d_values.reshape(-1, D).astype(jnp.bfloat16),
        ],
        axis=1,
    )
    d_bias_q = jnp.sum(d_packed[:, :D], axis=0, dtype=jnp.float32)
    d_bias_v = jnp.sum(d_packed[:, 2 * D :], axis=0, dtype=jnp.float32)
    d_hidden = right_dot(d_packed, w_qkv).reshape(leading + (D,))
    unused_first, first_back = jax.vjp(modulate, tokens, rows_mod[1], rows_mod[0])
    d_input, d_scale_one, d_shift_one = first_back(d_hidden)
    d_input = grad_mid + d_input
    d_modulation = jnp.stack(
        [
            d_shift_one.reshape(clips_here, D),
            d_scale_one.reshape(clips_here, D),
            d_gate_one,
            d_shift_two.reshape(clips_here, D),
            d_scale_two.reshape(clips_here, D),
            d_gate_two,
        ],
        axis=1,
    )
    d_vector = jnp.concatenate(
        [
            d_bias_q,
            d_bias_v,
            d_bias_o,
            d_bias_one,
            d_bias_two,
            jnp.sum(d_modulation, axis=0).reshape(-1),
        ]
    )
    factors = (
        hidden,
        d_packed,
        attended,
        d_branch_one,
        hidden_two,
        d_inner,
        active,
        d_branch_two,
        d_vector,
    )
    return (d_input, factors, d_modulation)


SHIFTS = (1, 2, 3)
VMEM_BYTES = 50 * 2**20
STRIP = 384


def swap(x, axis):
    return lax.ppermute(x, axis, [(0, 1), (1, 0)])


def shift_z(x, k):
    n = lax.axis_size("z")
    return lax.ppermute(x, "z", [(i, (i + k) % n) for i in range(n)])


def gather_four(x, axis):
    far = swap(x, axis)
    return [x, swap(x, "core"), far, swap(far, "core")]


def scatter_four(partial, axis):
    kept_own, kept_far, sent = partial
    got = swap(sent, "core")
    far = (kept_far + got[1].astype(jnp.float32)).astype(jnp.bfloat16)
    return kept_own, got, swap(far, axis)


def source_of(number, side):
    z, here = lax.axis_index("z"), lax.axis_index(side)
    return 2 * ((z - number % 4 + 4) % 4) + (here + number // 4) % 2


def target_of(number, side):
    z, here = lax.axis_index("z"), lax.axis_index(side)
    return 2 * ((z + number % 4) % 4) + (here + number // 4) % 2


def padded(count, unit):
    return -(-count // unit) * unit


def whole():
    return pl.BlockSpec(memory_space=pltpu.VMEM)


def anywhere():
    return pl.BlockSpec(memory_space=pltpu.HBM)


def run(kernel, ins, outs, specs=None, scratch=(), flops=0):
    moved = sum(x.size * x.dtype.itemsize for x in list(ins) + list(outs))
    return pl.pallas_call(
        kernel,
        out_shape=tuple(outs),
        in_specs=specs or [whole()] * len(ins),
        out_specs=tuple([whole()] * len(outs)),
        scratch_shapes=list(scratch),
        compiler_params=pltpu.CompilerParams(vmem_limit_bytes=VMEM_BYTES),
        cost_estimate=pl.CostEstimate(flops=flops, bytes_accessed=moved, transcendentals=0),
    )(*ins)


def f32(*shape):
    return jax.ShapeDtypeStruct(shape, jnp.float32)


def bf16(*shape):
    return jax.ShapeDtypeStruct(shape, jnp.bfloat16)


def normal_parts(x):
    average = jnp.mean(x, axis=-1, keepdims=True)
    centred = x - average
    variance = jnp.mean(centred * centred, axis=-1, keepdims=True)
    inverse = lax.rsqrt(variance + EPSILON)
    return centred * inverse, inverse


def modulated(x, modulation, scale_row, order):
    normal, _ = normal_parts(x)
    scale = modulation[scale_row : scale_row + 1]
    shift = modulation[scale_row - 1 : scale_row]
    hidden = (normal * (1.0 + scale) + shift).astype(jnp.bfloat16)
    return plain_dot(hidden, order).astype(jnp.bfloat16)


def enter_kernel(x_ref, modulation_ref, order_ref, hidden_ref):
    x = x_ref[...].astype(jnp.float32)
    hidden_ref[...] = modulated(x, modulation_ref[...], 1, order_ref[...])


def summed(own_ref, got_ref, far_ref):
    return own_ref[...] + got_ref[0].astype(jnp.float32) + far_ref[...].astype(jnp.float32)


def middle_kernel(
    own_ref, got_ref, far_ref, bias_ref, x_ref, modulation_ref, order_ref, branch_ref, middle_ref, hidden_ref
):
    branch = summed(own_ref, got_ref, far_ref) + bias_ref[...]
    modulation = modulation_ref[...]
    middle = x_ref[...].astype(jnp.float32) + modulation[2:3] * branch
    branch_ref[...] = branch
    middle_ref[...] = middle
    hidden_ref[...] = modulated(middle, modulation, 4, order_ref[...])


def leave_kernel(own_ref, got_ref, far_ref, bias_ref, middle_ref, modulation_ref, branch_ref, result_ref):
    branch = summed(own_ref, got_ref, far_ref) + bias_ref[...]
    branch_ref[...] = branch
    result_ref[...] = (middle_ref[...] + modulation_ref[5:6] * branch).astype(jnp.bfloat16)


def start_rows(pieces, buffer, sems, first):
    copies = []
    for number, piece in enumerate(pieces):
        rows = piece.shape[0]
        copies.append(
            pltpu.make_async_copy(piece, buffer.at[pl.ds(number * rows, rows)], sems.at[first + number])
        )
        copies[-1].start()
    return copies


def start_weights(pieces, side, at, rows, buffer, sems, first):
    if len(pieces) == 1:
        found = [(pieces[0].at[number], number) for number in range(8)]
    else:
        found = [(piece, source_of(number, side)) for number, piece in enumerate(pieces)]
    copies = []
    for number, (piece, source) in enumerate(found):
        target = pl.multiple_of(source * rows, 16)
        copies.append(
            pltpu.make_async_copy(
                piece.at[pl.ds(at, rows)], buffer.at[pl.ds(target, rows)], sems.at[first + number]
            )
        )
        copies[-1].start()
    return copies


def wait_all(copies):
    for copy in copies:
        copy.wait()


def strips(size):
    return [(at, min(STRIP, size - at)) for at in range(0, size, STRIP)]


def deal(product, at, width, own_ref, far_ref, sent_ref):
    count = own_ref.shape[0]
    columns = slice(at, at + width)
    own_ref[:, columns] = product[:count]
    sent_ref[0, :, columns] = product[count : 2 * count].astype(jnp.bfloat16)
    far_ref[:, columns] = product[2 * count : 3 * count]
    sent_ref[1, :, columns] = product[3 * count :].astype(jnp.bfloat16)


def softmax_of(scores, count, period):
    if period:
        row = lax.broadcasted_iota(jnp.int32, scores.shape, 0) % period
        column = lax.broadcasted_iota(jnp.int32, scores.shape, 1) % period
        scores = jnp.where(row == column, scores, -1e30)
    exponent = jnp.exp(scores - jnp.max(scores, axis=-1, keepdims=True))
    return exponent * (1.0 / jnp.sum(exponent, axis=-1, keepdims=True))


def owners(width, per_head):
    return lax.broadcasted_iota(jnp.int32, (1, width), 1) // per_head


def by_head(x, owner, heads):
    return jnp.concatenate([jnp.where(owner == head, x, 0) for head in range(heads)], axis=0)


def of_head(stacked, owner, heads, count):
    chosen = stacked[:count]
    for head in range(1, heads):
        chosen = jnp.where(owner == head, stacked[head * count : (head + 1) * count], chosen)
    return chosen


def attention_kernel(period, heads, split, n_pieces, *refs):
    hidden, pieces, refs = refs[:4], refs[4 : 4 + n_pieces], refs[4 + n_pieces :]
    bias_ref, packed_ref, mixed_ref, probs_ref, own_ref, far_ref, sent_ref, left, qkv, out, sems = refs
    copies = start_rows(hidden, left, sems, 0)
    copies += start_weights(pieces, "x", 0, split, qkv, sems, 4)
    later = start_weights(pieces, "x", split, out.shape[0] // 8, out, sems, 12)
    wide = out.shape[0]
    narrow = (qkv.shape[1] - wide) // 2
    count = own_ref.shape[0]
    narrow_owner, wide_owner = owners(narrow, HEAD_DIM), owners(wide, wide // heads)
    wait_all(copies)
    for at, size in strips(qkv.shape[1]):
        product = plain_dot(left[...], qkv[:, at : at + size]) + bias_ref[:, at : at + size]
        packed_ref[:, at : at + size] = product.astype(jnp.bfloat16)
    for number in range(4):
        rows = pl.ds(number * count, count)
        packed = packed_ref[rows, :]
        values = packed[:, :wide]
        queries = by_head(packed[:, wide : wide + narrow], narrow_owner, heads)
        scores = right_dot(queries, packed[:, wide + narrow :]) * HEAD_DIM ** (-0.5)
        weights_soft = softmax_of(scores, count, period)
        probs_ref[pl.ds(number * heads * count, heads * count), :] = weights_soft
        mixed = plain_dot(weights_soft.astype(jnp.bfloat16), values)
        mixed_ref[rows, :] = of_head(mixed, wide_owner, heads, count).astype(jnp.bfloat16)
    wait_all(later)
    for at, size in strips(out.shape[1]):
        deal(plain_dot(mixed_ref[...], out[:, at : at + size]), at, size, own_ref, far_ref, sent_ref)


def attention_back_kernel(heads, split, n_pieces, *refs):
    d_branch, pieces, refs = refs[:4], refs[4 : 4 + n_pieces], refs[4 + n_pieces :]
    packed_ref, probs_ref, d_packed_ref, sums_ref, own_ref, far_ref, sent_ref, left, qkv, out, sems = refs
    copies = start_rows(d_branch, left, sems, 0)
    copies += start_weights(pieces, "x", split, out.shape[0] // 8, out, sems, 4)
    later = start_weights(pieces, "x", 0, split, qkv, sems, 12)
    wide = out.shape[0]
    narrow = (qkv.shape[1] - wide) // 2
    count = own_ref.shape[0]
    scale = HEAD_DIM ** (-0.5)
    narrow_owner, wide_owner = owners(narrow, HEAD_DIM), owners(wide, wide // heads)
    sums = jnp.zeros((1, wide + 2 * narrow), jnp.float32)
    wait_all(copies)
    d_mixed_all = right_dot(left[...], out[...]).astype(jnp.bfloat16)
    for number in range(4):
        rows = pl.ds(number * count, count)
        d_mixed = by_head(d_mixed_all[number * count : (number + 1) * count], wide_owner, heads)
        packed = packed_ref[rows, :]
        queries = by_head(packed[:, wide : wide + narrow], narrow_owner, heads)
        weights_soft = probs_ref[pl.ds(number * heads * count, heads * count), :]
        d_probs = right_dot(d_mixed, packed[:, :wide])
        inner = jnp.sum(weights_soft * d_probs, axis=-1, keepdims=True)
        d_scores = (weights_soft * (d_probs - inner)).astype(jnp.bfloat16)
        d_values = left_dot(weights_soft.astype(jnp.bfloat16), d_mixed)
        d_keys = left_dot(d_scores, queries)
        d_queries = of_head(
            plain_dot(d_scores, packed[:, wide + narrow :]), narrow_owner, heads, count
        )
        d_packed = jnp.concatenate([d_values, d_queries * scale, d_keys * scale], axis=1)
        d_packed = d_packed.astype(jnp.bfloat16)
        d_packed_ref[rows, :] = d_packed
        sums = sums + jnp.sum(d_packed.astype(jnp.float32), axis=0, keepdims=True)
    sums_ref[...] = sums
    wait_all(later)
    for at, size in strips(qkv.shape[0]):
        product = right_dot(d_packed_ref[...], qkv[at : at + size, :])
        deal(product, at, size, own_ref, far_ref, sent_ref)


def gelu_pair(u):
    inner = 0.7978845608028654 * (u + 0.044715 * u * u * u)
    bent = jnp.tanh(inner)
    value = 0.5 * u * (1.0 + bent)
    slope = 0.5 * (1.0 + bent) + 0.5 * u * (1.0 - bent * bent) * (
        0.7978845608028654 * (1.0 + 3 * 0.044715 * u * u)
    )
    return value, slope


def mlp_kernel(split, at_two, n_one, n_two, *refs):
    refs = list(refs)
    hidden, refs = refs[:4], refs[4:]
    pieces, refs = refs[:n_one], refs[n_one:]
    pieces_two, refs = refs[:n_two], refs[n_two:]
    bias_ref, active_ref, slope_ref, own_ref, far_ref, sent_ref, left, one, two, sems = refs
    copies = start_rows(hidden, left, sems, 0)
    copies += start_weights(pieces, "y", 0, split, one, sems, 4)
    later = start_weights(pieces_two, "y", at_two, two.shape[0] // 8, two, sems, 12)
    wait_all(copies)
    for at, size in strips(one.shape[1]):
        columns = slice(at, at + size)
        u = plain_dot(left[...], one[:, columns]) + bias_ref[:, columns]
        value, slope = gelu_pair(u)
        active_ref[:, columns] = value.astype(jnp.bfloat16)
        slope_ref[:, columns] = slope.astype(jnp.bfloat16)
    wait_all(later)
    for at, size in strips(two.shape[1]):
        deal(plain_dot(active_ref[...], two[:, at : at + size]), at, size, own_ref, far_ref, sent_ref)


def mlp_back_kernel(split, at_two, n_one, n_two, *refs):
    refs = list(refs)
    d_branch, refs = refs[:4], refs[4:]
    pieces, refs = refs[:n_one], refs[n_one:]
    pieces_two, refs = refs[:n_two], refs[n_two:]
    slope_ref, d_inner_ref, sums_ref, own_ref, far_ref, sent_ref, left, one, two, sems = refs
    copies = start_rows(d_branch, left, sems, 0)
    copies += start_weights(pieces_two, "y", at_two, two.shape[0] // 8, two, sems, 4)
    later = start_weights(pieces, "y", 0, split, one, sems, 12)
    wait_all(copies)
    for at, size in strips(two.shape[0]):
        columns = slice(at, at + size)
        d_active = right_dot(left[...], two[columns, :])
        d_inner = (d_active * slope_ref[:, columns].astype(jnp.float32)).astype(jnp.bfloat16)
        d_inner_ref[:, columns] = d_inner
        sums_ref[:, columns] = jnp.sum(d_inner.astype(jnp.float32), axis=0, keepdims=True)
    wait_all(later)
    for at, size in strips(one.shape[0]):
        product = right_dot(d_inner_ref[...], one[at : at + size, :])
        deal(product, at, size, own_ref, far_ref, sent_ref)


def total_sums(ref, *members):
    rows = [jnp.sum(m.astype(jnp.float32), axis=0, keepdims=True) for m in members]
    ref[...] = jnp.concatenate(rows, axis=0)


def open_back_kernel(grad_ref, branch_ref, modulation_ref, d_branch_ref, sums_ref):
    grad = grad_ref[...].astype(jnp.float32)
    d_branch = (modulation_ref[5:6] * grad).astype(jnp.bfloat16)
    d_branch_ref[...] = d_branch
    total_sums(sums_ref, grad * branch_ref[...], d_branch)


def natural(total, order):
    high = total.astype(jnp.bfloat16)
    low = (total - high.astype(jnp.float32)).astype(jnp.bfloat16)
    both = right_dot(jnp.concatenate([high, low], axis=0), order)
    return both[: total.shape[0]] + both[total.shape[0] :]


def norm_back(d_hidden, x, scale):
    normal, inverse = normal_parts(x)
    entry = d_hidden * (1.0 + scale)
    average = jnp.mean(entry, axis=-1, keepdims=True)
    along = jnp.mean(entry * normal, axis=-1, keepdims=True)
    return (entry - average - normal * along) * inverse, d_hidden * normal


def middle_back_kernel(
    own_ref, got_ref, far_ref, grad_ref, x_ref, branch_ref, modulation_ref, order_ref, d_branch_ref, grad_mid_ref, sums_ref
):
    d_hidden = natural(summed(own_ref, got_ref, far_ref), order_ref[...])
    modulation = modulation_ref[...]
    d_x, d_scale = norm_back(d_hidden, x_ref[...], modulation[4:5])
    grad_mid = grad_ref[...].astype(jnp.float32) + d_x
    grad_mid_ref[...] = grad_mid
    d_branch = (modulation[2:3] * grad_mid).astype(jnp.bfloat16)
    d_branch_ref[...] = d_branch
    total_sums(sums_ref, d_hidden, d_scale, grad_mid * branch_ref[...], d_branch)


def close_back_kernel(own_ref, got_ref, far_ref, grad_ref, x_ref, modulation_ref, order_ref, d_x_ref, sums_ref):
    d_hidden = natural(summed(own_ref, got_ref, far_ref), order_ref[...])
    d_x, d_scale = norm_back(d_hidden, x_ref[...].astype(jnp.float32), modulation_ref[1:2])
    d_x_ref[...] = (grad_ref[...] + d_x).astype(d_x_ref.dtype)
    total_sums(sums_ref, d_hidden, d_scale)


def factor(groups):
    pairs = [pair for members, _ in groups for pair in members]
    ins, scratch, flops = [], [], 0
    for left, right, height in pairs:
        ins += left + right
        count = sum(piece.shape[0] for piece in left)
        scratch.append(pltpu.VMEM((left[0].shape[1], count), jnp.bfloat16))
        if len(right) > 1:
            scratch.append(pltpu.VMEM((count, right[0].shape[1]), jnp.bfloat16))
        flops += 2 * count * left[0].shape[1] * right[0].shape[1]
    outs = []
    for members, side in groups:
        height, width = sum(m[2] for m in members), members[0][1][0].shape[1]
        outs += [bf16(height, width) for _ in range(8)] if side else [bf16(8 * height, width)]

    def kernel(*refs):
        refs = iter(refs)
        taken = [
            ([next(refs) for _ in left], [next(refs) for _ in right], height)
            for left, right, height in pairs
        ]
        results = [next(refs) for _ in outs]
        ready = []
        for left, right, height in taken:
            flip = next(refs)
            at = 0
            for piece in left:
                flip[:, at : at + piece.shape[0]] = piece[...].T
                at += piece.shape[0]
            lay = right[0]
            if len(right) > 1:
                lay = next(refs)
                at = 0
                for piece in right:
                    lay[at : at + piece.shape[0], :] = piece[...]
                    at += piece.shape[0]
            ready.append((flip, lay, height))
        for members, side in groups:
            mine, ready = ready[: len(members)], ready[len(members) :]
            total = sum(member[2] for member in mine)
            for number in range(8):
                at = 0 if side else number * total
                result = results[number] if side else results[0]
                target = target_of(number, side) if side else number
                for flip, lay, height in mine:
                    rows = pl.ds(pl.multiple_of(target * height, 16), height)
                    product = plain_dot(flip[rows, :], lay[...])
                    result[at : at + height, :] = product.astype(jnp.bfloat16)
                    at += height
            results = results[8:] if side else results[1:]

    results = list(run(kernel, ins, outs, scratch=scratch, flops=flops))
    given = []
    for _, side in groups:
        if side:
            given.append((results[:4], results[4:8]))
        else:
            given.append(results[0])
        results = results[8:] if side else results[1:]
    return given


def placed_blocks(half, n_seq):
    for owner in range(4 * n_seq):
        y, core, z, x = owner // (2 * n_seq), (owner // n_seq) % 2, (owner % n_seq) // 2, owner % 2
        yield owner * half, 2 * x + core, (2 * z + y) * half


def part_kernel(half, n_seq, rows_ref, parts_ref):
    rows = rows_ref.shape[1]
    for layer in range(2):
        for at, part, place in placed_blocks(half, n_seq):
            parts_ref[layer, part, 0:rows, place : place + half] = rows_ref[layer, :, at : at + half]
        for part in range(4):
            parts_ref[layer, part, rows:, :] = jnp.zeros(
                (parts_ref.shape[2] - rows, parts_ref.shape[3]), parts_ref.dtype
            )


def join_kernel(half, n_seq, room, parts_ref, rows_ref):
    rows = rows_ref.shape[1]
    for layer in range(2):
        for at, part, place in placed_blocks(half, n_seq):
            block = parts_ref[part, layer * room : layer * room + rows, place : place + half]
            rows_ref[layer, :, at : at + half] = block.astype(jnp.float32)


def vector_kernel(
    n_seq, rows, sums_one_ref, sums_mid_ref, sums_two_ref, qkv_ref, one_ref, vector_ref, modulation_ref
):
    y, core, x = lax.axis_index("y"), lax.axis_index("core"), lax.axis_index("x")
    here = 2 * y + core
    room = padded(rows, 16)
    wide, width, half = n_seq * room, n_seq * rows, one_ref.shape[1] // n_seq
    for number in range(4):
        mine = here == number
        query = qkv_ref[:, wide : wide + width]
        vector_ref[:, number * width : (number + 1) * width] = jnp.where(mine, query, 0.0)
        for block in range(n_seq):
            at = D + number * width + block * rows
            value = qkv_ref[:, block * room : block * room + rows]
            vector_ref[:, at : at + rows] = jnp.where(mine, value, 0.0)
    for owner in range(4 * n_seq):
        mine = ((owner // n_seq) % 2 == core) & (owner % 2 == x)
        block = 2 * ((owner % n_seq) // 2) + owner // (2 * n_seq)
        at = 3 * D + owner * half
        vector_ref[:, at : at + half] = jnp.where(mine, one_ref[:, block * half : (block + 1) * half], 0.0)
    vector_ref[:, 2 * D : 3 * D] = sums_mid_ref[3:4]
    vector_ref[:, 3 * D + FF : 4 * D + FF] = sums_two_ref[1:2]
    members = (
        (sums_one_ref, 0),
        (sums_one_ref, 1),
        (sums_mid_ref, 2),
        (sums_mid_ref, 0),
        (sums_mid_ref, 1),
        (sums_two_ref, 0),
    )
    for number, (ref, row) in enumerate(members):
        at = (4 + number) * D + FF
        vector_ref[:, at : at + D] = ref[row : row + 1]
        modulation_ref[number : number + 1, :] = ref[row : row + 1]


def order_matrix(n_dp, n_seq, rows, room, crossed):
    place = lax.broadcasted_iota(jnp.int32, (D, n_dp * n_seq * room), 1)
    feature = lax.broadcasted_iota(jnp.int32, (D, n_dp * n_seq * room), 0)
    block, inner = place // room, place % room
    outer, local = block // n_dp, block % n_dp
    z, side, across, core = outer // 2, outer % 2, local // 2, local % 2
    x, y = (across, side) if crossed else (side, across)
    owner = (2 * y + core) * n_seq + 2 * z + x
    return ((feature == owner * rows + inner) & (inner < rows)).astype(jnp.bfloat16)


def grow(x, axis, size):
    pads = [(0, 0)] * x.ndim
    pads[axis] = (0, size - x.shape[axis])
    return jnp.pad(x, pads)


def exchange(parts, axis):
    return lax.all_to_all(parts, (axis, "core"), split_axis=0, concat_axis=0, tiled=True)


def spread(values, n_seq, rows, room):
    lead = values.shape[:-1]
    return grow(values.reshape(lead + (n_seq, rows)), len(lead) + 1, room).reshape(lead + (-1,))


def ordered_vectors(everyone, n_dp, n_seq, count):
    chosen = owner_rows(n_dp, n_seq, -1)
    ordered = left_dot(chosen.astype(jnp.bfloat16), everyone)
    return ordered.reshape(n_dp * n_seq, 2, count).transpose(1, 0, 2).reshape(2, -1)


def owner_rows(n_dp, n_seq, sign):
    count = n_dp * n_seq
    relative = lax.broadcasted_iota(jnp.int32, (count, count), 0)
    owner = lax.broadcasted_iota(jnp.int32, (count, count), 1)
    n_z = n_seq // 2
    z = (lax.axis_index("z") + sign * (relative // (2 * n_dp)) + n_z) % n_z
    x = lax.axis_index("x") ^ ((relative // n_dp) % 2)
    y = lax.axis_index("y") ^ ((relative // 2) % 2)
    core = lax.axis_index("core") ^ (relative % 2)
    source = (2 * y + core) * n_seq + 2 * z + x
    return (owner == source).astype(jnp.float32)


def scatter_vectors(sums, n_dp, n_seq, finish):
    count = sums.shape[1] // (n_dp * n_seq)
    rows = sums.reshape(2, n_dp * n_seq, count).transpose(1, 0, 2).reshape(n_dp * n_seq, -1)
    chosen = owner_rows(n_dp, n_seq, 1)
    rows = jnp.dot(chosen, rows, precision=lax.Precision.HIGHEST)
    quarters = jnp.split(rows, n_seq // 2)
    got = yield (quarters[0], [shift_z(quarters[k], k) for k in SHIFTS])
    total = got[0] + sum(got[1])
    got = yield (total, swap(total[n_dp:], "x"))
    total = got[0][:n_dp] + got[1]
    got = yield (total, swap(total[2:], "y"))
    total = got[0][:2] + got[1]
    got = yield (total, swap(total[1:], "core"))
    finish((got[0][:1] + got[1]).reshape(2, count))
    yield None


def sum_seq(x, finish):
    got = yield (x, swap(x, "x"))
    total = got[0] + got[1]
    got = yield (total, [shift_z(total, k) for k in SHIFTS])
    finish(got[0] + sum(got[1]))
    yield None


def slice_of(vector, n_dp):
    width = vector.shape[0] // n_dp
    here = 2 * lax.axis_index("y") + lax.axis_index("core")
    return lax.dynamic_slice(vector, (here * width,), (width,))


def crossed_slice(vector, n_z):
    blocks = vector.reshape(2, 2, n_z, 2, -1)
    blocks = lax.dynamic_index_in_dim(blocks, lax.axis_index("x"), 3, keepdims=False)
    blocks = lax.dynamic_index_in_dim(blocks, lax.axis_index("core"), 1, keepdims=False)
    return blocks.transpose(1, 0, 2).reshape(-1)


class Gather:
    def __init__(self, pieces, side):
        self.side = side
        self.column, self.across, self.sent, self.waiting = [pieces], [], 0, False

    def wants_x(self):
        return self.sent < len(self.column)

    def send_x(self):
        self.sent += 1
        return [swap(piece, self.side) for piece in self.column[self.sent - 1]]

    def got_x(self, pieces):
        self.across.append(pieces)

    def wants_z(self):
        return len(self.column) < 4 and not self.waiting

    def send_z(self):
        self.waiting = True
        return [shift_z(piece, 1) for piece in self.column[-1]]

    def got_z(self, pieces):
        self.waiting = False
        self.column.append(pieces)

    def finished(self):
        return len(self.across) == 4

    def pieces(self, index):
        return [piece[index] for piece in self.column + self.across]


class Reduce:
    def __init__(self, mine, other, side, wait, finish):
        self.side, self.wait = side, wait
        self.mine, self.other, self.finish = mine, other, finish
        self.sent, self.got, self.hops, self.carried, self.result = 3, {}, 3, None, None

    def wants_x(self):
        return self.sent >= 0

    def send_x(self):
        self.sent -= 1
        return [swap(piece, self.side) for piece in self.other[self.sent + 1]]

    def got_x(self, pieces):
        self.got[3 - len(self.got)] = pieces

    def added(self, k):
        total = [m.astype(jnp.float32) + g.astype(jnp.float32) for m, g in zip(self.mine[k], self.got[k])]
        if k < 3:
            total = [t + c.astype(jnp.float32) for t, c in zip(total, self.carried)]
        return total

    def wants_z(self):
        ready = self.hops == 3 or self.carried is not None
        return self.hops > 0 and self.hops in self.got and ready

    def send_z(self):
        total = self.added(self.hops)
        self.hops -= 1
        self.carried = None
        return [shift_z(t.astype(jnp.bfloat16), 1) for t in total]

    def got_z(self, pieces):
        self.carried = pieces

    def finished(self):
        return self.hops == 0 and self.carried is not None and 0 in self.got


class Lane:
    def __init__(self):
        self.jobs, self.flight, self.extra, self.scripts = [], [], [], []

    def issue(self):
        for job in [job for job in self.jobs if isinstance(job, Reduce)]:
            if job.wants_x():
                self.flight.append((job.wait, job, "x", job.send_x()))
            if job.wants_z():
                self.flight.append((1, job, "z", job.send_z()))
        busy = set()
        for job in [job for job in self.jobs if isinstance(job, Gather)]:
            for kind, link in (("x", job.side), ("z", "z")):
                if link not in busy and getattr(job, "wants_" + kind)():
                    busy.add(link)
                    self.flight.append((1, job, kind, getattr(job, "send_" + kind)()))
        for script in self.scripts:
            script[1] = script[0].send(script[1])
        self.scripts = [script for script in self.scripts if script[1] is not None]

    def add(self, mine, other, side, wait, finish):
        job = Reduce([[m] for m in mine], [[m] for m in other], side, wait, finish)
        self.jobs.append(job)
        self.flight.append((wait, job, "x", job.send_x()))

    def close(self):
        for job in [job for job in self.jobs if job.finished()]:
            self.jobs.remove(job)
            if isinstance(job, Reduce):
                job.finish(job.added(0))

    def tick(self, values):
        due = [f for f in self.flight if f[0] == 1]
        values, arrived, _, steps = lax.optimization_barrier(
            (values, [f[3] for f in due], self.extra, [script[1] for script in self.scripts])
        )
        for script, step in zip(self.scripts, steps):
            script[1] = step
        self.flight = [(f[0] - 1,) + f[1:] for f in self.flight if f[0] > 1]
        self.extra = []
        for (_, job, kind, _), pieces in zip(due, arrived):
            getattr(job, "got_" + kind)(pieces)
        self.close()
        self.issue()
        return values

    def until(self, job, values):
        while not job.finished():
            values = self.tick(values)
        return values


def on_device_split(tokens, cond, d_out, attn_in, attn_out, mlp_in, mlp_out, vectors):
    n_dp, n_seq = 4, 2 * lax.axis_size("z")
    heads = HEADS // n_dp
    width = heads * HEAD_DIM
    frames, places = tokens.shape[1] * n_seq, tokens.shape[2]
    periods = (0, places // n_seq)
    count = tokens.shape[1] * places
    group = n_dp * count
    rows = D // (n_dp * n_seq)
    room = padded(rows, 8)
    out_room = padded(rows, 16)
    deep, wide = n_dp * n_seq * room, n_seq * out_room
    narrow = padded(width, 128)
    packed_width = wide + 2 * narrow
    inner = FF // n_dp
    split = n_dp * room
    half = inner // n_seq
    order = order_matrix(n_dp, n_seq, rows, room, False)
    order_mlp = order_matrix(n_dp, n_seq, rows, room, True)

    parts = attn_in.reshape(2, rows, 3, n_dp, width).transpose(2, 0, 3, 1, 4)
    qkv_parts = jnp.concatenate(
        [spread(parts[2], n_seq, rows, out_room), grow(parts[0], 3, narrow), grow(parts[1], 3, narrow)],
        axis=3,
    )
    qkv_parts = grow(qkv_parts, 2, room)
    out_parts = grow(attn_out.reshape(2, rows, D), 1, out_room)
    two_parts = mlp_out.reshape(2, half, D)
    qkv_parts, out_parts, two_parts = lax.optimization_barrier((qkv_parts, out_parts, two_parts))

    def attention_piece(index):
        return jnp.concatenate([exchange(qkv_parts[index], "y").reshape(-1, packed_width), out_parts[index]])

    def regroup(x):
        x = x.reshape(n_seq, count // n_seq, D)
        return lax.all_to_all(x, ("z", "x"), split_axis=0, concat_axis=0, tiled=True).reshape(-1, D)

    lane = Lane()
    mine = vectors.reshape(1, -1)
    near = jnp.concatenate([mine, swap(mine, "core")])
    clips = jnp.concatenate([near, swap(near, "y")])
    pair = jnp.concatenate([clips, swap(clips, "x")])
    everyone = jnp.concatenate([pair] + [shift_z(pair, k) for k in SHIFTS])
    first = attention_piece(0)
    mlp_in = mlp_in.reshape(2, rows, FF)
    everyone, first, mlp_in, qkv_parts, out_parts, two_parts = lax.optimization_barrier(
        (everyone, first, mlp_in, qkv_parts, out_parts, two_parts)
    )
    attention_job = Gather([first], "x")
    lane.jobs.append(attention_job)
    lane.issue()
    (one_parts,) = run(
        functools.partial(part_kernel, half, n_seq), [mlp_in], [bf16(2, n_dp, room, inner)]
    )
    vector = ordered_vectors(everyone, n_dp, n_seq, vectors.shape[1])
    biases, modulations = [], []
    for index in range(2):
        v = vector[index]
        bias_q, bias_v = slice_of(v[0:D], n_dp), slice_of(v[D : 2 * D], n_dp)
        bias_q = grow(bias_q, 0, narrow)
        bias_v = spread(bias_v, n_seq, rows, out_room)
        biases.append(
            (
                jnp.concatenate([bias_v, bias_q, jnp.zeros_like(bias_q)])[None],
                v[None, 2 * D : 3 * D],
                crossed_slice(v[3 * D : 3 * D + FF], n_seq // 2)[None],
                v[None, 3 * D + FF : 4 * D + FF],
            )
        )
        modulations.append(v[4 * D + FF :].reshape(6, D) + cond[0])

    def scratch(left_width, *shapes):
        return [
            pltpu.VMEM((group, left_width), jnp.bfloat16),
            *[pltpu.VMEM(shape, jnp.bfloat16) for shape in shapes],
            pltpu.SemaphoreType.DMA((20,)),
        ]

    attention_rooms = ((deep, packed_width), (wide, D))
    mlp_rooms = ((deep, inner), (inner, D))
    attention_flops = 4 * group * (deep * packed_width + wide * D)
    mlp_flops = 2 * group * (deep + D) * inner
    own_shapes = [f32(count, D), f32(count, D), bf16(2, count, D)]
    deep_shapes = [f32(count, deep), f32(count, deep), bf16(2, count, deep)]

    def opened(x, index):
        return run(enter_kernel, [x, modulations[index], order], [bf16(count, deep)])[0]

    def attention(index, hidden, pieces):
        return run(
            functools.partial(attention_kernel, periods[index], heads, split, len(pieces)),
            hidden + pieces + [biases[index][0]],
            [bf16(group, packed_width), bf16(group, wide), f32(group * heads, count)] + own_shapes,
            specs=[anywhere()] * (4 + len(pieces)) + [whole()],
            scratch=scratch(deep, *attention_rooms),
            flops=attention_flops,
        )

    def attention_back(index, d_branch, pieces, packed, probs):
        return run(
            functools.partial(attention_back_kernel, heads, split, len(pieces)),
            d_branch + pieces + [packed, probs],
            [bf16(group, packed_width), f32(1, packed_width)] + deep_shapes,
            specs=[anywhere()] * (4 + len(pieces)) + [whole()] * 2,
            scratch=scratch(D, *attention_rooms),
            flops=attention_flops,
        )

    def middle(index, own, x):
        return run(
            middle_kernel,
            list(own) + [biases[index][1], x, modulations[index], order_mlp],
            [f32(count, D), f32(count, D), bf16(count, deep)],
        )

    def mlp(index, hidden, pieces, pieces_two, at):
        return run(
            functools.partial(mlp_kernel, split, at, len(pieces), len(pieces_two)),
            hidden + pieces + pieces_two + [biases[index][2]],
            [bf16(group, inner), bf16(group, inner)] + own_shapes,
            specs=[anywhere()] * (4 + len(pieces) + len(pieces_two)) + [whole()],
            scratch=scratch(deep, *mlp_rooms),
            flops=mlp_flops,
        )

    def mlp_back(d_branch, pieces, pieces_two, at, slope):
        return run(
            functools.partial(mlp_back_kernel, split, at, len(pieces), len(pieces_two)),
            d_branch + pieces + pieces_two + [slope],
            [bf16(group, inner), f32(1, inner)] + deep_shapes,
            specs=[anywhere()] * (4 + len(pieces) + len(pieces_two)) + [whole()],
            scratch=scratch(D, *mlp_rooms),
            flops=mlp_flops,
        )

    def left(index, own, x):
        return run(
            leave_kernel,
            list(own) + [biases[index][3], x, modulations[index]],
            [f32(count, D), bf16(count, D)],
        )

    def opened_back(index, grad, branch):
        return run(
            open_back_kernel, [grad, branch, modulations[index]], [bf16(count, D), f32(2, D)]
        )

    def middle_back(index, own, grad, x, branch):
        return run(
            middle_back_kernel,
            list(own) + [grad, x, branch, modulations[index], order_mlp],
            [bf16(count, D), f32(count, D), f32(4, D)],
        )

    def closed_back(index, own, grad, x, out_type):
        return run(
            close_back_kernel,
            list(own) + [grad, x, modulations[index], order],
            [jax.ShapeDtypeStruct((count, D), out_type), f32(2, D)],
        )

    def vector_sums(sums_one, sums_mid, sums_two, d_bias_qkv, d_bias_one):
        return run(
            functools.partial(vector_kernel, n_seq, rows),
            [sums_one, sums_mid, sums_two, d_bias_qkv, d_bias_one],
            [f32(1, 10 * D + FF), f32(6, D)],
        )

    x_zero = tokens.reshape(-1, D)
    hidden, one_parts, two_parts = lane.tick((opened(x_zero, 0), one_parts, two_parts))
    two_zero = [lax.all_gather(two_parts[0], ("z", "y"))]
    piece = exchange(one_parts[0], "x").reshape(-1, inner)
    hidden_zero, piece = lane.tick((gather_four(hidden, "y"), piece))
    mlp_job = Gather([piece], "y")
    lane.jobs.append(mlp_job)
    hidden_zero, one_parts = lane.tick((hidden_zero, one_parts))
    later = jnp.concatenate([exchange(one_parts[1], "x").reshape(-1, inner), two_parts[1]])
    hidden_zero = lane.until(attention_job, hidden_zero)
    attention_zero = attention_job.pieces(0)
    packed_zero, mixed_zero, probs_zero, *partial = attention(0, hidden_zero, attention_zero)
    partial, later, qkv_parts, out_parts = lane.tick((partial, later, qkv_parts, out_parts))
    mlp_one = [lax.all_gather(later, ("z", "y"))]
    piece = attention_piece(1)
    own, piece = lane.tick((scatter_four(partial, "y"), piece))
    next_job = Gather([piece], "x")
    lane.jobs.append(next_job)
    branch_zero, middle_zero, hidden = middle(0, own, x_zero)
    inside_zero = lane.until(mlp_job, lane.tick(gather_four(hidden, "x")))
    mlp_zero = mlp_job.pieces(0)
    active_zero, slope_zero, *partial = mlp(0, inside_zero, mlp_zero, two_zero, 0)
    own = lane.tick(scatter_four(lane.tick(partial), "x"))
    end_zero, result = left(0, own, middle_zero)

    x_one = lane.tick(regroup(result))
    hidden_one = lane.until(next_job, lane.tick(gather_four(opened(x_one, 1), "y")))
    attention_one = next_job.pieces(0)
    packed_one, mixed_one, probs_one, *partial = attention(1, hidden_one, attention_one)
    partial, d_out = lax.optimization_barrier((partial, d_out))
    grad_places = regroup(d_out.reshape(-1, D))
    branch_one, middle_one, hidden = middle(1, scatter_four(partial, "y"), x_one)
    inside_one, grad_places = lax.optimization_barrier((gather_four(hidden, "x"), grad_places))
    active_one, slope_one, *partial = mlp(1, inside_one, mlp_one, mlp_one, split)
    end_one, result = left(1, scatter_four(partial, "x"), middle_one)
    output = regroup(result).astype(jnp.float32)

    d_end, sums_two = opened_back(1, grad_places, end_one)
    d_end = gather_four(d_end, "x")
    d_inner, d_bias_one, *partial = mlp_back(d_end, mlp_one, mlp_one, split, slope_one)
    partial, output = lax.optimization_barrier((partial, output))
    owned = {}

    def keep(name):
        return functools.partial(owned.__setitem__, name)

    (d_mlp,) = factor(
        [([(inside_one, [d_inner], split), ([active_one], d_end, half)], None)]
    )
    own, d_mlp = lax.optimization_barrier((scatter_four(partial, "x"), d_mlp))
    d_mlp_one = lax.psum_scatter(d_mlp, ("z", "y"), scatter_dimension=0, tiled=True)
    d_branch, grad_mid, sums_mid = middle_back(1, own, grad_places, middle_one, branch_one)
    d_branch_one = gather_four(d_branch, "y")
    d_packed, d_bias_qkv, *partial = attention_back(
        1, d_branch_one, attention_one, packed_one, probs_one
    )
    (ring,) = factor(
        [([(hidden_one, [d_packed], split), ([mixed_one], d_branch_one, out_room)], "x")]
    )
    own, ring = lax.optimization_barrier((scatter_four(partial, "y"), ring))
    grad, sums_one = closed_back(1, own, grad_mid, x_one, jnp.bfloat16)
    vector_one, modulation_one = vector_sums(sums_one, sums_mid, sums_two, d_bias_qkv, d_bias_one)

    def finish_mlp(totals):
        total = totals[0]
        ones = jnp.concatenate(
            [x[:split].astype(jnp.bfloat16).reshape(n_dp, room, -1) for x in (total, d_mlp_one)],
            axis=1,
        )
        (joined,) = run(
            functools.partial(join_kernel, half, n_seq, room),
            [exchange(ones, "x")],
            [f32(2, rows, FF)],
        )
        owned["one"] = joined.reshape(2, -1)
        owned["two"] = jnp.stack([total[split:], d_mlp_one[split:].astype(jnp.float32)]).reshape(2, -1)

    def finish_attention(totals):
        pair = (totals[0], owned["attention later"][0])
        both = jnp.concatenate(
            [x[:split].astype(jnp.bfloat16).reshape(n_dp, room, -1) for x in pair], axis=1
        )
        both = exchange(both, "y").reshape(n_dp, 2, room, packed_width)[:, :, :rows]
        values = both[..., :wide].reshape(n_dp, 2, rows, n_seq, out_room)[..., :rows]
        joined = jnp.stack(
            [
                both[..., wide : wide + width],
                both[..., wide + narrow : wide + narrow + width],
                values.reshape(n_dp, 2, rows, width),
            ]
        )
        owned["qkv"] = joined.transpose(2, 3, 0, 1, 4).astype(jnp.float32).reshape(2, -1)
        owned["out"] = jnp.stack(
            [x[split : split + rows].astype(jnp.float32) for x in pair]
        ).reshape(2, -1)

    grad_frames, ring = lax.optimization_barrier((regroup(grad), ring))
    lane.add(*ring, "x", 2, keep("attention later"))
    d_end, sums_two = opened_back(0, grad_frames, end_zero)
    d_end = lane.tick(gather_four(d_end, "x"))
    d_inner, d_bias_one, *partial = mlp_back(d_end, mlp_zero, two_zero, 0, slope_zero)
    partial = lane.tick(partial)
    (ring,) = factor(
        [([(inside_zero, [d_inner], split), ([active_zero], d_end, half)], "y")]
    )
    lane.add(*ring, "y", 1, finish_mlp)
    own = lane.tick(scatter_four(partial, "x"))
    d_branch, grad_mid, sums_mid = middle_back(0, own, grad_frames, middle_zero, branch_zero)
    d_branch = lane.tick(gather_four(d_branch, "y"))
    d_packed, d_bias_qkv, *partial = attention_back(
        0, d_branch, attention_zero, packed_zero, probs_zero
    )
    partial = lane.tick(partial)
    (ring,) = factor(
        [([(hidden_zero, [d_packed], split), ([mixed_zero], d_branch, out_room)], "x")]
    )
    lane.add(*ring, "x", 1, finish_attention)
    lane.extra.append((ring, d_mlp_one))
    own = lane.tick(scatter_four(partial, "y"))
    d_tokens, sums_one = closed_back(0, own, grad_mid, x_zero, jnp.float32)
    vector_zero, modulation_zero = vector_sums(sums_one, sums_mid, sums_two, d_bias_qkv, d_bias_one)

    lane.scripts += [
        [scatter_vectors(jnp.concatenate([vector_zero, vector_one]), n_dp, n_seq, keep("vectors")), None],
        [sum_seq(modulation_zero + modulation_one, keep("cond")), None],
    ]
    while lane.jobs or lane.scripts:
        lane.tick(())
    return (
        output.reshape(tokens.shape),
        d_tokens.reshape(tokens.shape),
        owned["cond"][None],
        *[owned[name] for name in ("qkv", "out", "one", "two")],
        owned["vectors"],
    )


def on_device(tokens, cond, d_out, attn_in, attn_out, mlp_in, mlp_out, vectors):
    shards = (attn_in, attn_out, mlp_in, mlp_out, vectors)
    widths = (
        attn_in.shape[1],
        attn_out.shape[1],
        mlp_in.shape[1],
        mlp_out.shape[1],
        vectors.shape[1],
    )
    layer_zero = unpack(fetch_forward(shards, 0))
    spatial_out, stored_zero = layer_forward(tokens.astype(jnp.float32), cond, layer_zero, False)
    by_place = lax.all_to_all(
        spatial_out.astype(jnp.bfloat16), "seq", split_axis=2, concat_axis=1, tiled=True
    ).astype(spatial_out.dtype)
    layer_one = unpack(fetch_forward(shards, 1))
    temporal_out, stored_one = layer_forward(by_place, cond, layer_one, True)
    output = lax.all_to_all(
        temporal_out.astype(jnp.bfloat16), "seq", split_axis=1, concat_axis=2, tiled=True
    ).astype(temporal_out.dtype)
    grad_places = lax.all_to_all(d_out, "seq", split_axis=2, concat_axis=1, tiled=True).astype(
        jnp.float32
    )
    grad_mid, factors_one, modul_one = layer_backward(grad_places, stored_one, layer_one, True)
    owned_one = reduce_grads(factors_one, widths)
    grad_frames = lax.all_to_all(
        grad_mid.astype(jnp.bfloat16), "seq", split_axis=1, concat_axis=2, tiled=True
    ).astype(grad_mid.dtype)
    d_tokens, factors_zero, modul_zero = layer_backward(grad_frames, stored_zero, layer_zero, False)
    owned_zero = reduce_grads(factors_zero, widths)
    d_cond = lax.psum(modul_zero + modul_one, "seq")
    stacked = tuple((jnp.stack([former, latter]) for former, latter in zip(owned_zero, owned_one)))
    return (output, d_tokens, d_cond, stacked[0], stacked[1], stacked[2], stacked[3], stacked[4])


def solution(mesh):
    n_dp, n_seq = mesh.shape["dp"], mesh.shape["seq"]
    split = n_dp == 4 and n_seq == 8
    clips, frames = "dp", "seq"
    if split:
        devices = mesh.devices.reshape(n_dp // 2, 2, n_seq // 2, 2)
        mesh = jax.sharding.Mesh(devices, ("y", "core", "z", "x"))
        clips, frames = ("y", "core"), ("z", "x")
    everyone = P(None, ("y", "core", "z", "x") if split else ("dp", "seq"))
    tokens, cond = P(clips, frames, None, None), P(clips, None, None)
    return jax.shard_map(
        on_device_split if split else on_device,
        mesh=mesh,
        in_specs=(tokens, cond, tokens) + (everyone,) * 5,
        out_specs=(tokens, tokens, cond) + (everyone,) * 5,
        check_vma=False,
    )
```

```python
import functools

import jax
import jax.numpy as jnp
from jax import lax
from jax.experimental import pallas as pl
from jax.experimental.pallas import tpu as pltpu
from jax.sharding import PartitionSpec as P

D = 1152
HEADS = 16
HEAD_DIM = 72
FF = 4608


EPSILON = 1e-06


def as_sent(x):

    def short(part):
        return part.astype(jnp.bfloat16) if part.dtype == jnp.float32 else part

    return jax.tree.map(short, x)


def modulate(tokens, scale, shift):
    average = jnp.mean(tokens, axis=-1, keepdims=True)
    centred = tokens - average
    variance = jnp.mean(centred * centred, axis=-1, keepdims=True)
    return centred * lax.rsqrt(variance + EPSILON) * (1.0 + scale) + shift


def plain_dot(former, latter):
    return jnp.dot(former, latter, preferred_element_type=jnp.float32)


def left_dot(former, latter):
    return lax.dot_general(
        former, latter, (((0,), (0,)), ((), ())), preferred_element_type=jnp.float32
    )


def right_dot(former, latter):
    return lax.dot_general(
        former, latter, (((1,), (1,)), ((), ())), preferred_element_type=jnp.float32
    )


def contract(form, former, latter):
    return jnp.einsum(form, former, latter, preferred_element_type=jnp.float32)


def einsum_forms(temporal):
    if temporal:
        return ("aibhe,ajbhe->abhij", "abhij,ajbhe->aibhe", "abhij,aibhe->ajbhe")
    return ("abihe,abjhe->abhij", "abhij,abjhe->abihe", "abhij,abihe->abjhe")


def unpack(pieces):
    attn_in, attn_out, mlp_in, mlp_out, vector = pieces
    vector = vector.astype(jnp.float32)
    return (
        attn_in.reshape(D, 3 * D),
        attn_out.reshape(D, D),
        mlp_in.reshape(D, FF),
        mlp_out.reshape(FF, D),
        vector[0:D],
        vector[D : 2 * D],
        vector[2 * D : 3 * D],
        vector[3 * D : 3 * D + FF],
        vector[3 * D + FF : 4 * D + FF],
        vector[4 * D + FF :].reshape(6, D),
    )


def tuple_of(shards, layer_index):
    return (
        shards[0][layer_index],
        shards[1][layer_index],
        shards[2][layer_index],
        shards[3][layer_index],
        shards[4][layer_index],
    )


def fetch_forward(shards, layer_index):
    return lax.all_gather(as_sent(tuple_of(shards, layer_index)), ("dp", "seq"), axis=0, tiled=True)


def piece_of(left, right):
    product = left_dot(left, right).reshape(-1)
    return product


def reduce_grads(factors, widths):
    (
        hidden,
        d_packed,
        attended,
        d_branch_one,
        hidden_two,
        d_inner,
        active,
        d_branch_two,
        d_vector,
    ) = factors
    pairs = (
        (hidden, d_packed),
        (attended, d_branch_one),
        (hidden_two, d_inner),
        (active, d_branch_two),
    )
    block = sum(widths)
    blocks_here = lax.axis_size(("dp", "seq")) * block // block
    members = []
    for (left, right), term_width in zip(pairs, widths[:4]):
        piece = piece_of(left, right)
        members.append(piece.reshape(blocks_here, term_width))
    members.append(d_vector.reshape(blocks_here, widths[4]))
    owned = lax.psum_scatter(
        jnp.concatenate(members, axis=1).reshape(-1), ("dp", "seq"), scatter_dimension=0, tiled=True
    )
    results = []
    position = 0
    for width in widths:
        results.append(owned[position : position + width])
        position = position + width
    return tuple(results)


def mod_rows(modulation):
    return [modulation[:, number][:, None, None, :] for number in range(6)]


def layer_forward(tokens, cond, weight_set, temporal):
    w_qkv, w_out, w_one, w_two, bias_q, bias_v, bias_o, bias_one, bias_two, table = weight_set
    modulation = table[None] + cond
    rows_mod = mod_rows(modulation)
    leading = tokens.shape[:-1]
    head_shape = leading + (HEADS, HEAD_DIM)
    hidden = modulate(tokens, rows_mod[1], rows_mod[0]).astype(jnp.bfloat16).reshape(-1, D)
    packed = plain_dot(hidden, w_qkv)
    queries = (packed[:, :D] + bias_q).astype(jnp.bfloat16).reshape(head_shape)
    key_heads = packed[:, D : 2 * D].astype(jnp.bfloat16).reshape(head_shape)
    values = (packed[:, 2 * D :] + bias_v).astype(jnp.bfloat16).reshape(head_shape)
    score_form, mix_form, back_form = einsum_forms(temporal)
    scores = contract(score_form, queries, key_heads) * HEAD_DIM ** (-0.5)
    row_peak = jnp.max(scores, axis=-1, keepdims=True)
    exponent = jnp.exp(scores - row_peak)
    row_total = jnp.sum(exponent, axis=-1, keepdims=True)
    weights_soft = exponent / row_total
    log_total = row_peak + jnp.log(row_total)
    attended = (
        contract(mix_form, weights_soft.astype(jnp.bfloat16), values)
        .astype(jnp.bfloat16)
        .reshape(-1, D)
    )
    branch_one = (plain_dot(attended, w_out) + bias_o).reshape(leading + (D,))
    middle = tokens + rows_mod[2] * branch_one
    hidden_two = modulate(middle, rows_mod[4], rows_mod[3]).astype(jnp.bfloat16).reshape(-1, D)
    inner_sum = plain_dot(hidden_two, w_one) + bias_one
    active = jax.nn.gelu(inner_sum, approximate=True).astype(jnp.bfloat16)
    branch_two = (plain_dot(active, w_two) + bias_two).reshape(leading + (D,))
    result = middle + rows_mod[5] * branch_two
    stored = (
        tokens,
        modulation,
        hidden,
        queries,
        key_heads,
        values,
        log_total,
        attended,
        branch_one,
        middle,
        hidden_two,
        inner_sum,
        active,
        branch_two,
    )
    return (result, stored)


def layer_backward(grad_out, stored, weight_set, temporal):
    w_qkv, w_out, w_one, w_two = (weight_set[0], weight_set[1], weight_set[2], weight_set[3])
    (
        tokens,
        modulation,
        hidden,
        queries,
        key_heads,
        values,
        log_total,
        attended,
        branch_one,
        middle,
        hidden_two,
        inner_sum,
        active,
        branch_two,
    ) = stored
    rows_mod = mod_rows(modulation)
    leading = tokens.shape[:-1]
    clips_here = tokens.shape[0]
    d_gate_two = jnp.sum(grad_out * branch_two, axis=(1, 2))
    d_branch_two = (rows_mod[5] * grad_out).astype(jnp.bfloat16).reshape(-1, D)
    d_bias_two = jnp.sum(d_branch_two, axis=0, dtype=jnp.float32)
    d_active = right_dot(d_branch_two, w_two)
    unused_gelu, gelu_back = jax.vjp(
        lambda entries: jax.nn.gelu(entries, approximate=True), inner_sum
    )
    d_inner = gelu_back(d_active)[0].astype(jnp.bfloat16)
    d_bias_one = jnp.sum(d_inner, axis=0, dtype=jnp.float32)
    d_hidden_two = right_dot(d_inner, w_one).reshape(leading + (D,))
    unused_norm, norm_back = jax.vjp(modulate, middle, rows_mod[4], rows_mod[3])
    d_middle, d_scale_two, d_shift_two = norm_back(d_hidden_two)
    grad_mid = grad_out + d_middle
    d_gate_one = jnp.sum(grad_mid * branch_one, axis=(1, 2))
    d_branch_one = (rows_mod[2] * grad_mid).astype(jnp.bfloat16).reshape(-1, D)
    d_bias_o = jnp.sum(d_branch_one, axis=0, dtype=jnp.float32)
    d_attended = (
        right_dot(d_branch_one, w_out).astype(jnp.bfloat16).reshape(leading + (HEADS, HEAD_DIM))
    )
    score_form, mix_form, back_form = einsum_forms(temporal)
    scale_qk = HEAD_DIM ** (-0.5)
    scores = contract(score_form, queries, key_heads) * scale_qk
    weights_soft = jnp.exp(scores - log_total)
    d_values = contract(back_form, weights_soft.astype(jnp.bfloat16), d_attended)
    d_probs = contract(score_form, d_attended, values)
    d_scores = weights_soft * (d_probs - jnp.sum(weights_soft * d_probs, axis=-1, keepdims=True))
    d_scores = d_scores.astype(jnp.bfloat16)
    d_queries = contract(mix_form, d_scores, key_heads) * scale_qk
    d_keys = contract(back_form, d_scores, queries) * scale_qk
    d_packed = jnp.concatenate(
        [
            d_queries.reshape(-1, D).astype(jnp.bfloat16),
            d_keys.reshape(-1, D).astype(jnp.bfloat16),
            d_values.reshape(-1, D).astype(jnp.bfloat16),
        ],
        axis=1,
    )
    d_bias_q = jnp.sum(d_packed[:, :D], axis=0, dtype=jnp.float32)
    d_bias_v = jnp.sum(d_packed[:, 2 * D :], axis=0, dtype=jnp.float32)
    d_hidden = right_dot(d_packed, w_qkv).reshape(leading + (D,))
    unused_first, first_back = jax.vjp(modulate, tokens, rows_mod[1], rows_mod[0])
    d_input, d_scale_one, d_shift_one = first_back(d_hidden)
    d_input = grad_mid + d_input
    d_modulation = jnp.stack(
        [
            d_shift_one.reshape(clips_here, D),
            d_scale_one.reshape(clips_here, D),
            d_gate_one,
            d_shift_two.reshape(clips_here, D),
            d_scale_two.reshape(clips_here, D),
            d_gate_two,
        ],
        axis=1,
    )
    d_vector = jnp.concatenate(
        [
            d_bias_q,
            d_bias_v,
            d_bias_o,
            d_bias_one,
            d_bias_two,
            jnp.sum(d_modulation, axis=0).reshape(-1),
        ]
    )
    factors = (
        hidden,
        d_packed,
        attended,
        d_branch_one,
        hidden_two,
        d_inner,
        active,
        d_branch_two,
        d_vector,
    )
    return (d_input, factors, d_modulation)


SHIFTS = (1, 2, 3)
SMALL_BYTES, LARGE_BYTES = 14 * 2**20, 24 * 2**20
STRIP = 384


def swap(x, axis):
    return lax.ppermute(x, axis, [(0, 1), (1, 0)])


def shift_z(x, k):
    n = lax.axis_size("z")
    return lax.ppermute(x, "z", [(i, (i + k) % n) for i in range(n)])


def gather_four(x, axis):
    far = swap(x, axis)
    return [x, swap(x, "core"), far, swap(far, "core")]


def scatter_four(partial, axis):
    kept_own, kept_far, sent = partial
    got = swap(sent, "core")
    far = (kept_far + got[1].astype(jnp.float32)).astype(jnp.bfloat16)
    return kept_own, got, swap(far, axis)


def source_of(number, side):
    z, here = lax.axis_index("z"), lax.axis_index(side)
    return 2 * ((z - number % 4 + 4) % 4) + (here + number // 4) % 2


def target_of(number, side):
    z, here = lax.axis_index("z"), lax.axis_index(side)
    return 2 * ((z + number % 4) % 4) + (here + number // 4) % 2


def padded(count, unit):
    return -(-count // unit) * unit


def whole():
    return pl.BlockSpec(memory_space=pltpu.VMEM)


def anywhere():
    return pl.BlockSpec(memory_space=pltpu.HBM)


def run(kernel, ins, outs, specs=None, scratch=(), flops=0):
    moved = sum(x.size * x.dtype.itemsize for x in list(ins) + list(outs))
    return pl.pallas_call(
        kernel,
        out_shape=tuple(outs),
        in_specs=specs or [whole()] * len(ins),
        out_specs=tuple([whole()] * len(outs)),
        scratch_shapes=list(scratch),
        compiler_params=pltpu.CompilerParams(vmem_limit_bytes=LARGE_BYTES if scratch else SMALL_BYTES),
        cost_estimate=pl.CostEstimate(flops=flops, bytes_accessed=moved, transcendentals=0),
    )(*ins)


def f32(*shape):
    return jax.ShapeDtypeStruct(shape, jnp.float32)


def bf16(*shape):
    return jax.ShapeDtypeStruct(shape, jnp.bfloat16)


def normal_parts(x):
    average = jnp.mean(x, axis=-1, keepdims=True)
    centred = x - average
    variance = jnp.mean(centred * centred, axis=-1, keepdims=True)
    inverse = lax.rsqrt(variance + EPSILON)
    return centred * inverse, inverse


def modulated(x, modulation, scale_row, order):
    normal, _ = normal_parts(x)
    scale = modulation[scale_row : scale_row + 1]
    shift = modulation[scale_row - 1 : scale_row]
    hidden = (normal * (1.0 + scale) + shift).astype(jnp.bfloat16)
    return plain_dot(hidden, order).astype(jnp.bfloat16)


def enter_kernel(x_ref, modulation_ref, order_ref, hidden_ref):
    x = x_ref[...].astype(jnp.float32)
    hidden_ref[...] = modulated(x, modulation_ref[...], 1, order_ref[...])


def summed(own_ref, got_ref, far_ref):
    return own_ref[...] + got_ref[0].astype(jnp.float32) + far_ref[...].astype(jnp.float32)


def middle_kernel(
    own_ref, got_ref, far_ref, bias_ref, x_ref, modulation_ref, order_ref, branch_ref, middle_ref, hidden_ref
):
    branch = summed(own_ref, got_ref, far_ref) + bias_ref[...]
    modulation = modulation_ref[...]
    middle = x_ref[...].astype(jnp.float32) + modulation[2:3] * branch
    branch_ref[...] = branch
    middle_ref[...] = middle
    hidden_ref[...] = modulated(middle, modulation, 4, order_ref[...])


def leave_kernel(own_ref, got_ref, far_ref, bias_ref, middle_ref, modulation_ref, branch_ref, result_ref):
    branch = summed(own_ref, got_ref, far_ref) + bias_ref[...]
    branch_ref[...] = branch
    result_ref[...] = (middle_ref[...] + modulation_ref[5:6] * branch).astype(jnp.bfloat16)


def start_rows(pieces, buffer, sems, first):
    copies = []
    for number, piece in enumerate(pieces):
        rows = piece.shape[0]
        copies.append(
            pltpu.make_async_copy(piece, buffer.at[pl.ds(number * rows, rows)], sems.at[first + number])
        )
        copies[-1].start()
    return copies


def start_weights(pieces, side, at, rows, buffer, sems, first):
    if len(pieces) == 1:
        found = [(pieces[0].at[number], number) for number in range(8)]
    else:
        found = [(piece, source_of(number, side)) for number, piece in enumerate(pieces)]
    copies = []
    for number, (piece, source) in enumerate(found):
        target = pl.multiple_of(source * rows, 16)
        copies.append(
            pltpu.make_async_copy(
                piece.at[pl.ds(at, rows)], buffer.at[pl.ds(target, rows)], sems.at[first + number]
            )
        )
        copies[-1].start()
    return copies


def wait_all(copies):
    for copy in copies:
        copy.wait()


def strips(size):
    return [(at, min(STRIP, size - at)) for at in range(0, size, STRIP)]


def deal(product, at, width, own_ref, far_ref, sent_ref):
    count = own_ref.shape[0]
    columns = slice(at, at + width)
    own_ref[:, columns] = product[:count]
    sent_ref[0, :, columns] = product[count : 2 * count].astype(jnp.bfloat16)
    far_ref[:, columns] = product[2 * count : 3 * count]
    sent_ref[1, :, columns] = product[3 * count :].astype(jnp.bfloat16)


def softmax_of(scores, count, period):
    if period:
        row = lax.broadcasted_iota(jnp.int32, scores.shape, 0) % period
        column = lax.broadcasted_iota(jnp.int32, scores.shape, 1) % period
        scores = jnp.where(row == column, scores, -1e30)
    exponent = jnp.exp(scores - jnp.max(scores, axis=-1, keepdims=True))
    return exponent * (1.0 / jnp.sum(exponent, axis=-1, keepdims=True))


def owners(width, per_head):
    return lax.broadcasted_iota(jnp.int32, (1, width), 1) // per_head


def by_head(x, owner, heads):
    return jnp.concatenate([jnp.where(owner == head, x, 0) for head in range(heads)], axis=0)


def of_head(stacked, owner, heads, count):
    chosen = stacked[:count]
    for head in range(1, heads):
        chosen = jnp.where(owner == head, stacked[head * count : (head + 1) * count], chosen)
    return chosen


def attention_kernel(period, heads, split, n_pieces, *refs):
    hidden, pieces, refs = refs[:4], refs[4 : 4 + n_pieces], refs[4 + n_pieces :]
    bias_ref, packed_ref, mixed_ref, probs_ref, own_ref, far_ref, sent_ref, left, qkv, out, sems = refs
    copies = start_rows(hidden, left, sems, 0)
    copies += start_weights(pieces, "x", 0, split, qkv, sems, 4)
    later = start_weights(pieces, "x", split, out.shape[0] // 8, out, sems, 12)
    wide = out.shape[0]
    narrow = (qkv.shape[1] - wide) // 2
    count = own_ref.shape[0]
    narrow_owner, wide_owner = owners(narrow, HEAD_DIM), owners(wide, wide // heads)
    wait_all(copies)
    for at, size in strips(qkv.shape[1]):
        product = plain_dot(left[...], qkv[:, at : at + size]) + bias_ref[:, at : at + size]
        packed_ref[:, at : at + size] = product.astype(jnp.bfloat16)
    for number in range(4):
        rows = pl.ds(number * count, count)
        packed = packed_ref[rows, :]
        values = packed[:, :wide]
        queries = by_head(packed[:, wide : wide + narrow], narrow_owner, heads)
        scores = right_dot(queries, packed[:, wide + narrow :]) * HEAD_DIM ** (-0.5)
        weights_soft = softmax_of(scores, count, period)
        probs_ref[pl.ds(number * heads * count, heads * count), :] = weights_soft
        mixed = plain_dot(weights_soft.astype(jnp.bfloat16), values)
        mixed_ref[rows, :] = of_head(mixed, wide_owner, heads, count).astype(jnp.bfloat16)
    wait_all(later)
    for at, size in strips(out.shape[1]):
        deal(plain_dot(mixed_ref[...], out[:, at : at + size]), at, size, own_ref, far_ref, sent_ref)


def attention_back_kernel(heads, split, n_pieces, *refs):
    d_branch, pieces, refs = refs[:4], refs[4 : 4 + n_pieces], refs[4 + n_pieces :]
    packed_ref, probs_ref, d_packed_ref, sums_ref, own_ref, far_ref, sent_ref, left, qkv, out, sems = refs
    copies = start_rows(d_branch, left, sems, 0)
    copies += start_weights(pieces, "x", split, out.shape[0] // 8, out, sems, 4)
    later = start_weights(pieces, "x", 0, split, qkv, sems, 12)
    wide = out.shape[0]
    narrow = (qkv.shape[1] - wide) // 2
    count = own_ref.shape[0]
    scale = HEAD_DIM ** (-0.5)
    narrow_owner, wide_owner = owners(narrow, HEAD_DIM), owners(wide, wide // heads)
    sums = jnp.zeros((1, wide + 2 * narrow), jnp.float32)
    wait_all(copies)
    d_mixed_all = right_dot(left[...], out[...]).astype(jnp.bfloat16)
    for number in range(4):
        rows = pl.ds(number * count, count)
        d_mixed = by_head(d_mixed_all[number * count : (number + 1) * count], wide_owner, heads)
        packed = packed_ref[rows, :]
        queries = by_head(packed[:, wide : wide + narrow], narrow_owner, heads)
        weights_soft = probs_ref[pl.ds(number * heads * count, heads * count), :]
        d_probs = right_dot(d_mixed, packed[:, :wide])
        inner = jnp.sum(weights_soft * d_probs, axis=-1, keepdims=True)
        d_scores = (weights_soft * (d_probs - inner)).astype(jnp.bfloat16)
        d_values = left_dot(weights_soft.astype(jnp.bfloat16), d_mixed)
        d_keys = left_dot(d_scores, queries)
        d_queries = of_head(
            plain_dot(d_scores, packed[:, wide + narrow :]), narrow_owner, heads, count
        )
        d_packed = jnp.concatenate([d_values, d_queries * scale, d_keys * scale], axis=1)
        d_packed = d_packed.astype(jnp.bfloat16)
        d_packed_ref[rows, :] = d_packed
        sums = sums + jnp.sum(d_packed.astype(jnp.float32), axis=0, keepdims=True)
    sums_ref[...] = sums
    wait_all(later)
    for at, size in strips(qkv.shape[0]):
        product = right_dot(d_packed_ref[...], qkv[at : at + size, :])
        deal(product, at, size, own_ref, far_ref, sent_ref)


def gelu_pair(u):
    inner = 0.7978845608028654 * (u + 0.044715 * u * u * u)
    bent = jnp.tanh(inner)
    value = 0.5 * u * (1.0 + bent)
    slope = 0.5 * (1.0 + bent) + 0.5 * u * (1.0 - bent * bent) * (
        0.7978845608028654 * (1.0 + 3 * 0.044715 * u * u)
    )
    return value, slope


def mlp_kernel(split, at_two, n_one, n_two, *refs):
    refs = list(refs)
    hidden, refs = refs[:4], refs[4:]
    pieces, refs = refs[:n_one], refs[n_one:]
    pieces_two, refs = refs[:n_two], refs[n_two:]
    bias_ref, active_ref, slope_ref, own_ref, far_ref, sent_ref, left, one, two, sems = refs
    copies = start_rows(hidden, left, sems, 0)
    copies += start_weights(pieces, "y", 0, split, one, sems, 4)
    later = start_weights(pieces_two, "y", at_two, two.shape[0] // 8, two, sems, 12)
    wait_all(copies)
    for at, size in strips(one.shape[1]):
        columns = slice(at, at + size)
        u = plain_dot(left[...], one[:, columns]) + bias_ref[:, columns]
        value, slope = gelu_pair(u)
        active_ref[:, columns] = value.astype(jnp.bfloat16)
        slope_ref[:, columns] = slope.astype(jnp.bfloat16)
    wait_all(later)
    for at, size in strips(two.shape[1]):
        deal(plain_dot(active_ref[...], two[:, at : at + size]), at, size, own_ref, far_ref, sent_ref)


def mlp_back_kernel(split, at_two, n_one, n_two, *refs):
    refs = list(refs)
    d_branch, refs = refs[:4], refs[4:]
    pieces, refs = refs[:n_one], refs[n_one:]
    pieces_two, refs = refs[:n_two], refs[n_two:]
    slope_ref, d_inner_ref, sums_ref, own_ref, far_ref, sent_ref, left, one, two, sems = refs
    copies = start_rows(d_branch, left, sems, 0)
    copies += start_weights(pieces_two, "y", at_two, two.shape[0] // 8, two, sems, 4)
    later = start_weights(pieces, "y", 0, split, one, sems, 12)
    wait_all(copies)
    for at, size in strips(two.shape[0]):
        columns = slice(at, at + size)
        d_active = right_dot(left[...], two[columns, :])
        d_inner = (d_active * slope_ref[:, columns].astype(jnp.float32)).astype(jnp.bfloat16)
        d_inner_ref[:, columns] = d_inner
        sums_ref[:, columns] = jnp.sum(d_inner.astype(jnp.float32), axis=0, keepdims=True)
    wait_all(later)
    for at, size in strips(one.shape[0]):
        product = right_dot(d_inner_ref[...], one[at : at + size, :])
        deal(product, at, size, own_ref, far_ref, sent_ref)


def total_sums(ref, *members):
    rows = [jnp.sum(m.astype(jnp.float32), axis=0, keepdims=True) for m in members]
    ref[...] = jnp.concatenate(rows, axis=0)


def open_back_kernel(grad_ref, branch_ref, modulation_ref, d_branch_ref, sums_ref):
    grad = grad_ref[...].astype(jnp.float32)
    d_branch = (modulation_ref[5:6] * grad).astype(jnp.bfloat16)
    d_branch_ref[...] = d_branch
    total_sums(sums_ref, grad * branch_ref[...], d_branch)


def natural(total, order):
    high = total.astype(jnp.bfloat16)
    low = (total - high.astype(jnp.float32)).astype(jnp.bfloat16)
    both = right_dot(jnp.concatenate([high, low], axis=0), order)
    return both[: total.shape[0]] + both[total.shape[0] :]


def norm_back(d_hidden, x, scale):
    normal, inverse = normal_parts(x)
    entry = d_hidden * (1.0 + scale)
    average = jnp.mean(entry, axis=-1, keepdims=True)
    along = jnp.mean(entry * normal, axis=-1, keepdims=True)
    return (entry - average - normal * along) * inverse, d_hidden * normal


def middle_back_kernel(
    own_ref, got_ref, far_ref, grad_ref, x_ref, branch_ref, modulation_ref, order_ref, d_branch_ref, grad_mid_ref, sums_ref
):
    d_hidden = natural(summed(own_ref, got_ref, far_ref), order_ref[...])
    modulation = modulation_ref[...]
    d_x, d_scale = norm_back(d_hidden, x_ref[...], modulation[4:5])
    grad_mid = grad_ref[...].astype(jnp.float32) + d_x
    grad_mid_ref[...] = grad_mid
    d_branch = (modulation[2:3] * grad_mid).astype(jnp.bfloat16)
    d_branch_ref[...] = d_branch
    total_sums(sums_ref, d_hidden, d_scale, grad_mid * branch_ref[...], d_branch)


def close_back_kernel(own_ref, got_ref, far_ref, grad_ref, x_ref, modulation_ref, order_ref, d_x_ref, sums_ref):
    d_hidden = natural(summed(own_ref, got_ref, far_ref), order_ref[...])
    d_x, d_scale = norm_back(d_hidden, x_ref[...].astype(jnp.float32), modulation_ref[1:2])
    d_x_ref[...] = (grad_ref[...] + d_x).astype(d_x_ref.dtype)
    total_sums(sums_ref, d_hidden, d_scale)


def factor(groups):
    pairs = [pair for members, _ in groups for pair in members]
    ins, scratch, flops = [], [], 0
    for left, right, height in pairs:
        ins += left + right
        count = sum(piece.shape[0] for piece in left)
        scratch.append(pltpu.VMEM((left[0].shape[1], count), jnp.bfloat16))
        if len(right) > 1:
            scratch.append(pltpu.VMEM((count, right[0].shape[1]), jnp.bfloat16))
        flops += 2 * count * left[0].shape[1] * right[0].shape[1]
    outs = []
    for members, side in groups:
        height, width = sum(m[2] for m in members), members[0][1][0].shape[1]
        outs += [bf16(height, width) for _ in range(8)] if side else [bf16(8 * height, width)]

    def kernel(*refs):
        refs = iter(refs)
        taken = [
            ([next(refs) for _ in left], [next(refs) for _ in right], height)
            for left, right, height in pairs
        ]
        results = [next(refs) for _ in outs]
        ready = []
        for left, right, height in taken:
            flip = next(refs)
            at = 0
            for piece in left:
                flip[:, at : at + piece.shape[0]] = piece[...].T
                at += piece.shape[0]
            lay = right[0]
            if len(right) > 1:
                lay = next(refs)
                at = 0
                for piece in right:
                    lay[at : at + piece.shape[0], :] = piece[...]
                    at += piece.shape[0]
            ready.append((flip, lay, height))
        for members, side in groups:
            mine, ready = ready[: len(members)], ready[len(members) :]
            total = sum(member[2] for member in mine)
            for number in range(8):
                at = 0 if side else number * total
                result = results[number] if side else results[0]
                target = target_of(number, side) if side else number
                for flip, lay, height in mine:
                    rows = pl.ds(pl.multiple_of(target * height, 16), height)
                    product = plain_dot(flip[rows, :], lay[...])
                    result[at : at + height, :] = product.astype(jnp.bfloat16)
                    at += height
            results = results[8:] if side else results[1:]

    results = list(run(kernel, ins, outs, scratch=scratch, flops=flops))
    given = []
    for _, side in groups:
        if side:
            given.append((results[:4], results[4:8]))
        else:
            given.append(results[0])
        results = results[8:] if side else results[1:]
    return given


def placed_blocks(half, n_seq):
    for owner in range(4 * n_seq):
        y, core, z, x = owner // (2 * n_seq), (owner // n_seq) % 2, (owner % n_seq) // 2, owner % 2
        yield owner * half, 2 * x + core, (2 * z + y) * half


def part_kernel(half, n_seq, rows_ref, parts_ref):
    rows = rows_ref.shape[1]
    for layer in range(2):
        for at, part, place in placed_blocks(half, n_seq):
            parts_ref[part, layer, 0:rows, place : place + half] = rows_ref[layer, :, at : at + half]
        for part in range(4):
            parts_ref[part, layer, rows:, :] = jnp.zeros(
                (parts_ref.shape[2] - rows, parts_ref.shape[3]), parts_ref.dtype
            )


def join_kernel(half, n_seq, room, parts_ref, rows_ref):
    rows = rows_ref.shape[1]
    for layer in range(2):
        for at, part, place in placed_blocks(half, n_seq):
            block = parts_ref[part, layer * room : layer * room + rows, place : place + half]
            rows_ref[layer, :, at : at + half] = block.astype(jnp.float32)


def vector_kernel(
    n_seq, rows, sums_one_ref, sums_mid_ref, sums_two_ref, qkv_ref, one_ref, vector_ref, modulation_ref
):
    y, core, x = lax.axis_index("y"), lax.axis_index("core"), lax.axis_index("x")
    here = 2 * y + core
    room = padded(rows, 16)
    wide, width, half = n_seq * room, n_seq * rows, one_ref.shape[1] // n_seq
    for number in range(4):
        mine = here == number
        query = qkv_ref[:, wide : wide + width]
        vector_ref[:, number * width : (number + 1) * width] = jnp.where(mine, query, 0.0)
        for block in range(n_seq):
            at = D + number * width + block * rows
            value = qkv_ref[:, block * room : block * room + rows]
            vector_ref[:, at : at + rows] = jnp.where(mine, value, 0.0)
    for owner in range(4 * n_seq):
        mine = ((owner // n_seq) % 2 == core) & (owner % 2 == x)
        block = 2 * ((owner % n_seq) // 2) + owner // (2 * n_seq)
        at = 3 * D + owner * half
        vector_ref[:, at : at + half] = jnp.where(mine, one_ref[:, block * half : (block + 1) * half], 0.0)
    vector_ref[:, 2 * D : 3 * D] = sums_mid_ref[3:4]
    vector_ref[:, 3 * D + FF : 4 * D + FF] = sums_two_ref[1:2]
    members = (
        (sums_one_ref, 0),
        (sums_one_ref, 1),
        (sums_mid_ref, 2),
        (sums_mid_ref, 0),
        (sums_mid_ref, 1),
        (sums_two_ref, 0),
    )
    for number, (ref, row) in enumerate(members):
        at = (4 + number) * D + FF
        vector_ref[:, at : at + D] = ref[row : row + 1]
        modulation_ref[number : number + 1, :] = ref[row : row + 1]


def order_matrix(n_dp, n_seq, rows, room, crossed):
    place = lax.broadcasted_iota(jnp.int32, (D, n_dp * n_seq * room), 1)
    feature = lax.broadcasted_iota(jnp.int32, (D, n_dp * n_seq * room), 0)
    block, inner = place // room, place % room
    outer, local = block // n_dp, block % n_dp
    z, side, across, core = outer // 2, outer % 2, local // 2, local % 2
    x, y = (across, side) if crossed else (side, across)
    owner = (2 * y + core) * n_seq + 2 * z + x
    return ((feature == owner * rows + inner) & (inner < rows)).astype(jnp.bfloat16)


def grow(x, axis, size):
    pads = [(0, 0)] * x.ndim
    pads[axis] = (0, size - x.shape[axis])
    return jnp.pad(x, pads)


def exchange(parts, axis):
    return lax.all_to_all(parts, (axis, "core"), split_axis=0, concat_axis=0, tiled=True)


def spread(values, n_seq, rows, room):
    lead = values.shape[:-1]
    return grow(values.reshape(lead + (n_seq, rows)), len(lead) + 1, room).reshape(lead + (-1,))


def ordered_vectors(everyone, n_dp, n_seq, count):
    chosen = owner_rows(n_dp, n_seq, -1)
    ordered = left_dot(chosen.astype(jnp.bfloat16), everyone)
    return ordered.reshape(n_dp * n_seq, 2, count).transpose(1, 0, 2).reshape(2, -1)


def owner_rows(n_dp, n_seq, sign):
    count = n_dp * n_seq
    relative = lax.broadcasted_iota(jnp.int32, (count, count), 0)
    owner = lax.broadcasted_iota(jnp.int32, (count, count), 1)
    n_z = n_seq // 2
    z = (lax.axis_index("z") + sign * (relative // (2 * n_dp)) + n_z) % n_z
    x = lax.axis_index("x") ^ ((relative // n_dp) % 2)
    y = lax.axis_index("y") ^ ((relative // 2) % 2)
    core = lax.axis_index("core") ^ (relative % 2)
    source = (2 * y + core) * n_seq + 2 * z + x
    return (owner == source).astype(jnp.float32)


def scatter_vectors(sums, n_dp, n_seq, finish):
    count = sums.shape[1] // (n_dp * n_seq)
    rows = sums.reshape(2, n_dp * n_seq, count).transpose(1, 0, 2).reshape(n_dp * n_seq, -1)
    chosen = owner_rows(n_dp, n_seq, 1)
    rows = jnp.dot(chosen, rows, precision=lax.Precision.HIGHEST)
    quarters = jnp.split(rows, n_seq // 2)
    got = yield (quarters[0], [shift_z(quarters[k], k) for k in SHIFTS])
    total = got[0] + sum(got[1])
    got = yield (total, swap(total[n_dp:], "x"))
    total = got[0][:n_dp] + got[1]
    got = yield (total, swap(total[2:], "y"))
    total = got[0][:2] + got[1]
    got = yield (total, swap(total[1:], "core"))
    finish((got[0][:1] + got[1]).reshape(2, count))
    yield None


def sum_seq(x, finish):
    got = yield (x, swap(x, "x"))
    total = got[0] + got[1]
    got = yield (total, [shift_z(total, k) for k in SHIFTS])
    finish(got[0] + sum(got[1]))
    yield None


def slice_of(vector, n_dp):
    width = vector.shape[0] // n_dp
    here = 2 * lax.axis_index("y") + lax.axis_index("core")
    return lax.dynamic_slice(vector, (here * width,), (width,))


def crossed_slice(vector, n_z):
    blocks = vector.reshape(2, 2, n_z, 2, -1)
    blocks = lax.dynamic_index_in_dim(blocks, lax.axis_index("x"), 3, keepdims=False)
    blocks = lax.dynamic_index_in_dim(blocks, lax.axis_index("core"), 1, keepdims=False)
    return blocks.transpose(1, 0, 2).reshape(-1)


class Gather:
    def __init__(self, pieces, side, wait):
        self.side, self.wait = side, wait
        self.column, self.across, self.sent, self.waiting = [pieces], [], 0, False

    def wants_x(self):
        return self.sent < len(self.column)

    def send_x(self):
        self.sent += 1
        return [swap(piece, self.side) for piece in self.column[self.sent - 1]]

    def got_x(self, pieces):
        self.across.append(pieces)

    def wants_z(self):
        return len(self.column) < 4 and not self.waiting

    def send_z(self):
        self.waiting = True
        return [shift_z(piece, 1) for piece in self.column[-1]]

    def got_z(self, pieces):
        self.waiting = False
        self.column.append(pieces)

    def finished(self):
        return len(self.across) == 4

    def pieces(self, index):
        return [piece[index] for piece in self.column + self.across]


class Reduce:
    def __init__(self, mine, other, side, wait, finish):
        self.side, self.wait = side, wait
        self.mine, self.other, self.finish = mine, other, finish
        self.sent, self.got, self.hops, self.carried, self.result = 3, {}, 3, None, None

    def wants_x(self):
        return self.sent >= 0

    def send_x(self):
        self.sent -= 1
        return [swap(piece, self.side) for piece in self.other[self.sent + 1]]

    def got_x(self, pieces):
        self.got[3 - len(self.got)] = pieces

    def added(self, k):
        total = [m.astype(jnp.float32) + g.astype(jnp.float32) for m, g in zip(self.mine[k], self.got[k])]
        if k < 3:
            total = [t + c.astype(jnp.float32) for t, c in zip(total, self.carried)]
        return total

    def wants_z(self):
        ready = self.hops == 3 or self.carried is not None
        return self.hops > 0 and self.hops in self.got and ready

    def send_z(self):
        total = self.added(self.hops)
        self.hops -= 1
        self.carried = None
        return [shift_z(t.astype(jnp.bfloat16), 1) for t in total]

    def got_z(self, pieces):
        self.carried = pieces

    def finished(self):
        return self.hops == 0 and self.carried is not None and 0 in self.got


class Lane:
    def __init__(self):
        self.jobs, self.flight, self.extra, self.scripts = [], [], [], []

    def issue(self):
        for job in [job for job in self.jobs if isinstance(job, Reduce)]:
            if job.wants_x():
                self.flight.append((job.wait, job, "x", job.send_x()))
            if job.wants_z():
                self.flight.append((1, job, "z", job.send_z()))
        for job in [job for job in self.jobs if isinstance(job, Gather)]:
            for kind, link in (("x", job.side), ("z", "z")):
                if getattr(job, "wants_" + kind)():
                    self.flight.append((job.wait, job, kind, getattr(job, "send_" + kind)()))
        for script in self.scripts:
            script[1] = script[0].send(script[1])
        self.scripts = [script for script in self.scripts if script[1] is not None]

    def add(self, mine, other, side, wait, finish):
        job = Reduce([[m] for m in mine], [[m] for m in other], side, wait, finish)
        self.jobs.append(job)
        self.flight.append((wait, job, "x", job.send_x()))

    def close(self):
        for job in [job for job in self.jobs if job.finished()]:
            self.jobs.remove(job)
            if isinstance(job, Reduce):
                job.finish(job.added(0))

    def tick(self, values):
        due = [f for f in self.flight if f[0] == 1]
        values, arrived, _, steps = lax.optimization_barrier(
            (values, [f[3] for f in due], self.extra, [script[1] for script in self.scripts])
        )
        for script, step in zip(self.scripts, steps):
            script[1] = step
        self.flight = [(f[0] - 1,) + f[1:] for f in self.flight if f[0] > 1]
        self.extra = []
        for (_, job, kind, _), pieces in zip(due, arrived):
            getattr(job, "got_" + kind)(pieces)
        self.close()
        self.issue()
        return values

    def until(self, job, values):
        while not job.finished():
            values = self.tick(values)
        return values


def on_device_split(tokens, cond, d_out, attn_in, attn_out, mlp_in, mlp_out, vectors):
    n_dp, n_seq = 4, 2 * lax.axis_size("z")
    heads = HEADS // n_dp
    width = heads * HEAD_DIM
    frames, places = tokens.shape[1] * n_seq, tokens.shape[2]
    periods = (0, places // n_seq)
    count = tokens.shape[1] * places
    group = n_dp * count
    rows = D // (n_dp * n_seq)
    room = padded(rows, 8)
    out_room = padded(rows, 16)
    deep, wide = n_dp * n_seq * room, n_seq * out_room
    narrow = padded(width, 128)
    packed_width = wide + 2 * narrow
    inner = FF // n_dp
    split = n_dp * room
    half = inner // n_seq
    order = order_matrix(n_dp, n_seq, rows, room, False)
    order_mlp = order_matrix(n_dp, n_seq, rows, room, True)

    parts = attn_in.reshape(2, rows, 3, n_dp, width).transpose(2, 3, 0, 1, 4)
    qkv_parts = jnp.concatenate(
        [spread(parts[2], n_seq, rows, out_room), grow(parts[0], 3, narrow), grow(parts[1], 3, narrow)],
        axis=3,
    )
    qkv_parts = exchange(grow(qkv_parts, 2, room).reshape(n_dp, 2 * room, -1), "y")
    qkv_parts = qkv_parts.reshape(n_dp, 2, room, -1)
    out_parts = grow(attn_out.reshape(2, rows, D), 1, out_room)
    two_parts = mlp_out.reshape(2, half, D)

    def attention_piece(index):
        return jnp.concatenate([qkv_parts[:, index].reshape(split, -1), out_parts[index]])

    def regroup(x):
        x = x.reshape(n_seq, count // n_seq, D)
        return lax.all_to_all(x, ("z", "x"), split_axis=0, concat_axis=0, tiled=True).reshape(-1, D)

    lane = Lane()
    mine = vectors.reshape(1, -1)
    near = jnp.concatenate([mine, swap(mine, "core")])
    clips = jnp.concatenate([near, swap(near, "y")])
    pair = jnp.concatenate([clips, swap(clips, "x")])
    everyone = jnp.concatenate([pair] + [shift_z(pair, k) for k in SHIFTS])
    first = attention_piece(0)
    mlp_in = mlp_in.reshape(2, rows, FF)
    everyone, first, mlp_in, qkv_parts, out_parts, two_parts = lax.optimization_barrier(
        (everyone, first, mlp_in, qkv_parts, out_parts, two_parts)
    )
    attention_job = Gather([first], "x", 1)
    lane.jobs.append(attention_job)
    lane.issue()
    (one_parts,) = run(
        functools.partial(part_kernel, half, n_seq), [mlp_in], [bf16(n_dp, 2, room, inner)]
    )
    vector = ordered_vectors(everyone, n_dp, n_seq, vectors.shape[1])
    biases, modulations = [], []
    for index in range(2):
        v = vector[index]
        bias_q, bias_v = slice_of(v[0:D], n_dp), slice_of(v[D : 2 * D], n_dp)
        bias_q = grow(bias_q, 0, narrow)
        bias_v = spread(bias_v, n_seq, rows, out_room)
        biases.append(
            (
                jnp.concatenate([bias_v, bias_q, jnp.zeros_like(bias_q)])[None],
                v[None, 2 * D : 3 * D],
                crossed_slice(v[3 * D : 3 * D + FF], n_seq // 2)[None],
                v[None, 3 * D + FF : 4 * D + FF],
            )
        )
        modulations.append(v[4 * D + FF :].reshape(6, D) + cond[0])

    def scratch(left_width, *shapes):
        return [
            pltpu.VMEM((group, left_width), jnp.bfloat16),
            *[pltpu.VMEM(shape, jnp.bfloat16) for shape in shapes],
            pltpu.SemaphoreType.DMA((20,)),
        ]

    attention_rooms = ((deep, packed_width), (wide, D))
    mlp_rooms = ((deep, inner), (inner, D))
    attention_flops = 4 * group * (deep * packed_width + wide * D)
    mlp_flops = 2 * group * (deep + D) * inner
    own_shapes = [f32(count, D), f32(count, D), bf16(2, count, D)]
    deep_shapes = [f32(count, deep), f32(count, deep), bf16(2, count, deep)]

    def opened(x, index):
        return run(enter_kernel, [x, modulations[index], order], [bf16(count, deep)])[0]

    def attention(index, hidden, pieces):
        return run(
            functools.partial(attention_kernel, periods[index], heads, split, len(pieces)),
            hidden + pieces + [biases[index][0]],
            [bf16(group, packed_width), bf16(group, wide), f32(group * heads, count)] + own_shapes,
            specs=[anywhere()] * (4 + len(pieces)) + [whole()],
            scratch=scratch(deep, *attention_rooms),
            flops=attention_flops,
        )

    def attention_back(index, d_branch, pieces, packed, probs):
        return run(
            functools.partial(attention_back_kernel, heads, split, len(pieces)),
            d_branch + pieces + [packed, probs],
            [bf16(group, packed_width), f32(1, packed_width)] + deep_shapes,
            specs=[anywhere()] * (4 + len(pieces)) + [whole()] * 2,
            scratch=scratch(D, *attention_rooms),
            flops=attention_flops,
        )

    def middle(index, own, x):
        return run(
            middle_kernel,
            list(own) + [biases[index][1], x, modulations[index], order_mlp],
            [f32(count, D), f32(count, D), bf16(count, deep)],
        )

    def mlp(index, hidden, pieces, pieces_two, at):
        return run(
            functools.partial(mlp_kernel, split, at, len(pieces), len(pieces_two)),
            hidden + pieces + pieces_two + [biases[index][2]],
            [bf16(group, inner), bf16(group, inner)] + own_shapes,
            specs=[anywhere()] * (4 + len(pieces) + len(pieces_two)) + [whole()],
            scratch=scratch(deep, *mlp_rooms),
            flops=mlp_flops,
        )

    def mlp_back(d_branch, pieces, pieces_two, at, slope):
        return run(
            functools.partial(mlp_back_kernel, split, at, len(pieces), len(pieces_two)),
            d_branch + pieces + pieces_two + [slope],
            [bf16(group, inner), f32(1, inner)] + deep_shapes,
            specs=[anywhere()] * (4 + len(pieces) + len(pieces_two)) + [whole()],
            scratch=scratch(D, *mlp_rooms),
            flops=mlp_flops,
        )

    def left(index, own, x):
        return run(
            leave_kernel,
            list(own) + [biases[index][3], x, modulations[index]],
            [f32(count, D), bf16(count, D)],
        )

    def opened_back(index, grad, branch):
        return run(
            open_back_kernel, [grad, branch, modulations[index]], [bf16(count, D), f32(2, D)]
        )

    def middle_back(index, own, grad, x, branch):
        return run(
            middle_back_kernel,
            list(own) + [grad, x, branch, modulations[index], order_mlp],
            [bf16(count, D), f32(count, D), f32(4, D)],
        )

    def closed_back(index, own, grad, x, out_type):
        return run(
            close_back_kernel,
            list(own) + [grad, x, modulations[index], order],
            [jax.ShapeDtypeStruct((count, D), out_type), f32(2, D)],
        )

    def vector_sums(sums_one, sums_mid, sums_two, d_bias_qkv, d_bias_one):
        return run(
            functools.partial(vector_kernel, n_seq, rows),
            [sums_one, sums_mid, sums_two, d_bias_qkv, d_bias_one],
            [f32(1, 10 * D + FF), f32(6, D)],
        )

    x_zero = tokens.reshape(-1, D)
    hidden, one_parts, two_parts = lane.tick((opened(x_zero, 0), one_parts, two_parts))
    one_parts = exchange(one_parts.reshape(n_dp, 2 * room, inner), "x").reshape(n_dp, 2, room, inner)
    hidden_zero, one_parts, two_parts, qkv_parts, out_parts = lane.tick(
        (gather_four(hidden, "y"), one_parts, two_parts, qkv_parts, out_parts)
    )
    two_zero = [lax.all_gather(two_parts[0], ("z", "y"))]
    piece = one_parts[:, 0].reshape(split, inner)
    later = jnp.concatenate([one_parts[:, 1].reshape(split, inner), two_parts[1]])
    hidden_zero, piece, later, second = lane.tick((hidden_zero, piece, later, attention_piece(1)))
    mlp_job = Gather([piece], "y", 1)
    lane.jobs.append(mlp_job)
    lane.issue()
    hidden_zero = lane.until(attention_job, hidden_zero)
    attention_zero = attention_job.pieces(0)
    packed_zero, mixed_zero, probs_zero, *partial = attention(0, hidden_zero, attention_zero)
    next_job = Gather([second], "x", 1)
    lane.jobs.append(next_job)
    partial = lane.tick(partial)
    own = lane.tick(scatter_four(partial, "y"))
    branch_zero, middle_zero, hidden = middle(0, own, x_zero)
    inside_zero, later = lane.until(mlp_job, lane.tick((gather_four(hidden, "x"), later)))
    mlp_one = [lax.all_gather(later, ("z", "y"))]
    mlp_zero = mlp_job.pieces(0)
    active_zero, slope_zero, *partial = mlp(0, inside_zero, mlp_zero, two_zero, 0)
    own = lane.tick(scatter_four(lane.tick(partial), "x"))
    end_zero, result = left(0, own, middle_zero)

    x_one = lane.tick(regroup(result))
    hidden_one = lane.until(next_job, lane.tick(gather_four(opened(x_one, 1), "y")))
    attention_one = next_job.pieces(0)
    packed_one, mixed_one, probs_one, *partial = attention(1, hidden_one, attention_one)
    partial, d_out = lax.optimization_barrier((partial, d_out))
    grad_places = regroup(d_out.reshape(-1, D))
    branch_one, middle_one, hidden = middle(1, scatter_four(partial, "y"), x_one)
    inside_one, grad_places = lax.optimization_barrier((gather_four(hidden, "x"), grad_places))
    active_one, slope_one, *partial = mlp(1, inside_one, mlp_one, mlp_one, split)
    end_one, result = left(1, scatter_four(partial, "x"), middle_one)
    output = regroup(result).astype(jnp.float32)

    d_end, sums_two = opened_back(1, grad_places, end_one)
    d_end = gather_four(d_end, "x")
    d_inner, d_bias_one, *partial = mlp_back(d_end, mlp_one, mlp_one, split, slope_one)
    partial, output = lax.optimization_barrier((partial, output))
    owned = {}

    def keep(name):
        return functools.partial(owned.__setitem__, name)

    (d_mlp,) = factor(
        [([(inside_one, [d_inner], split), ([active_one], d_end, half)], None)]
    )
    own, d_mlp = lax.optimization_barrier((scatter_four(partial, "x"), d_mlp))
    d_mlp_one = lax.psum_scatter(d_mlp, ("z", "y"), scatter_dimension=0, tiled=True)
    d_branch, grad_mid, sums_mid = middle_back(1, own, grad_places, middle_one, branch_one)
    d_branch_one = gather_four(d_branch, "y")
    d_packed, d_bias_qkv, *partial = attention_back(
        1, d_branch_one, attention_one, packed_one, probs_one
    )
    (ring,) = factor(
        [([(hidden_one, [d_packed], split), ([mixed_one], d_branch_one, out_room)], "x")]
    )
    own, ring = lax.optimization_barrier((scatter_four(partial, "y"), ring))
    grad, sums_one = closed_back(1, own, grad_mid, x_one, jnp.bfloat16)
    vector_one, modulation_one = vector_sums(sums_one, sums_mid, sums_two, d_bias_qkv, d_bias_one)

    def finish_mlp(totals):
        total = totals[0]
        ones = jnp.concatenate(
            [x[:split].astype(jnp.bfloat16).reshape(n_dp, room, -1) for x in (total, d_mlp_one)],
            axis=1,
        )
        (joined,) = run(
            functools.partial(join_kernel, half, n_seq, room),
            [exchange(ones, "x")],
            [f32(2, rows, FF)],
        )
        owned["one"] = joined.reshape(2, -1)
        owned["two"] = jnp.stack([total[split:], d_mlp_one[split:].astype(jnp.float32)]).reshape(2, -1)

    def finish_attention(totals):
        pair = (totals[0], owned["attention later"][0])
        both = jnp.concatenate(
            [x[:split].astype(jnp.bfloat16).reshape(n_dp, room, -1) for x in pair], axis=1
        )
        both = exchange(both, "y").reshape(n_dp, 2, room, packed_width)[:, :, :rows]
        values = both[..., :wide].reshape(n_dp, 2, rows, n_seq, out_room)[..., :rows]
        joined = jnp.stack(
            [
                both[..., wide : wide + width],
                both[..., wide + narrow : wide + narrow + width],
                values.reshape(n_dp, 2, rows, width),
            ]
        )
        owned["qkv"] = joined.transpose(2, 3, 0, 1, 4).astype(jnp.float32).reshape(2, -1)
        owned["out"] = jnp.stack(
            [x[split : split + rows].astype(jnp.float32) for x in pair]
        ).reshape(2, -1)

    grad_frames, ring = lax.optimization_barrier((regroup(grad), ring))
    lane.add(*ring, "x", 2, keep("attention later"))
    d_end, sums_two = opened_back(0, grad_frames, end_zero)
    d_end = lane.tick(gather_four(d_end, "x"))
    d_inner, d_bias_one, *partial = mlp_back(d_end, mlp_zero, two_zero, 0, slope_zero)
    partial = lane.tick(partial)
    (ring,) = factor(
        [([(inside_zero, [d_inner], split), ([active_zero], d_end, half)], "y")]
    )
    lane.add(*ring, "y", 1, finish_mlp)
    own = lane.tick(scatter_four(partial, "x"))
    d_branch, grad_mid, sums_mid = middle_back(0, own, grad_frames, middle_zero, branch_zero)
    d_branch = lane.tick(gather_four(d_branch, "y"))
    d_packed, d_bias_qkv, *partial = attention_back(
        0, d_branch, attention_zero, packed_zero, probs_zero
    )
    partial = lane.tick(partial)
    (ring,) = factor(
        [([(hidden_zero, [d_packed], split), ([mixed_zero], d_branch, out_room)], "x")]
    )
    lane.add(*ring, "x", 1, finish_attention)
    lane.extra.append((ring, d_mlp_one))
    own = scatter_four(partial, "y")
    lane.tick(())
    own = lane.tick(own)
    d_tokens, sums_one = closed_back(0, own, grad_mid, x_zero, jnp.float32)
    vector_zero, modulation_zero = vector_sums(sums_one, sums_mid, sums_two, d_bias_qkv, d_bias_one)

    lane.scripts += [
        [scatter_vectors(jnp.concatenate([vector_zero, vector_one]), n_dp, n_seq, keep("vectors")), None],
        [sum_seq(modulation_zero + modulation_one, keep("cond")), None],
    ]
    while lane.jobs or lane.scripts:
        lane.tick(())
    return (
        output.reshape(tokens.shape),
        d_tokens.reshape(tokens.shape),
        owned["cond"][None],
        *[owned[name] for name in ("qkv", "out", "one", "two")],
        owned["vectors"],
    )


def on_device(tokens, cond, d_out, attn_in, attn_out, mlp_in, mlp_out, vectors):
    shards = (attn_in, attn_out, mlp_in, mlp_out, vectors)
    widths = (
        attn_in.shape[1],
        attn_out.shape[1],
        mlp_in.shape[1],
        mlp_out.shape[1],
        vectors.shape[1],
    )
    layer_zero = unpack(fetch_forward(shards, 0))
    spatial_out, stored_zero = layer_forward(tokens.astype(jnp.float32), cond, layer_zero, False)
    by_place = lax.all_to_all(
        spatial_out.astype(jnp.bfloat16), "seq", split_axis=2, concat_axis=1, tiled=True
    ).astype(spatial_out.dtype)
    layer_one = unpack(fetch_forward(shards, 1))
    temporal_out, stored_one = layer_forward(by_place, cond, layer_one, True)
    output = lax.all_to_all(
        temporal_out.astype(jnp.bfloat16), "seq", split_axis=1, concat_axis=2, tiled=True
    ).astype(temporal_out.dtype)
    grad_places = lax.all_to_all(d_out, "seq", split_axis=2, concat_axis=1, tiled=True).astype(
        jnp.float32
    )
    grad_mid, factors_one, modul_one = layer_backward(grad_places, stored_one, layer_one, True)
    owned_one = reduce_grads(factors_one, widths)
    grad_frames = lax.all_to_all(
        grad_mid.astype(jnp.bfloat16), "seq", split_axis=1, concat_axis=2, tiled=True
    ).astype(grad_mid.dtype)
    d_tokens, factors_zero, modul_zero = layer_backward(grad_frames, stored_zero, layer_zero, False)
    owned_zero = reduce_grads(factors_zero, widths)
    d_cond = lax.psum(modul_zero + modul_one, "seq")
    stacked = tuple((jnp.stack([former, latter]) for former, latter in zip(owned_zero, owned_one)))
    return (output, d_tokens, d_cond, stacked[0], stacked[1], stacked[2], stacked[3], stacked[4])


def solution(mesh):
    n_dp, n_seq = mesh.shape["dp"], mesh.shape["seq"]
    split = n_dp == 4 and n_seq == 8
    clips, frames = "dp", "seq"
    if split:
        devices = mesh.devices.reshape(n_dp // 2, 2, n_seq // 2, 2)
        mesh = jax.sharding.Mesh(devices, ("y", "core", "z", "x"))
        clips, frames = ("y", "core"), ("z", "x")
    everyone = P(None, ("y", "core", "z", "x") if split else ("dp", "seq"))
    tokens, cond = P(clips, frames, None, None), P(clips, None, None)
    return jax.shard_map(
        on_device_split if split else on_device,
        mesh=mesh,
        in_specs=(tokens, cond, tokens) + (everyone,) * 5,
        out_specs=(tokens, tokens, cond) + (everyone,) * 5,
        check_vma=False,
    )
```

```python
import functools

import jax
import jax.numpy as jnp
from jax import lax
from jax.experimental import pallas as pl
from jax.experimental.pallas import tpu as pltpu
from jax.sharding import PartitionSpec as P

D = 1152
HEADS = 16
HEAD_DIM = 72
FF = 4608


EPSILON = 1e-06


def as_sent(x):

    def short(part):
        return part.astype(jnp.bfloat16) if part.dtype == jnp.float32 else part

    return jax.tree.map(short, x)


def modulate(tokens, scale, shift):
    average = jnp.mean(tokens, axis=-1, keepdims=True)
    centred = tokens - average
    variance = jnp.mean(centred * centred, axis=-1, keepdims=True)
    return centred * lax.rsqrt(variance + EPSILON) * (1.0 + scale) + shift


def plain_dot(former, latter):
    return jnp.dot(former, latter, preferred_element_type=jnp.float32)


def left_dot(former, latter):
    return lax.dot_general(
        former, latter, (((0,), (0,)), ((), ())), preferred_element_type=jnp.float32
    )


def right_dot(former, latter):
    return lax.dot_general(
        former, latter, (((1,), (1,)), ((), ())), preferred_element_type=jnp.float32
    )


def contract(form, former, latter):
    return jnp.einsum(form, former, latter, preferred_element_type=jnp.float32)


def einsum_forms(temporal):
    if temporal:
        return ("aibhe,ajbhe->abhij", "abhij,ajbhe->aibhe", "abhij,aibhe->ajbhe")
    return ("abihe,abjhe->abhij", "abhij,abjhe->abihe", "abhij,abihe->abjhe")


def unpack(pieces):
    attn_in, attn_out, mlp_in, mlp_out, vector = pieces
    vector = vector.astype(jnp.float32)
    return (
        attn_in.reshape(D, 3 * D),
        attn_out.reshape(D, D),
        mlp_in.reshape(D, FF),
        mlp_out.reshape(FF, D),
        vector[0:D],
        vector[D : 2 * D],
        vector[2 * D : 3 * D],
        vector[3 * D : 3 * D + FF],
        vector[3 * D + FF : 4 * D + FF],
        vector[4 * D + FF :].reshape(6, D),
    )


def tuple_of(shards, layer_index):
    return (
        shards[0][layer_index],
        shards[1][layer_index],
        shards[2][layer_index],
        shards[3][layer_index],
        shards[4][layer_index],
    )


def fetch_forward(shards, layer_index):
    return lax.all_gather(as_sent(tuple_of(shards, layer_index)), ("dp", "seq"), axis=0, tiled=True)


def piece_of(left, right):
    product = left_dot(left, right).reshape(-1)
    return product


def reduce_grads(factors, widths):
    (
        hidden,
        d_packed,
        attended,
        d_branch_one,
        hidden_two,
        d_inner,
        active,
        d_branch_two,
        d_vector,
    ) = factors
    pairs = (
        (hidden, d_packed),
        (attended, d_branch_one),
        (hidden_two, d_inner),
        (active, d_branch_two),
    )
    block = sum(widths)
    blocks_here = lax.axis_size(("dp", "seq")) * block // block
    members = []
    for (left, right), term_width in zip(pairs, widths[:4]):
        piece = piece_of(left, right)
        members.append(piece.reshape(blocks_here, term_width))
    members.append(d_vector.reshape(blocks_here, widths[4]))
    owned = lax.psum_scatter(
        jnp.concatenate(members, axis=1).reshape(-1), ("dp", "seq"), scatter_dimension=0, tiled=True
    )
    results = []
    position = 0
    for width in widths:
        results.append(owned[position : position + width])
        position = position + width
    return tuple(results)


def mod_rows(modulation):
    return [modulation[:, number][:, None, None, :] for number in range(6)]


def layer_forward(tokens, cond, weight_set, temporal):
    w_qkv, w_out, w_one, w_two, bias_q, bias_v, bias_o, bias_one, bias_two, table = weight_set
    modulation = table[None] + cond
    rows_mod = mod_rows(modulation)
    leading = tokens.shape[:-1]
    head_shape = leading + (HEADS, HEAD_DIM)
    hidden = modulate(tokens, rows_mod[1], rows_mod[0]).astype(jnp.bfloat16).reshape(-1, D)
    packed = plain_dot(hidden, w_qkv)
    queries = (packed[:, :D] + bias_q).astype(jnp.bfloat16).reshape(head_shape)
    key_heads = packed[:, D : 2 * D].astype(jnp.bfloat16).reshape(head_shape)
    values = (packed[:, 2 * D :] + bias_v).astype(jnp.bfloat16).reshape(head_shape)
    score_form, mix_form, back_form = einsum_forms(temporal)
    scores = contract(score_form, queries, key_heads) * HEAD_DIM ** (-0.5)
    row_peak = jnp.max(scores, axis=-1, keepdims=True)
    exponent = jnp.exp(scores - row_peak)
    row_total = jnp.sum(exponent, axis=-1, keepdims=True)
    weights_soft = exponent / row_total
    log_total = row_peak + jnp.log(row_total)
    attended = (
        contract(mix_form, weights_soft.astype(jnp.bfloat16), values)
        .astype(jnp.bfloat16)
        .reshape(-1, D)
    )
    branch_one = (plain_dot(attended, w_out) + bias_o).reshape(leading + (D,))
    middle = tokens + rows_mod[2] * branch_one
    hidden_two = modulate(middle, rows_mod[4], rows_mod[3]).astype(jnp.bfloat16).reshape(-1, D)
    inner_sum = plain_dot(hidden_two, w_one) + bias_one
    active = jax.nn.gelu(inner_sum, approximate=True).astype(jnp.bfloat16)
    branch_two = (plain_dot(active, w_two) + bias_two).reshape(leading + (D,))
    result = middle + rows_mod[5] * branch_two
    stored = (
        tokens,
        modulation,
        hidden,
        queries,
        key_heads,
        values,
        log_total,
        attended,
        branch_one,
        middle,
        hidden_two,
        inner_sum,
        active,
        branch_two,
    )
    return (result, stored)


def layer_backward(grad_out, stored, weight_set, temporal):
    w_qkv, w_out, w_one, w_two = (weight_set[0], weight_set[1], weight_set[2], weight_set[3])
    (
        tokens,
        modulation,
        hidden,
        queries,
        key_heads,
        values,
        log_total,
        attended,
        branch_one,
        middle,
        hidden_two,
        inner_sum,
        active,
        branch_two,
    ) = stored
    rows_mod = mod_rows(modulation)
    leading = tokens.shape[:-1]
    clips_here = tokens.shape[0]
    d_gate_two = jnp.sum(grad_out * branch_two, axis=(1, 2))
    d_branch_two = (rows_mod[5] * grad_out).astype(jnp.bfloat16).reshape(-1, D)
    d_bias_two = jnp.sum(d_branch_two, axis=0, dtype=jnp.float32)
    d_active = right_dot(d_branch_two, w_two)
    unused_gelu, gelu_back = jax.vjp(
        lambda entries: jax.nn.gelu(entries, approximate=True), inner_sum
    )
    d_inner = gelu_back(d_active)[0].astype(jnp.bfloat16)
    d_bias_one = jnp.sum(d_inner, axis=0, dtype=jnp.float32)
    d_hidden_two = right_dot(d_inner, w_one).reshape(leading + (D,))
    unused_norm, norm_back = jax.vjp(modulate, middle, rows_mod[4], rows_mod[3])
    d_middle, d_scale_two, d_shift_two = norm_back(d_hidden_two)
    grad_mid = grad_out + d_middle
    d_gate_one = jnp.sum(grad_mid * branch_one, axis=(1, 2))
    d_branch_one = (rows_mod[2] * grad_mid).astype(jnp.bfloat16).reshape(-1, D)
    d_bias_o = jnp.sum(d_branch_one, axis=0, dtype=jnp.float32)
    d_attended = (
        right_dot(d_branch_one, w_out).astype(jnp.bfloat16).reshape(leading + (HEADS, HEAD_DIM))
    )
    score_form, mix_form, back_form = einsum_forms(temporal)
    scale_qk = HEAD_DIM ** (-0.5)
    scores = contract(score_form, queries, key_heads) * scale_qk
    weights_soft = jnp.exp(scores - log_total)
    d_values = contract(back_form, weights_soft.astype(jnp.bfloat16), d_attended)
    d_probs = contract(score_form, d_attended, values)
    d_scores = weights_soft * (d_probs - jnp.sum(weights_soft * d_probs, axis=-1, keepdims=True))
    d_scores = d_scores.astype(jnp.bfloat16)
    d_queries = contract(mix_form, d_scores, key_heads) * scale_qk
    d_keys = contract(back_form, d_scores, queries) * scale_qk
    d_packed = jnp.concatenate(
        [
            d_queries.reshape(-1, D).astype(jnp.bfloat16),
            d_keys.reshape(-1, D).astype(jnp.bfloat16),
            d_values.reshape(-1, D).astype(jnp.bfloat16),
        ],
        axis=1,
    )
    d_bias_q = jnp.sum(d_packed[:, :D], axis=0, dtype=jnp.float32)
    d_bias_v = jnp.sum(d_packed[:, 2 * D :], axis=0, dtype=jnp.float32)
    d_hidden = right_dot(d_packed, w_qkv).reshape(leading + (D,))
    unused_first, first_back = jax.vjp(modulate, tokens, rows_mod[1], rows_mod[0])
    d_input, d_scale_one, d_shift_one = first_back(d_hidden)
    d_input = grad_mid + d_input
    d_modulation = jnp.stack(
        [
            d_shift_one.reshape(clips_here, D),
            d_scale_one.reshape(clips_here, D),
            d_gate_one,
            d_shift_two.reshape(clips_here, D),
            d_scale_two.reshape(clips_here, D),
            d_gate_two,
        ],
        axis=1,
    )
    d_vector = jnp.concatenate(
        [
            d_bias_q,
            d_bias_v,
            d_bias_o,
            d_bias_one,
            d_bias_two,
            jnp.sum(d_modulation, axis=0).reshape(-1),
        ]
    )
    factors = (
        hidden,
        d_packed,
        attended,
        d_branch_one,
        hidden_two,
        d_inner,
        active,
        d_branch_two,
        d_vector,
    )
    return (d_input, factors, d_modulation)


SHIFTS = (1, 2, 3)
SMALL_BYTES, LARGE_BYTES = 14 * 2**20, 24 * 2**20
STRIP = 384


def swap(x, axis):
    return lax.ppermute(x, axis, [(0, 1), (1, 0)])


def shift_z(x, k):
    n = lax.axis_size("z")
    return lax.ppermute(x, "z", [(i, (i + k) % n) for i in range(n)])


def gather_four(x, axis):
    far = swap(x, axis)
    return [x, swap(x, "core"), far, swap(far, "core")]


def scatter_four(partial, axis):
    kept_own, kept_far, sent = partial
    got = swap(sent, "core")
    far = (kept_far + got[1].astype(jnp.float32)).astype(jnp.bfloat16)
    return kept_own, got, swap(far, axis)


def source_of(number, side):
    z, here = lax.axis_index("z"), lax.axis_index(side)
    return 2 * ((z - number % 4 + 4) % 4) + (here + number // 4) % 2


def target_of(number, side):
    z, here = lax.axis_index("z"), lax.axis_index(side)
    return 2 * ((z + number % 4) % 4) + (here + number // 4) % 2


def padded(count, unit):
    return -(-count // unit) * unit


def whole():
    return pl.BlockSpec(memory_space=pltpu.VMEM)


def anywhere():
    return pl.BlockSpec(memory_space=pltpu.HBM)


def run(kernel, ins, outs, specs=None, scratch=(), flops=0):
    moved = sum(x.size * x.dtype.itemsize for x in list(ins) + list(outs))
    if specs:
        far = [spec.memory_space == pltpu.HBM for spec in specs]
        ins = [
            pltpu.with_memory_space_constraint(x, pltpu.HBM) if away else x for x, away in zip(ins, far)
        ]
    return pl.pallas_call(
        kernel,
        out_shape=tuple(outs),
        in_specs=specs or [whole()] * len(ins),
        out_specs=tuple([whole()] * len(outs)),
        scratch_shapes=list(scratch),
        compiler_params=pltpu.CompilerParams(vmem_limit_bytes=LARGE_BYTES if scratch else SMALL_BYTES),
        cost_estimate=pl.CostEstimate(flops=flops, bytes_accessed=moved, transcendentals=0),
    )(*ins)


def f32(*shape):
    return jax.ShapeDtypeStruct(shape, jnp.float32)


def bf16(*shape):
    return jax.ShapeDtypeStruct(shape, jnp.bfloat16)


def normal_parts(x):
    average = jnp.mean(x, axis=-1, keepdims=True)
    centred = x - average
    variance = jnp.mean(centred * centred, axis=-1, keepdims=True)
    inverse = lax.rsqrt(variance + EPSILON)
    return centred * inverse, inverse


def modulated(x, modulation, scale_row, order):
    normal, _ = normal_parts(x)
    scale = modulation[scale_row : scale_row + 1]
    shift = modulation[scale_row - 1 : scale_row]
    hidden = (normal * (1.0 + scale) + shift).astype(jnp.bfloat16)
    return plain_dot(hidden, order).astype(jnp.bfloat16)


def enter_kernel(x_ref, modulation_ref, order_ref, hidden_ref):
    x = x_ref[...].astype(jnp.float32)
    hidden_ref[...] = modulated(x, modulation_ref[...], 1, order_ref[...])


def summed(own_ref, got_ref, far_ref):
    return own_ref[...] + got_ref[0].astype(jnp.float32) + far_ref[...].astype(jnp.float32)


def middle_kernel(
    own_ref, got_ref, far_ref, bias_ref, x_ref, modulation_ref, order_ref, branch_ref, middle_ref, hidden_ref
):
    branch = summed(own_ref, got_ref, far_ref) + bias_ref[...]
    modulation = modulation_ref[...]
    middle = x_ref[...].astype(jnp.float32) + modulation[2:3] * branch
    branch_ref[...] = branch
    middle_ref[...] = middle
    hidden_ref[...] = modulated(middle, modulation, 4, order_ref[...])


def leave_kernel(own_ref, got_ref, far_ref, bias_ref, middle_ref, modulation_ref, branch_ref, result_ref):
    branch = summed(own_ref, got_ref, far_ref) + bias_ref[...]
    branch_ref[...] = branch
    result_ref[...] = (middle_ref[...] + modulation_ref[5:6] * branch).astype(jnp.bfloat16)


def start_rows(pieces, buffer, sems, first):
    copies = []
    for number, piece in enumerate(pieces):
        rows = piece.shape[0]
        copies.append(
            pltpu.make_async_copy(piece, buffer.at[pl.ds(number * rows, rows)], sems.at[first + number])
        )
        copies[-1].start()
    return copies


def start_weights(pieces, side, at, rows, buffer, sems, first):
    if len(pieces) == 1:
        found = [(pieces[0].at[number], number) for number in range(8)]
    else:
        found = [(piece, source_of(number, side)) for number, piece in enumerate(pieces)]
    copies = []
    for number, (piece, source) in enumerate(found):
        target = pl.multiple_of(source * rows, 16)
        copies.append(
            pltpu.make_async_copy(
                piece.at[pl.ds(at, rows)], buffer.at[pl.ds(target, rows)], sems.at[first + number]
            )
        )
        copies[-1].start()
    return copies


def wait_all(copies):
    for copy in copies:
        copy.wait()


def strips(size):
    return [(at, min(STRIP, size - at)) for at in range(0, size, STRIP)]


def deal(product, at, width, own_ref, far_ref, sent_ref):
    count = own_ref.shape[0]
    columns = slice(at, at + width)
    own_ref[:, columns] = product[:count]
    sent_ref[0, :, columns] = product[count : 2 * count].astype(jnp.bfloat16)
    far_ref[:, columns] = product[2 * count : 3 * count]
    sent_ref[1, :, columns] = product[3 * count :].astype(jnp.bfloat16)


def softmax_of(scores, count, period):
    if period:
        row = lax.broadcasted_iota(jnp.int32, scores.shape, 0) % period
        column = lax.broadcasted_iota(jnp.int32, scores.shape, 1) % period
        scores = jnp.where(row == column, scores, -1e30)
    exponent = jnp.exp(scores - jnp.max(scores, axis=-1, keepdims=True))
    return exponent * (1.0 / jnp.sum(exponent, axis=-1, keepdims=True))


def owners(width, per_head):
    return lax.broadcasted_iota(jnp.int32, (1, width), 1) // per_head


def by_head(x, owner, heads):
    return jnp.concatenate([jnp.where(owner == head, x, 0) for head in range(heads)], axis=0)


def of_head(stacked, owner, heads, count):
    chosen = stacked[:count]
    for head in range(1, heads):
        chosen = jnp.where(owner == head, stacked[head * count : (head + 1) * count], chosen)
    return chosen


def attention_kernel(period, heads, split, n_pieces, *refs):
    hidden, pieces, refs = refs[:4], refs[4 : 4 + n_pieces], refs[4 + n_pieces :]
    bias_ref, packed_ref, mixed_ref, probs_ref, own_ref, far_ref, sent_ref, left, qkv, out, sems = refs
    copies = start_rows(hidden, left, sems, 0)
    copies += start_weights(pieces, "x", 0, split, qkv, sems, 4)
    later = start_weights(pieces, "x", split, out.shape[0] // 8, out, sems, 12)
    wide = out.shape[0]
    narrow = (qkv.shape[1] - wide) // 2
    count = own_ref.shape[0]
    narrow_owner, wide_owner = owners(narrow, HEAD_DIM), owners(wide, wide // heads)
    wait_all(copies)
    for at, size in strips(qkv.shape[1]):
        product = plain_dot(left[...], qkv[:, at : at + size]) + bias_ref[:, at : at + size]
        packed_ref[:, at : at + size] = product.astype(jnp.bfloat16)
    for number in range(4):
        rows = pl.ds(number * count, count)
        packed = packed_ref[rows, :]
        values = packed[:, :wide]
        queries = by_head(packed[:, wide : wide + narrow], narrow_owner, heads)
        scores = right_dot(queries, packed[:, wide + narrow :]) * HEAD_DIM ** (-0.5)
        weights_soft = softmax_of(scores, count, period)
        probs_ref[pl.ds(number * heads * count, heads * count), :] = weights_soft
        mixed = plain_dot(weights_soft.astype(jnp.bfloat16), values)
        mixed_ref[rows, :] = of_head(mixed, wide_owner, heads, count).astype(jnp.bfloat16)
    wait_all(later)
    for at, size in strips(out.shape[1]):
        deal(plain_dot(mixed_ref[...], out[:, at : at + size]), at, size, own_ref, far_ref, sent_ref)


def attention_back_kernel(heads, split, n_pieces, *refs):
    d_branch, pieces, refs = refs[:4], refs[4 : 4 + n_pieces], refs[4 + n_pieces :]
    packed_ref, probs_ref, d_packed_ref, sums_ref, own_ref, far_ref, sent_ref, left, qkv, out, sems = refs
    copies = start_rows(d_branch, left, sems, 0)
    copies += start_weights(pieces, "x", split, out.shape[0] // 8, out, sems, 4)
    later = start_weights(pieces, "x", 0, split, qkv, sems, 12)
    wide = out.shape[0]
    narrow = (qkv.shape[1] - wide) // 2
    count = own_ref.shape[0]
    scale = HEAD_DIM ** (-0.5)
    narrow_owner, wide_owner = owners(narrow, HEAD_DIM), owners(wide, wide // heads)
    sums = jnp.zeros((1, wide + 2 * narrow), jnp.float32)
    wait_all(copies)
    d_mixed_all = right_dot(left[...], out[...]).astype(jnp.bfloat16)
    for number in range(4):
        rows = pl.ds(number * count, count)
        d_mixed = by_head(d_mixed_all[number * count : (number + 1) * count], wide_owner, heads)
        packed = packed_ref[rows, :]
        queries = by_head(packed[:, wide : wide + narrow], narrow_owner, heads)
        weights_soft = probs_ref[pl.ds(number * heads * count, heads * count), :]
        d_probs = right_dot(d_mixed, packed[:, :wide])
        inner = jnp.sum(weights_soft * d_probs, axis=-1, keepdims=True)
        d_scores = (weights_soft * (d_probs - inner)).astype(jnp.bfloat16)
        d_values = left_dot(weights_soft.astype(jnp.bfloat16), d_mixed)
        d_keys = left_dot(d_scores, queries)
        d_queries = of_head(
            plain_dot(d_scores, packed[:, wide + narrow :]), narrow_owner, heads, count
        )
        d_packed = jnp.concatenate([d_values, d_queries * scale, d_keys * scale], axis=1)
        d_packed = d_packed.astype(jnp.bfloat16)
        d_packed_ref[rows, :] = d_packed
        sums = sums + jnp.sum(d_packed.astype(jnp.float32), axis=0, keepdims=True)
    sums_ref[...] = sums
    wait_all(later)
    for at, size in strips(qkv.shape[0]):
        product = right_dot(d_packed_ref[...], qkv[at : at + size, :])
        deal(product, at, size, own_ref, far_ref, sent_ref)


def gelu_pair(u):
    inner = 0.7978845608028654 * (u + 0.044715 * u * u * u)
    bent = jnp.tanh(inner)
    value = 0.5 * u * (1.0 + bent)
    slope = 0.5 * (1.0 + bent) + 0.5 * u * (1.0 - bent * bent) * (
        0.7978845608028654 * (1.0 + 3 * 0.044715 * u * u)
    )
    return value, slope


def mlp_kernel(split, at_two, n_one, n_two, *refs):
    refs = list(refs)
    hidden, refs = refs[:4], refs[4:]
    pieces, refs = refs[:n_one], refs[n_one:]
    pieces_two, refs = refs[:n_two], refs[n_two:]
    bias_ref, active_ref, slope_ref, own_ref, far_ref, sent_ref, left, one, two, sems = refs
    copies = start_rows(hidden, left, sems, 0)
    copies += start_weights(pieces, "y", 0, split, one, sems, 4)
    later = start_weights(pieces_two, "y", at_two, two.shape[0] // 8, two, sems, 12)
    wait_all(copies)
    for at, size in strips(one.shape[1]):
        columns = slice(at, at + size)
        u = plain_dot(left[...], one[:, columns]) + bias_ref[:, columns]
        value, slope = gelu_pair(u)
        active_ref[:, columns] = value.astype(jnp.bfloat16)
        slope_ref[:, columns] = slope.astype(jnp.bfloat16)
    wait_all(later)
    for at, size in strips(two.shape[1]):
        deal(plain_dot(active_ref[...], two[:, at : at + size]), at, size, own_ref, far_ref, sent_ref)


def mlp_back_kernel(split, at_two, n_one, n_two, *refs):
    refs = list(refs)
    d_branch, refs = refs[:4], refs[4:]
    pieces, refs = refs[:n_one], refs[n_one:]
    pieces_two, refs = refs[:n_two], refs[n_two:]
    slope_ref, d_inner_ref, sums_ref, own_ref, far_ref, sent_ref, left, one, two, sems = refs
    copies = start_rows(d_branch, left, sems, 0)
    copies += start_weights(pieces_two, "y", at_two, two.shape[0] // 8, two, sems, 4)
    later = start_weights(pieces, "y", 0, split, one, sems, 12)
    wait_all(copies)
    for at, size in strips(two.shape[0]):
        columns = slice(at, at + size)
        d_active = right_dot(left[...], two[columns, :])
        d_inner = (d_active * slope_ref[:, columns].astype(jnp.float32)).astype(jnp.bfloat16)
        d_inner_ref[:, columns] = d_inner
        sums_ref[:, columns] = jnp.sum(d_inner.astype(jnp.float32), axis=0, keepdims=True)
    wait_all(later)
    for at, size in strips(one.shape[0]):
        product = right_dot(d_inner_ref[...], one[at : at + size, :])
        deal(product, at, size, own_ref, far_ref, sent_ref)


def total_sums(ref, *members):
    rows = [jnp.sum(m.astype(jnp.float32), axis=0, keepdims=True) for m in members]
    ref[...] = jnp.concatenate(rows, axis=0)


def open_back_kernel(grad_ref, branch_ref, modulation_ref, d_branch_ref, sums_ref):
    grad = grad_ref[...].astype(jnp.float32)
    d_branch = (modulation_ref[5:6] * grad).astype(jnp.bfloat16)
    d_branch_ref[...] = d_branch
    total_sums(sums_ref, grad * branch_ref[...], d_branch)


def natural(total, order):
    high = total.astype(jnp.bfloat16)
    low = (total - high.astype(jnp.float32)).astype(jnp.bfloat16)
    both = right_dot(jnp.concatenate([high, low], axis=0), order)
    return both[: total.shape[0]] + both[total.shape[0] :]


def norm_back(d_hidden, x, scale):
    normal, inverse = normal_parts(x)
    entry = d_hidden * (1.0 + scale)
    average = jnp.mean(entry, axis=-1, keepdims=True)
    along = jnp.mean(entry * normal, axis=-1, keepdims=True)
    return (entry - average - normal * along) * inverse, d_hidden * normal


def middle_back_kernel(
    own_ref, got_ref, far_ref, grad_ref, x_ref, branch_ref, modulation_ref, order_ref, d_branch_ref, grad_mid_ref, sums_ref
):
    d_hidden = natural(summed(own_ref, got_ref, far_ref), order_ref[...])
    modulation = modulation_ref[...]
    d_x, d_scale = norm_back(d_hidden, x_ref[...], modulation[4:5])
    grad_mid = grad_ref[...].astype(jnp.float32) + d_x
    grad_mid_ref[...] = grad_mid
    d_branch = (modulation[2:3] * grad_mid).astype(jnp.bfloat16)
    d_branch_ref[...] = d_branch
    total_sums(sums_ref, d_hidden, d_scale, grad_mid * branch_ref[...], d_branch)


def close_back_kernel(own_ref, got_ref, far_ref, grad_ref, x_ref, modulation_ref, order_ref, d_x_ref, sums_ref):
    d_hidden = natural(summed(own_ref, got_ref, far_ref), order_ref[...])
    d_x, d_scale = norm_back(d_hidden, x_ref[...].astype(jnp.float32), modulation_ref[1:2])
    d_x_ref[...] = (grad_ref[...] + d_x).astype(d_x_ref.dtype)
    total_sums(sums_ref, d_hidden, d_scale)


def factor(groups):
    pairs = [pair for members, _ in groups for pair in members]
    ins, scratch, flops = [], [], 0
    for left, right, height in pairs:
        ins += left + right
        count = sum(piece.shape[0] for piece in left)
        scratch.append(pltpu.VMEM((left[0].shape[1], count), jnp.bfloat16))
        if len(right) > 1:
            scratch.append(pltpu.VMEM((count, right[0].shape[1]), jnp.bfloat16))
        flops += 2 * count * left[0].shape[1] * right[0].shape[1]
    outs = []
    for members, side in groups:
        height, width = sum(m[2] for m in members), members[0][1][0].shape[1]
        outs += [bf16(height, width) for _ in range(8)] if side else [bf16(8 * height, width)]

    def kernel(*refs):
        refs = iter(refs)
        taken = [
            ([next(refs) for _ in left], [next(refs) for _ in right], height)
            for left, right, height in pairs
        ]
        results = [next(refs) for _ in outs]
        ready = []
        for left, right, height in taken:
            flip = next(refs)
            at = 0
            for piece in left:
                flip[:, at : at + piece.shape[0]] = piece[...].T
                at += piece.shape[0]
            lay = right[0]
            if len(right) > 1:
                lay = next(refs)
                at = 0
                for piece in right:
                    lay[at : at + piece.shape[0], :] = piece[...]
                    at += piece.shape[0]
            ready.append((flip, lay, height))
        for members, side in groups:
            mine, ready = ready[: len(members)], ready[len(members) :]
            total = sum(member[2] for member in mine)
            for number in range(8):
                at = 0 if side else number * total
                result = results[number] if side else results[0]
                target = target_of(number, side) if side else number
                for flip, lay, height in mine:
                    rows = pl.ds(pl.multiple_of(target * height, 16), height)
                    product = plain_dot(flip[rows, :], lay[...])
                    result[at : at + height, :] = product.astype(jnp.bfloat16)
                    at += height
            results = results[8:] if side else results[1:]

    results = list(run(kernel, ins, outs, scratch=scratch, flops=flops))
    given = []
    for _, side in groups:
        if side:
            given.append((results[:4], results[4:8]))
        else:
            given.append(results[0])
        results = results[8:] if side else results[1:]
    return given


def placed_blocks(half, n_seq):
    for owner in range(4 * n_seq):
        y, core, z, x = owner // (2 * n_seq), (owner // n_seq) % 2, (owner % n_seq) // 2, owner % 2
        yield owner * half, 2 * x + core, (2 * z + y) * half


def part_kernel(half, n_seq, rows_ref, parts_ref):
    rows = rows_ref.shape[1]
    for layer in range(2):
        for at, part, place in placed_blocks(half, n_seq):
            parts_ref[part, layer, 0:rows, place : place + half] = rows_ref[layer, :, at : at + half]


def join_kernel(half, n_seq, room, parts_ref, rows_ref):
    rows = rows_ref.shape[1]
    for layer in range(2):
        for at, part, place in placed_blocks(half, n_seq):
            block = parts_ref[part, layer * room : layer * room + rows, place : place + half]
            rows_ref[layer, :, at : at + half] = block.astype(jnp.float32)


def vector_kernel(
    n_seq, rows, sums_one_ref, sums_mid_ref, sums_two_ref, qkv_ref, one_ref, vector_ref, modulation_ref
):
    y, core, x = lax.axis_index("y"), lax.axis_index("core"), lax.axis_index("x")
    here = 2 * y + core
    room = padded(rows, 16)
    wide, width, half = n_seq * room, n_seq * rows, one_ref.shape[1] // n_seq
    for number in range(4):
        mine = here == number
        query = qkv_ref[:, wide : wide + width]
        vector_ref[:, number * width : (number + 1) * width] = jnp.where(mine, query, 0.0)
        for block in range(n_seq):
            at = D + number * width + block * rows
            value = qkv_ref[:, block * room : block * room + rows]
            vector_ref[:, at : at + rows] = jnp.where(mine, value, 0.0)
    for owner in range(4 * n_seq):
        mine = ((owner // n_seq) % 2 == core) & (owner % 2 == x)
        block = 2 * ((owner % n_seq) // 2) + owner // (2 * n_seq)
        at = 3 * D + owner * half
        vector_ref[:, at : at + half] = jnp.where(mine, one_ref[:, block * half : (block + 1) * half], 0.0)
    vector_ref[:, 2 * D : 3 * D] = sums_mid_ref[3:4]
    vector_ref[:, 3 * D + FF : 4 * D + FF] = sums_two_ref[1:2]
    members = (
        (sums_one_ref, 0),
        (sums_one_ref, 1),
        (sums_mid_ref, 2),
        (sums_mid_ref, 0),
        (sums_mid_ref, 1),
        (sums_two_ref, 0),
    )
    for number, (ref, row) in enumerate(members):
        at = (4 + number) * D + FF
        vector_ref[:, at : at + D] = ref[row : row + 1]
        modulation_ref[number : number + 1, :] = ref[row : row + 1]


def order_matrix(n_dp, n_seq, rows, room, crossed):
    place = lax.broadcasted_iota(jnp.int32, (D, n_dp * n_seq * room), 1)
    feature = lax.broadcasted_iota(jnp.int32, (D, n_dp * n_seq * room), 0)
    block, inner = place // room, place % room
    outer, local = block // n_dp, block % n_dp
    z, side, across, core = outer // 2, outer % 2, local // 2, local % 2
    x, y = (across, side) if crossed else (side, across)
    owner = (2 * y + core) * n_seq + 2 * z + x
    return ((feature == owner * rows + inner) & (inner < rows)).astype(jnp.bfloat16)


def grow(x, axis, size):
    pads = [(0, 0)] * x.ndim
    pads[axis] = (0, size - x.shape[axis])
    return jnp.pad(x, pads)


def exchange(parts, axis):
    return lax.all_to_all(parts, (axis, "core"), split_axis=0, concat_axis=0, tiled=True)


def spread(values, n_seq, rows, room):
    lead = values.shape[:-1]
    return grow(values.reshape(lead + (n_seq, rows)), len(lead) + 1, room).reshape(lead + (-1,))


def ordered_vectors(everyone, n_dp, n_seq, count):
    chosen = owner_rows(n_dp, n_seq, -1)
    ordered = left_dot(chosen.astype(jnp.bfloat16), everyone)
    return ordered.reshape(n_dp * n_seq, 2, count).transpose(1, 0, 2).reshape(2, -1)


def owner_rows(n_dp, n_seq, sign):
    count = n_dp * n_seq
    relative = lax.broadcasted_iota(jnp.int32, (count, count), 0)
    owner = lax.broadcasted_iota(jnp.int32, (count, count), 1)
    n_z = n_seq // 2
    z = (lax.axis_index("z") + sign * (relative // (2 * n_dp)) + n_z) % n_z
    x = lax.axis_index("x") ^ ((relative // n_dp) % 2)
    y = lax.axis_index("y") ^ ((relative // 2) % 2)
    core = lax.axis_index("core") ^ (relative % 2)
    source = (2 * y + core) * n_seq + 2 * z + x
    return (owner == source).astype(jnp.float32)


def scatter_vectors(sums, n_dp, n_seq, finish):
    count = sums.shape[1] // (n_dp * n_seq)
    rows = sums.reshape(2, n_dp * n_seq, count).transpose(1, 0, 2).reshape(n_dp * n_seq, -1)
    chosen = owner_rows(n_dp, n_seq, 1)
    rows = jnp.dot(chosen, rows, precision=lax.Precision.HIGHEST)
    quarters = jnp.split(rows, n_seq // 2)
    got = yield (quarters[0], [shift_z(quarters[k], k) for k in SHIFTS])
    total = got[0] + sum(got[1])
    got = yield (total, swap(total[n_dp:], "x"))
    total = got[0][:n_dp] + got[1]
    got = yield (total, swap(total[2:], "y"))
    total = got[0][:2] + got[1]
    got = yield (total, swap(total[1:], "core"))
    finish((got[0][:1] + got[1]).reshape(2, count))
    yield None


def sum_seq(x, finish):
    got = yield (x, swap(x, "x"))
    total = got[0] + got[1]
    got = yield (total, [shift_z(total, k) for k in SHIFTS])
    finish(got[0] + sum(got[1]))
    yield None


def slice_of(vector, n_dp):
    width = vector.shape[0] // n_dp
    here = 2 * lax.axis_index("y") + lax.axis_index("core")
    return lax.dynamic_slice(vector, (here * width,), (width,))


def crossed_slice(vector, n_z):
    blocks = vector.reshape(2, 2, n_z, 2, -1)
    blocks = lax.dynamic_index_in_dim(blocks, lax.axis_index("x"), 3, keepdims=False)
    blocks = lax.dynamic_index_in_dim(blocks, lax.axis_index("core"), 1, keepdims=False)
    return blocks.transpose(1, 0, 2).reshape(-1)


class Gather:
    def __init__(self, pieces, side, wait):
        self.side, self.wait = side, wait
        self.column, self.across, self.sent, self.waiting = [pieces], [], 0, False

    def wants_x(self):
        return self.sent < len(self.column)

    def send_x(self):
        self.sent += 1
        return [swap(piece, self.side) for piece in self.column[self.sent - 1]]

    def got_x(self, pieces):
        self.across.append(pieces)

    def wants_z(self):
        return len(self.column) < 4 and not self.waiting

    def send_z(self):
        self.waiting = True
        return [shift_z(piece, 1) for piece in self.column[-1]]

    def got_z(self, pieces):
        self.waiting = False
        self.column.append(pieces)

    def finished(self):
        return len(self.across) == 4

    def pieces(self, index):
        return [piece[index] for piece in self.column + self.across]


class Reduce:
    def __init__(self, mine, other, side, wait, finish):
        self.side, self.wait = side, wait
        self.mine, self.other, self.finish = mine, other, finish
        self.sent, self.got, self.hops, self.carried, self.result = 3, {}, 3, None, None

    def wants_x(self):
        return self.sent >= 0

    def send_x(self):
        self.sent -= 1
        return [swap(piece, self.side) for piece in self.other[self.sent + 1]]

    def got_x(self, pieces):
        self.got[3 - len(self.got)] = pieces

    def added(self, k):
        total = [m.astype(jnp.float32) + g.astype(jnp.float32) for m, g in zip(self.mine[k], self.got[k])]
        if k < 3:
            total = [t + c.astype(jnp.float32) for t, c in zip(total, self.carried)]
        return total

    def wants_z(self):
        ready = self.hops == 3 or self.carried is not None
        return self.hops > 0 and self.hops in self.got and ready

    def send_z(self):
        total = self.added(self.hops)
        self.hops -= 1
        self.carried = None
        return [shift_z(t.astype(jnp.bfloat16), 1) for t in total]

    def got_z(self, pieces):
        self.carried = pieces

    def finished(self):
        return self.hops == 0 and self.carried is not None and 0 in self.got


class Lane:
    def __init__(self):
        self.jobs, self.flight, self.extra, self.scripts = [], [], [], []

    def issue(self):
        for job in [job for job in self.jobs if isinstance(job, Reduce)]:
            if job.wants_x():
                self.flight.append((job.wait[0], job, "x", job.send_x()))
            if job.wants_z():
                self.flight.append((job.wait[1], job, "z", job.send_z()))
        for job in [job for job in self.jobs if isinstance(job, Gather)]:
            for kind, link in (("x", job.side), ("z", "z")):
                if getattr(job, "wants_" + kind)():
                    self.flight.append((job.wait, job, kind, getattr(job, "send_" + kind)()))
        for script in self.scripts:
            script[1] = script[0].send(script[1])
        self.scripts = [script for script in self.scripts if script[1] is not None]

    def add(self, mine, other, side, wait, finish):
        job = Reduce([[m] for m in mine], [[m] for m in other], side, wait, finish)
        self.jobs.append(job)
        self.flight.append((wait[0], job, "x", job.send_x()))

    def close(self):
        for job in [job for job in self.jobs if job.finished()]:
            self.jobs.remove(job)
            if isinstance(job, Reduce):
                job.finish(job.added(0))

    def tick(self, values):
        due = [f for f in self.flight if f[0] == 1]
        values, arrived, _, steps = lax.optimization_barrier(
            (values, [f[3] for f in due], self.extra, [script[1] for script in self.scripts])
        )
        for script, step in zip(self.scripts, steps):
            script[1] = step
        self.flight = [(f[0] - 1,) + f[1:] for f in self.flight if f[0] > 1]
        self.extra = []
        for (_, job, kind, _), pieces in zip(due, arrived):
            getattr(job, "got_" + kind)(pieces)
        self.close()
        self.issue()
        return values

    def until(self, job, values):
        while not job.finished():
            values = self.tick(values)
        return values


def on_device_split(tokens, cond, d_out, attn_in, attn_out, mlp_in, mlp_out, vectors):
    n_dp, n_seq = 4, 2 * lax.axis_size("z")
    heads = HEADS // n_dp
    width = heads * HEAD_DIM
    frames, places = tokens.shape[1] * n_seq, tokens.shape[2]
    periods = (0, places // n_seq)
    count = tokens.shape[1] * places
    group = n_dp * count
    rows = D // (n_dp * n_seq)
    room = rows
    out_room = padded(rows, 16)
    deep, wide = n_dp * n_seq * room, n_seq * out_room
    narrow = padded(width, 128)
    packed_width = wide + 2 * narrow
    inner = FF // n_dp
    split = n_dp * room
    half = inner // n_seq
    order = order_matrix(n_dp, n_seq, rows, room, False)
    order_mlp = order_matrix(n_dp, n_seq, rows, room, True)

    parts = attn_in.reshape(2, rows, 3, n_dp, width).transpose(2, 3, 0, 1, 4)
    qkv_parts = jnp.concatenate(
        [spread(parts[2], n_seq, rows, out_room), grow(parts[0], 3, narrow), grow(parts[1], 3, narrow)],
        axis=3,
    )
    qkv_parts = exchange(grow(qkv_parts, 2, room).reshape(n_dp, 2 * room, -1), "y")
    qkv_parts = qkv_parts.reshape(n_dp, 2, room, -1)
    out_parts = grow(attn_out.reshape(2, rows, D), 1, out_room)
    two_parts = mlp_out.reshape(2, half, D)

    def attention_piece(index):
        return jnp.concatenate([qkv_parts[:, index].reshape(split, -1), out_parts[index]])

    def regroup(x):
        x = x.reshape(n_seq, count // n_seq, D)
        return lax.all_to_all(x, ("z", "x"), split_axis=0, concat_axis=0, tiled=True).reshape(-1, D)

    lane = Lane()
    mine = vectors.reshape(1, -1)
    near = jnp.concatenate([mine, swap(mine, "core")])
    clips = jnp.concatenate([near, swap(near, "y")])
    pair = jnp.concatenate([clips, swap(clips, "x")])
    everyone = jnp.concatenate([pair] + [shift_z(pair, k) for k in SHIFTS])
    first = attention_piece(0)
    mlp_in = mlp_in.reshape(2, rows, FF)
    everyone, first, mlp_in, qkv_parts, out_parts, two_parts = lax.optimization_barrier(
        (everyone, first, mlp_in, qkv_parts, out_parts, two_parts)
    )
    attention_job = Gather([first], "x", 1)
    lane.jobs.append(attention_job)
    lane.issue()
    (one_parts,) = run(
        functools.partial(part_kernel, half, n_seq), [mlp_in], [bf16(n_dp, 2, room, inner)]
    )
    vector = ordered_vectors(everyone, n_dp, n_seq, vectors.shape[1])
    biases, modulations = [], []
    for index in range(2):
        v = vector[index]
        bias_q, bias_v = slice_of(v[0:D], n_dp), slice_of(v[D : 2 * D], n_dp)
        bias_q = grow(bias_q, 0, narrow)
        bias_v = spread(bias_v, n_seq, rows, out_room)
        biases.append(
            (
                jnp.concatenate([bias_v, bias_q, jnp.zeros_like(bias_q)])[None],
                v[None, 2 * D : 3 * D],
                crossed_slice(v[3 * D : 3 * D + FF], n_seq // 2)[None],
                v[None, 3 * D + FF : 4 * D + FF],
            )
        )
        modulations.append(v[4 * D + FF :].reshape(6, D) + cond[0])

    def scratch(left_width, *shapes):
        return [
            pltpu.VMEM((group, left_width), jnp.bfloat16),
            *[pltpu.VMEM(shape, jnp.bfloat16) for shape in shapes],
            pltpu.SemaphoreType.DMA((20,)),
        ]

    attention_rooms = ((deep, packed_width), (wide, D))
    mlp_rooms = ((deep, inner), (inner, D))
    attention_flops = 4 * group * (deep * packed_width + wide * D)
    mlp_flops = 2 * group * (deep + D) * inner
    own_shapes = [f32(count, D), f32(count, D), bf16(2, count, D)]
    deep_shapes = [f32(count, deep), f32(count, deep), bf16(2, count, deep)]

    def opened(x, index):
        return run(enter_kernel, [x, modulations[index], order], [bf16(count, deep)])[0]

    def attention(index, hidden, pieces):
        return run(
            functools.partial(attention_kernel, periods[index], heads, split, len(pieces)),
            hidden + pieces + [biases[index][0]],
            [bf16(group, packed_width), bf16(group, wide), f32(group * heads, count)] + own_shapes,
            specs=[anywhere()] * (4 + len(pieces)) + [whole()],
            scratch=scratch(deep, *attention_rooms),
            flops=attention_flops,
        )

    def attention_back(index, d_branch, pieces, packed, probs):
        return run(
            functools.partial(attention_back_kernel, heads, split, len(pieces)),
            d_branch + pieces + [packed, probs],
            [bf16(group, packed_width), f32(1, packed_width)] + deep_shapes,
            specs=[anywhere()] * (4 + len(pieces)) + [whole()] * 2,
            scratch=scratch(D, *attention_rooms),
            flops=attention_flops,
        )

    def middle(index, own, x):
        return run(
            middle_kernel,
            list(own) + [biases[index][1], x, modulations[index], order_mlp],
            [f32(count, D), f32(count, D), bf16(count, deep)],
        )

    def mlp(index, hidden, pieces, pieces_two, at):
        return run(
            functools.partial(mlp_kernel, split, at, len(pieces), len(pieces_two)),
            hidden + pieces + pieces_two + [biases[index][2]],
            [bf16(group, inner), bf16(group, inner)] + own_shapes,
            specs=[anywhere()] * (4 + len(pieces) + len(pieces_two)) + [whole()],
            scratch=scratch(deep, *mlp_rooms),
            flops=mlp_flops,
        )

    def mlp_back(d_branch, pieces, pieces_two, at, slope):
        return run(
            functools.partial(mlp_back_kernel, split, at, len(pieces), len(pieces_two)),
            d_branch + pieces + pieces_two + [slope],
            [bf16(group, inner), f32(1, inner)] + deep_shapes,
            specs=[anywhere()] * (4 + len(pieces) + len(pieces_two)) + [whole()],
            scratch=scratch(D, *mlp_rooms),
            flops=mlp_flops,
        )

    def left(index, own, x):
        return run(
            leave_kernel,
            list(own) + [biases[index][3], x, modulations[index]],
            [f32(count, D), bf16(count, D)],
        )

    def opened_back(index, grad, branch):
        return run(
            open_back_kernel, [grad, branch, modulations[index]], [bf16(count, D), f32(2, D)]
        )

    def middle_back(index, own, grad, x, branch):
        return run(
            middle_back_kernel,
            list(own) + [grad, x, branch, modulations[index], order_mlp],
            [bf16(count, D), f32(count, D), f32(4, D)],
        )

    def closed_back(index, own, grad, x, out_type):
        return run(
            close_back_kernel,
            list(own) + [grad, x, modulations[index], order],
            [jax.ShapeDtypeStruct((count, D), out_type), f32(2, D)],
        )

    def vector_sums(sums_one, sums_mid, sums_two, d_bias_qkv, d_bias_one):
        return run(
            functools.partial(vector_kernel, n_seq, rows),
            [sums_one, sums_mid, sums_two, d_bias_qkv, d_bias_one],
            [f32(1, 10 * D + FF), f32(6, D)],
        )

    x_zero = tokens.reshape(-1, D)
    hidden, one_parts, two_parts = lane.tick((opened(x_zero, 0), one_parts, two_parts))
    one_parts = exchange(one_parts.reshape(n_dp, 2 * room, inner), "x").reshape(n_dp, 2, room, inner)
    hidden_zero, one_parts, two_parts, qkv_parts, out_parts = lane.tick(
        (gather_four(hidden, "y"), one_parts, two_parts, qkv_parts, out_parts)
    )
    two_zero = [lax.all_gather(two_parts[0], ("z", "y"))]
    piece = one_parts[:, 0].reshape(split, inner)
    later = jnp.concatenate([one_parts[:, 1].reshape(split, inner), two_parts[1]])
    hidden_zero, piece, later, second = lane.tick((hidden_zero, piece, later, attention_piece(1)))
    mlp_job = Gather([piece], "y", 1)
    lane.jobs.append(mlp_job)
    lane.issue()
    hidden_zero = lane.until(attention_job, hidden_zero)
    attention_zero = attention_job.pieces(0)
    packed_zero, mixed_zero, probs_zero, *partial = attention(0, hidden_zero, attention_zero)
    next_job = Gather([second], "x", 1)
    lane.jobs.append(next_job)
    partial = lane.tick(partial)
    own = lane.tick(scatter_four(partial, "y"))
    branch_zero, middle_zero, hidden = middle(0, own, x_zero)
    inside_zero, later = lane.until(mlp_job, lane.tick((gather_four(hidden, "x"), later)))
    mlp_one = [lax.all_gather(later, ("z", "y"))]
    mlp_zero = mlp_job.pieces(0)
    active_zero, slope_zero, *partial = mlp(0, inside_zero, mlp_zero, two_zero, 0)
    own = lane.tick(scatter_four(lane.tick(partial), "x"))
    end_zero, result = left(0, own, middle_zero)

    x_one = lane.tick(regroup(result))
    hidden_one = lane.until(next_job, lane.tick(gather_four(opened(x_one, 1), "y")))
    attention_one = next_job.pieces(0)
    packed_one, mixed_one, probs_one, *partial = attention(1, hidden_one, attention_one)
    partial, d_out = lax.optimization_barrier((partial, d_out))
    grad_places = regroup(d_out.reshape(-1, D))
    branch_one, middle_one, hidden = middle(1, scatter_four(partial, "y"), x_one)
    inside_one, grad_places = lax.optimization_barrier((gather_four(hidden, "x"), grad_places))
    active_one, slope_one, *partial = mlp(1, inside_one, mlp_one, mlp_one, split)
    end_one, result = left(1, scatter_four(partial, "x"), middle_one)
    output = regroup(result).astype(jnp.float32)

    d_end, sums_two = opened_back(1, grad_places, end_one)
    d_end = gather_four(d_end, "x")
    d_inner, d_bias_one, *partial = mlp_back(d_end, mlp_one, mlp_one, split, slope_one)
    partial, output = lax.optimization_barrier((partial, output))
    owned = {}

    def keep(name):
        return functools.partial(owned.__setitem__, name)

    (d_mlp,) = factor(
        [([(inside_one, [d_inner], split), ([active_one], d_end, half)], None)]
    )
    own, d_mlp = lax.optimization_barrier((scatter_four(partial, "x"), d_mlp))
    d_mlp_one = lax.psum_scatter(d_mlp, ("z", "y"), scatter_dimension=0, tiled=True)
    d_branch, grad_mid, sums_mid = middle_back(1, own, grad_places, middle_one, branch_one)
    d_branch_one = gather_four(d_branch, "y")
    d_packed, d_bias_qkv, *partial = attention_back(
        1, d_branch_one, attention_one, packed_one, probs_one
    )
    (ring,) = factor(
        [([(hidden_one, [d_packed], split), ([mixed_one], d_branch_one, out_room)], "x")]
    )
    own, ring = lax.optimization_barrier((scatter_four(partial, "y"), ring))
    grad, sums_one = closed_back(1, own, grad_mid, x_one, jnp.bfloat16)
    vector_one, modulation_one = vector_sums(sums_one, sums_mid, sums_two, d_bias_qkv, d_bias_one)

    def finish_mlp(totals):
        total = totals[0]
        ones = jnp.concatenate(
            [x[:split].astype(jnp.bfloat16).reshape(n_dp, room, -1) for x in (total, d_mlp_one)],
            axis=1,
        )
        (joined,) = run(
            functools.partial(join_kernel, half, n_seq, room),
            [exchange(ones, "x")],
            [f32(2, rows, FF)],
        )
        owned["one"] = joined.reshape(2, -1)
        owned["two"] = jnp.stack([total[split:], d_mlp_one[split:].astype(jnp.float32)]).reshape(2, -1)

    def finish_attention(totals):
        pair = (totals[0], owned["attention later"][0])
        both = jnp.concatenate(
            [x[:split].astype(jnp.bfloat16).reshape(n_dp, room, -1) for x in pair], axis=1
        )
        both = exchange(both, "y").reshape(n_dp, 2, room, packed_width)[:, :, :rows]
        values = both[..., :wide].reshape(n_dp, 2, rows, n_seq, out_room)[..., :rows]
        joined = jnp.stack(
            [
                both[..., wide : wide + width],
                both[..., wide + narrow : wide + narrow + width],
                values.reshape(n_dp, 2, rows, width),
            ]
        )
        owned["qkv"] = joined.transpose(2, 3, 0, 1, 4).astype(jnp.float32).reshape(2, -1)
        owned["out"] = jnp.stack(
            [x[split : split + rows].astype(jnp.float32) for x in pair]
        ).reshape(2, -1)

    grad_frames, ring = lax.optimization_barrier((regroup(grad), ring))
    lane.add(*ring, "x", (2, 2), keep("attention later"))
    d_end, sums_two = opened_back(0, grad_frames, end_zero)
    d_end = lane.tick(gather_four(d_end, "x"))
    d_inner, d_bias_one, *partial = mlp_back(d_end, mlp_zero, two_zero, 0, slope_zero)
    partial = lane.tick(partial)
    (ring,) = factor(
        [([(inside_zero, [d_inner], split), ([active_zero], d_end, half)], "y")]
    )
    lane.add(*ring, "y", (1, 1), finish_mlp)
    own = lane.tick(scatter_four(partial, "x"))
    d_branch, grad_mid, sums_mid = middle_back(0, own, grad_frames, middle_zero, branch_zero)
    d_branch = lane.tick(gather_four(d_branch, "y"))
    d_packed, d_bias_qkv, *partial = attention_back(
        0, d_branch, attention_zero, packed_zero, probs_zero
    )
    partial = lane.tick(partial)
    (ring,) = factor(
        [([(hidden_zero, [d_packed], split), ([mixed_zero], d_branch, out_room)], "x")]
    )
    lane.add(*ring, "x", (1, 1), finish_attention)
    lane.extra.append((ring, d_mlp_one))
    own = scatter_four(partial, "y")
    lane.tick(())
    own = lane.tick(own)
    d_tokens, sums_one = closed_back(0, own, grad_mid, x_zero, jnp.float32)
    vector_zero, modulation_zero = vector_sums(sums_one, sums_mid, sums_two, d_bias_qkv, d_bias_one)

    lane.scripts += [
        [scatter_vectors(jnp.concatenate([vector_zero, vector_one]), n_dp, n_seq, keep("vectors")), None],
        [sum_seq(modulation_zero + modulation_one, keep("cond")), None],
    ]
    while lane.jobs or lane.scripts:
        lane.tick(())
    return (
        output.reshape(tokens.shape),
        d_tokens.reshape(tokens.shape),
        owned["cond"][None],
        *[owned[name] for name in ("qkv", "out", "one", "two")],
        owned["vectors"],
    )


def on_device(tokens, cond, d_out, attn_in, attn_out, mlp_in, mlp_out, vectors):
    shards = (attn_in, attn_out, mlp_in, mlp_out, vectors)
    widths = (
        attn_in.shape[1],
        attn_out.shape[1],
        mlp_in.shape[1],
        mlp_out.shape[1],
        vectors.shape[1],
    )
    layer_zero = unpack(fetch_forward(shards, 0))
    spatial_out, stored_zero = layer_forward(tokens.astype(jnp.float32), cond, layer_zero, False)
    by_place = lax.all_to_all(
        spatial_out.astype(jnp.bfloat16), "seq", split_axis=2, concat_axis=1, tiled=True
    ).astype(spatial_out.dtype)
    layer_one = unpack(fetch_forward(shards, 1))
    temporal_out, stored_one = layer_forward(by_place, cond, layer_one, True)
    output = lax.all_to_all(
        temporal_out.astype(jnp.bfloat16), "seq", split_axis=1, concat_axis=2, tiled=True
    ).astype(temporal_out.dtype)
    grad_places = lax.all_to_all(d_out, "seq", split_axis=2, concat_axis=1, tiled=True).astype(
        jnp.float32
    )
    grad_mid, factors_one, modul_one = layer_backward(grad_places, stored_one, layer_one, True)
    owned_one = reduce_grads(factors_one, widths)
    grad_frames = lax.all_to_all(
        grad_mid.astype(jnp.bfloat16), "seq", split_axis=1, concat_axis=2, tiled=True
    ).astype(grad_mid.dtype)
    d_tokens, factors_zero, modul_zero = layer_backward(grad_frames, stored_zero, layer_zero, False)
    owned_zero = reduce_grads(factors_zero, widths)
    d_cond = lax.psum(modul_zero + modul_one, "seq")
    stacked = tuple((jnp.stack([former, latter]) for former, latter in zip(owned_zero, owned_one)))
    return (output, d_tokens, d_cond, stacked[0], stacked[1], stacked[2], stacked[3], stacked[4])


def solution(mesh):
    n_dp, n_seq = mesh.shape["dp"], mesh.shape["seq"]
    split = n_dp == 4 and n_seq == 8
    clips, frames = "dp", "seq"
    if split:
        devices = mesh.devices.reshape(n_dp // 2, 2, n_seq // 2, 2)
        mesh = jax.sharding.Mesh(devices, ("y", "core", "z", "x"))
        clips, frames = ("y", "core"), ("z", "x")
    everyone = P(None, ("y", "core", "z", "x") if split else ("dp", "seq"))
    tokens, cond = P(clips, frames, None, None), P(clips, None, None)
    return jax.shard_map(
        on_device_split if split else on_device,
        mesh=mesh,
        in_specs=(tokens, cond, tokens) + (everyone,) * 5,
        out_specs=(tokens, tokens, cond) + (everyone,) * 5,
        check_vma=False,
    )
```

```python
import functools

import jax
import jax.numpy as jnp
from jax import lax
from jax.experimental import pallas as pl
from jax.experimental.pallas import tpu as pltpu
from jax.sharding import PartitionSpec as P

D = 1152
HEADS = 16
HEAD_DIM = 72
FF = 4608


EPSILON = 1e-06


def as_sent(x):

    def short(part):
        return part.astype(jnp.bfloat16) if part.dtype == jnp.float32 else part

    return jax.tree.map(short, x)


def modulate(tokens, scale, shift):
    average = jnp.mean(tokens, axis=-1, keepdims=True)
    centred = tokens - average
    variance = jnp.mean(centred * centred, axis=-1, keepdims=True)
    return centred * lax.rsqrt(variance + EPSILON) * (1.0 + scale) + shift


def plain_dot(former, latter):
    return jnp.dot(former, latter, preferred_element_type=jnp.float32)


def left_dot(former, latter):
    return lax.dot_general(
        former, latter, (((0,), (0,)), ((), ())), preferred_element_type=jnp.float32
    )


def right_dot(former, latter):
    return lax.dot_general(
        former, latter, (((1,), (1,)), ((), ())), preferred_element_type=jnp.float32
    )


def contract(form, former, latter):
    return jnp.einsum(form, former, latter, preferred_element_type=jnp.float32)


def einsum_forms(temporal):
    if temporal:
        return ("aibhe,ajbhe->abhij", "abhij,ajbhe->aibhe", "abhij,aibhe->ajbhe")
    return ("abihe,abjhe->abhij", "abhij,abjhe->abihe", "abhij,abihe->abjhe")


def unpack(pieces):
    attn_in, attn_out, mlp_in, mlp_out, vector = pieces
    vector = vector.astype(jnp.float32)
    return (
        attn_in.reshape(D, 3 * D),
        attn_out.reshape(D, D),
        mlp_in.reshape(D, FF),
        mlp_out.reshape(FF, D),
        vector[0:D],
        vector[D : 2 * D],
        vector[2 * D : 3 * D],
        vector[3 * D : 3 * D + FF],
        vector[3 * D + FF : 4 * D + FF],
        vector[4 * D + FF :].reshape(6, D),
    )


def tuple_of(shards, layer_index):
    return (
        shards[0][layer_index],
        shards[1][layer_index],
        shards[2][layer_index],
        shards[3][layer_index],
        shards[4][layer_index],
    )


def fetch_forward(shards, layer_index):
    return lax.all_gather(as_sent(tuple_of(shards, layer_index)), ("dp", "seq"), axis=0, tiled=True)


def piece_of(left, right):
    product = left_dot(left, right).reshape(-1)
    return product


def reduce_grads(factors, widths):
    (
        hidden,
        d_packed,
        attended,
        d_branch_one,
        hidden_two,
        d_inner,
        active,
        d_branch_two,
        d_vector,
    ) = factors
    pairs = (
        (hidden, d_packed),
        (attended, d_branch_one),
        (hidden_two, d_inner),
        (active, d_branch_two),
    )
    block = sum(widths)
    blocks_here = lax.axis_size(("dp", "seq")) * block // block
    members = []
    for (left, right), term_width in zip(pairs, widths[:4]):
        piece = piece_of(left, right)
        members.append(piece.reshape(blocks_here, term_width))
    members.append(d_vector.reshape(blocks_here, widths[4]))
    owned = lax.psum_scatter(
        jnp.concatenate(members, axis=1).reshape(-1), ("dp", "seq"), scatter_dimension=0, tiled=True
    )
    results = []
    position = 0
    for width in widths:
        results.append(owned[position : position + width])
        position = position + width
    return tuple(results)


def mod_rows(modulation):
    return [modulation[:, number][:, None, None, :] for number in range(6)]


def layer_forward(tokens, cond, weight_set, temporal):
    w_qkv, w_out, w_one, w_two, bias_q, bias_v, bias_o, bias_one, bias_two, table = weight_set
    modulation = table[None] + cond
    rows_mod = mod_rows(modulation)
    leading = tokens.shape[:-1]
    head_shape = leading + (HEADS, HEAD_DIM)
    hidden = modulate(tokens, rows_mod[1], rows_mod[0]).astype(jnp.bfloat16).reshape(-1, D)
    packed = plain_dot(hidden, w_qkv)
    queries = (packed[:, :D] + bias_q).astype(jnp.bfloat16).reshape(head_shape)
    key_heads = packed[:, D : 2 * D].astype(jnp.bfloat16).reshape(head_shape)
    values = (packed[:, 2 * D :] + bias_v).astype(jnp.bfloat16).reshape(head_shape)
    score_form, mix_form, back_form = einsum_forms(temporal)
    scores = contract(score_form, queries, key_heads) * HEAD_DIM ** (-0.5)
    row_peak = jnp.max(scores, axis=-1, keepdims=True)
    exponent = jnp.exp(scores - row_peak)
    row_total = jnp.sum(exponent, axis=-1, keepdims=True)
    weights_soft = exponent / row_total
    log_total = row_peak + jnp.log(row_total)
    attended = (
        contract(mix_form, weights_soft.astype(jnp.bfloat16), values)
        .astype(jnp.bfloat16)
        .reshape(-1, D)
    )
    branch_one = (plain_dot(attended, w_out) + bias_o).reshape(leading + (D,))
    middle = tokens + rows_mod[2] * branch_one
    hidden_two = modulate(middle, rows_mod[4], rows_mod[3]).astype(jnp.bfloat16).reshape(-1, D)
    inner_sum = plain_dot(hidden_two, w_one) + bias_one
    active = jax.nn.gelu(inner_sum, approximate=True).astype(jnp.bfloat16)
    branch_two = (plain_dot(active, w_two) + bias_two).reshape(leading + (D,))
    result = middle + rows_mod[5] * branch_two
    stored = (
        tokens,
        modulation,
        hidden,
        queries,
        key_heads,
        values,
        log_total,
        attended,
        branch_one,
        middle,
        hidden_two,
        inner_sum,
        active,
        branch_two,
    )
    return (result, stored)


def layer_backward(grad_out, stored, weight_set, temporal):
    w_qkv, w_out, w_one, w_two = (weight_set[0], weight_set[1], weight_set[2], weight_set[3])
    (
        tokens,
        modulation,
        hidden,
        queries,
        key_heads,
        values,
        log_total,
        attended,
        branch_one,
        middle,
        hidden_two,
        inner_sum,
        active,
        branch_two,
    ) = stored
    rows_mod = mod_rows(modulation)
    leading = tokens.shape[:-1]
    clips_here = tokens.shape[0]
    d_gate_two = jnp.sum(grad_out * branch_two, axis=(1, 2))
    d_branch_two = (rows_mod[5] * grad_out).astype(jnp.bfloat16).reshape(-1, D)
    d_bias_two = jnp.sum(d_branch_two, axis=0, dtype=jnp.float32)
    d_active = right_dot(d_branch_two, w_two)
    unused_gelu, gelu_back = jax.vjp(
        lambda entries: jax.nn.gelu(entries, approximate=True), inner_sum
    )
    d_inner = gelu_back(d_active)[0].astype(jnp.bfloat16)
    d_bias_one = jnp.sum(d_inner, axis=0, dtype=jnp.float32)
    d_hidden_two = right_dot(d_inner, w_one).reshape(leading + (D,))
    unused_norm, norm_back = jax.vjp(modulate, middle, rows_mod[4], rows_mod[3])
    d_middle, d_scale_two, d_shift_two = norm_back(d_hidden_two)
    grad_mid = grad_out + d_middle
    d_gate_one = jnp.sum(grad_mid * branch_one, axis=(1, 2))
    d_branch_one = (rows_mod[2] * grad_mid).astype(jnp.bfloat16).reshape(-1, D)
    d_bias_o = jnp.sum(d_branch_one, axis=0, dtype=jnp.float32)
    d_attended = (
        right_dot(d_branch_one, w_out).astype(jnp.bfloat16).reshape(leading + (HEADS, HEAD_DIM))
    )
    score_form, mix_form, back_form = einsum_forms(temporal)
    scale_qk = HEAD_DIM ** (-0.5)
    scores = contract(score_form, queries, key_heads) * scale_qk
    weights_soft = jnp.exp(scores - log_total)
    d_values = contract(back_form, weights_soft.astype(jnp.bfloat16), d_attended)
    d_probs = contract(score_form, d_attended, values)
    d_scores = weights_soft * (d_probs - jnp.sum(weights_soft * d_probs, axis=-1, keepdims=True))
    d_scores = d_scores.astype(jnp.bfloat16)
    d_queries = contract(mix_form, d_scores, key_heads) * scale_qk
    d_keys = contract(back_form, d_scores, queries) * scale_qk
    d_packed = jnp.concatenate(
        [
            d_queries.reshape(-1, D).astype(jnp.bfloat16),
            d_keys.reshape(-1, D).astype(jnp.bfloat16),
            d_values.reshape(-1, D).astype(jnp.bfloat16),
        ],
        axis=1,
    )
    d_bias_q = jnp.sum(d_packed[:, :D], axis=0, dtype=jnp.float32)
    d_bias_v = jnp.sum(d_packed[:, 2 * D :], axis=0, dtype=jnp.float32)
    d_hidden = right_dot(d_packed, w_qkv).reshape(leading + (D,))
    unused_first, first_back = jax.vjp(modulate, tokens, rows_mod[1], rows_mod[0])
    d_input, d_scale_one, d_shift_one = first_back(d_hidden)
    d_input = grad_mid + d_input
    d_modulation = jnp.stack(
        [
            d_shift_one.reshape(clips_here, D),
            d_scale_one.reshape(clips_here, D),
            d_gate_one,
            d_shift_two.reshape(clips_here, D),
            d_scale_two.reshape(clips_here, D),
            d_gate_two,
        ],
        axis=1,
    )
    d_vector = jnp.concatenate(
        [
            d_bias_q,
            d_bias_v,
            d_bias_o,
            d_bias_one,
            d_bias_two,
            jnp.sum(d_modulation, axis=0).reshape(-1),
        ]
    )
    factors = (
        hidden,
        d_packed,
        attended,
        d_branch_one,
        hidden_two,
        d_inner,
        active,
        d_branch_two,
        d_vector,
    )
    return (d_input, factors, d_modulation)


SHIFTS = (1, 2, 3)
SMALL_BYTES, LARGE_BYTES = 14 * 2**20, 24 * 2**20
STRIP = 384


def swap(x, axis):
    return lax.ppermute(x, axis, [(0, 1), (1, 0)])


def shift_z(x, k):
    n = lax.axis_size("z")
    return lax.ppermute(x, "z", [(i, (i + k) % n) for i in range(n)])


def gather_four(x, axis):
    far = swap(x, axis)
    return [x, swap(x, "core"), far, swap(far, "core")]


def scatter_four(partial, axis):
    kept_own, kept_far, sent = partial
    got = swap(sent, "core")
    far = (kept_far + got[1].astype(jnp.float32)).astype(jnp.bfloat16)
    return kept_own, got, swap(far, axis)


def source_of(number, side):
    z, here = lax.axis_index("z"), lax.axis_index(side)
    return 2 * ((z - number % 4 + 4) % 4) + (here + number // 4) % 2


def target_of(number, side):
    z, here = lax.axis_index("z"), lax.axis_index(side)
    return 2 * ((z + number % 4) % 4) + (here + number // 4) % 2


def padded(count, unit):
    return -(-count // unit) * unit


def whole():
    return pl.BlockSpec(memory_space=pltpu.VMEM)


def anywhere():
    return pl.BlockSpec(memory_space=pltpu.HBM)


def run(kernel, ins, outs, specs=None, scratch=(), flops=0):
    moved = sum(x.size * x.dtype.itemsize for x in list(ins) + list(outs))
    if specs:
        far = [spec.memory_space == pltpu.HBM for spec in specs]
        ins = [
            pltpu.with_memory_space_constraint(x, pltpu.HBM) if away else x for x, away in zip(ins, far)
        ]
    return pl.pallas_call(
        kernel,
        out_shape=tuple(outs),
        in_specs=specs or [whole()] * len(ins),
        out_specs=tuple([whole()] * len(outs)),
        scratch_shapes=list(scratch),
        compiler_params=pltpu.CompilerParams(vmem_limit_bytes=LARGE_BYTES if scratch else SMALL_BYTES),
        cost_estimate=pl.CostEstimate(flops=flops, bytes_accessed=moved, transcendentals=0),
    )(*ins)


def f32(*shape):
    return jax.ShapeDtypeStruct(shape, jnp.float32)


def bf16(*shape):
    return jax.ShapeDtypeStruct(shape, jnp.bfloat16)


def normal_parts(x):
    average = jnp.mean(x, axis=-1, keepdims=True)
    centred = x - average
    variance = jnp.mean(centred * centred, axis=-1, keepdims=True)
    inverse = lax.rsqrt(variance + EPSILON)
    return centred * inverse, inverse


def modulated(x, modulation, scale_row, order):
    normal, _ = normal_parts(x)
    scale = modulation[scale_row : scale_row + 1]
    shift = modulation[scale_row - 1 : scale_row]
    hidden = (normal * (1.0 + scale) + shift).astype(jnp.bfloat16)
    return plain_dot(hidden, order).astype(jnp.bfloat16)


def enter_kernel(x_ref, modulation_ref, order_ref, hidden_ref):
    x = x_ref[...].astype(jnp.float32)
    hidden_ref[...] = modulated(x, modulation_ref[...], 1, order_ref[...])


def summed(own_ref, got_ref, far_ref):
    return own_ref[...] + got_ref[0].astype(jnp.float32) + far_ref[...].astype(jnp.float32)


def middle_kernel(
    own_ref, got_ref, far_ref, bias_ref, x_ref, modulation_ref, order_ref, branch_ref, middle_ref, hidden_ref
):
    branch = summed(own_ref, got_ref, far_ref) + bias_ref[...]
    modulation = modulation_ref[...]
    middle = x_ref[...].astype(jnp.float32) + modulation[2:3] * branch
    branch_ref[...] = branch
    middle_ref[...] = middle
    hidden_ref[...] = modulated(middle, modulation, 4, order_ref[...])


def leave_kernel(own_ref, got_ref, far_ref, bias_ref, middle_ref, modulation_ref, branch_ref, result_ref):
    branch = summed(own_ref, got_ref, far_ref) + bias_ref[...]
    branch_ref[...] = branch
    result_ref[...] = (middle_ref[...] + modulation_ref[5:6] * branch).astype(jnp.bfloat16)


def start_rows(pieces, buffer, sems, first):
    copies = []
    for number, piece in enumerate(pieces):
        rows = piece.shape[0]
        copies.append(
            pltpu.make_async_copy(piece, buffer.at[pl.ds(number * rows, rows)], sems.at[first + number])
        )
        copies[-1].start()
    return copies


def start_weights(pieces, side, at, rows, buffer, sems, first):
    if len(pieces) == 1:
        found = [(pieces[0].at[number], number) for number in range(8)]
    else:
        found = [(piece, source_of(number, side)) for number, piece in enumerate(pieces)]
    copies = []
    for number, (piece, source) in enumerate(found):
        target = pl.multiple_of(source * rows, 16)
        copies.append(
            pltpu.make_async_copy(
                piece.at[pl.ds(at, rows)], buffer.at[pl.ds(target, rows)], sems.at[first + number]
            )
        )
        copies[-1].start()
    return copies


def wait_all(copies):
    for copy in copies:
        copy.wait()


def strips(size):
    return [(at, min(STRIP, size - at)) for at in range(0, size, STRIP)]


def deal(product, at, width, own_ref, far_ref, sent_ref):
    count = own_ref.shape[0]
    columns = slice(at, at + width)
    own_ref[:, columns] = product[:count]
    sent_ref[0, :, columns] = product[count : 2 * count].astype(jnp.bfloat16)
    far_ref[:, columns] = product[2 * count : 3 * count]
    sent_ref[1, :, columns] = product[3 * count :].astype(jnp.bfloat16)


def softmax_of(scores, count, period):
    if period:
        row = lax.broadcasted_iota(jnp.int32, scores.shape, 0) % period
        column = lax.broadcasted_iota(jnp.int32, scores.shape, 1) % period
        scores = jnp.where(row == column, scores, -1e30)
    exponent = jnp.exp(scores - jnp.max(scores, axis=-1, keepdims=True))
    return exponent * (1.0 / jnp.sum(exponent, axis=-1, keepdims=True))


def owners(width, per_head):
    return lax.broadcasted_iota(jnp.int32, (1, width), 1) // per_head


def by_head(x, owner, heads):
    return jnp.concatenate([jnp.where(owner == head, x, 0) for head in range(heads)], axis=0)


def of_head(stacked, owner, heads, count):
    chosen = stacked[:count]
    for head in range(1, heads):
        chosen = jnp.where(owner == head, stacked[head * count : (head + 1) * count], chosen)
    return chosen


def attention_kernel(period, heads, split, n_pieces, *refs):
    hidden, pieces, refs = refs[:4], refs[4 : 4 + n_pieces], refs[4 + n_pieces :]
    bias_ref, packed_ref, mixed_ref, probs_ref, own_ref, far_ref, sent_ref, left, qkv, out, sems = refs
    copies = start_rows(hidden, left, sems, 0)
    copies += start_weights(pieces, "x", 0, split, qkv, sems, 4)
    later = start_weights(pieces, "x", split, out.shape[0] // 8, out, sems, 12)
    wide = out.shape[0]
    narrow = (qkv.shape[1] - wide) // 2
    count = own_ref.shape[0]
    narrow_owner, wide_owner = owners(narrow, HEAD_DIM), owners(wide, wide // heads)
    wait_all(copies)
    for at, size in strips(qkv.shape[1]):
        product = plain_dot(left[...], qkv[:, at : at + size]) + bias_ref[:, at : at + size]
        packed_ref[:, at : at + size] = product.astype(jnp.bfloat16)
    for number in range(4):
        rows = pl.ds(number * count, count)
        packed = packed_ref[rows, :]
        values = packed[:, :wide]
        queries = by_head(packed[:, wide : wide + narrow], narrow_owner, heads)
        scores = right_dot(queries, packed[:, wide + narrow :]) * HEAD_DIM ** (-0.5)
        weights_soft = softmax_of(scores, count, period)
        probs_ref[pl.ds(number * heads * count, heads * count), :] = weights_soft
        mixed = plain_dot(weights_soft.astype(jnp.bfloat16), values)
        mixed_ref[rows, :] = of_head(mixed, wide_owner, heads, count).astype(jnp.bfloat16)
    wait_all(later)
    for at, size in strips(out.shape[1]):
        deal(plain_dot(mixed_ref[...], out[:, at : at + size]), at, size, own_ref, far_ref, sent_ref)


def attention_back_kernel(heads, split, n_pieces, *refs):
    d_branch, pieces, refs = refs[:4], refs[4 : 4 + n_pieces], refs[4 + n_pieces :]
    packed_ref, probs_ref, d_packed_ref, sums_ref, own_ref, far_ref, sent_ref, left, qkv, out, sems = refs
    copies = start_rows(d_branch, left, sems, 0)
    copies += start_weights(pieces, "x", split, out.shape[0] // 8, out, sems, 4)
    later = start_weights(pieces, "x", 0, split, qkv, sems, 12)
    wide = out.shape[0]
    narrow = (qkv.shape[1] - wide) // 2
    count = own_ref.shape[0]
    scale = HEAD_DIM ** (-0.5)
    narrow_owner, wide_owner = owners(narrow, HEAD_DIM), owners(wide, wide // heads)
    sums = jnp.zeros((1, wide + 2 * narrow), jnp.float32)
    wait_all(copies)
    d_mixed_all = right_dot(left[...], out[...]).astype(jnp.bfloat16)
    for number in range(4):
        rows = pl.ds(number * count, count)
        d_mixed = by_head(d_mixed_all[number * count : (number + 1) * count], wide_owner, heads)
        packed = packed_ref[rows, :]
        queries = by_head(packed[:, wide : wide + narrow], narrow_owner, heads)
        weights_soft = probs_ref[pl.ds(number * heads * count, heads * count), :]
        d_probs = right_dot(d_mixed, packed[:, :wide])
        inner = jnp.sum(weights_soft * d_probs, axis=-1, keepdims=True)
        d_scores = (weights_soft * (d_probs - inner)).astype(jnp.bfloat16)
        d_values = left_dot(weights_soft.astype(jnp.bfloat16), d_mixed)
        d_keys = left_dot(d_scores, queries)
        d_queries = of_head(
            plain_dot(d_scores, packed[:, wide + narrow :]), narrow_owner, heads, count
        )
        d_packed = jnp.concatenate([d_values, d_queries * scale, d_keys * scale], axis=1)
        d_packed = d_packed.astype(jnp.bfloat16)
        d_packed_ref[rows, :] = d_packed
        sums = sums + jnp.sum(d_packed.astype(jnp.float32), axis=0, keepdims=True)
    sums_ref[...] = sums
    wait_all(later)
    for at, size in strips(qkv.shape[0]):
        product = right_dot(d_packed_ref[...], qkv[at : at + size, :])
        deal(product, at, size, own_ref, far_ref, sent_ref)


def gelu_pair(u):
    inner = 0.7978845608028654 * (u + 0.044715 * u * u * u)
    bent = jnp.tanh(inner)
    value = 0.5 * u * (1.0 + bent)
    slope = 0.5 * (1.0 + bent) + 0.5 * u * (1.0 - bent * bent) * (
        0.7978845608028654 * (1.0 + 3 * 0.044715 * u * u)
    )
    return value, slope


def mlp_kernel(split, at_two, n_one, n_two, *refs):
    refs = list(refs)
    hidden, refs = refs[:4], refs[4:]
    pieces, refs = refs[:n_one], refs[n_one:]
    pieces_two, refs = refs[:n_two], refs[n_two:]
    bias_ref, active_ref, slope_ref, own_ref, far_ref, sent_ref, left, one, two, sems = refs
    copies = start_rows(hidden, left, sems, 0)
    copies += start_weights(pieces, "y", 0, split, one, sems, 4)
    later = start_weights(pieces_two, "y", at_two, two.shape[0] // 8, two, sems, 12)
    wait_all(copies)
    for at, size in strips(one.shape[1]):
        columns = slice(at, at + size)
        u = plain_dot(left[...], one[:, columns]) + bias_ref[:, columns]
        value, slope = gelu_pair(u)
        active_ref[:, columns] = value.astype(jnp.bfloat16)
        slope_ref[:, columns] = slope.astype(jnp.bfloat16)
    wait_all(later)
    for at, size in strips(two.shape[1]):
        deal(plain_dot(active_ref[...], two[:, at : at + size]), at, size, own_ref, far_ref, sent_ref)


def mlp_back_kernel(split, at_two, n_one, n_two, *refs):
    refs = list(refs)
    d_branch, refs = refs[:4], refs[4:]
    pieces, refs = refs[:n_one], refs[n_one:]
    pieces_two, refs = refs[:n_two], refs[n_two:]
    slope_ref, d_inner_ref, sums_ref, own_ref, far_ref, sent_ref, left, one, two, sems = refs
    copies = start_rows(d_branch, left, sems, 0)
    copies += start_weights(pieces_two, "y", at_two, two.shape[0] // 8, two, sems, 4)
    later = start_weights(pieces, "y", 0, split, one, sems, 12)
    wait_all(copies)
    for at, size in strips(two.shape[0]):
        columns = slice(at, at + size)
        d_active = right_dot(left[...], two[columns, :])
        d_inner = (d_active * slope_ref[:, columns].astype(jnp.float32)).astype(jnp.bfloat16)
        d_inner_ref[:, columns] = d_inner
        sums_ref[:, columns] = jnp.sum(d_inner.astype(jnp.float32), axis=0, keepdims=True)
    wait_all(later)
    for at, size in strips(one.shape[0]):
        product = right_dot(d_inner_ref[...], one[at : at + size, :])
        deal(product, at, size, own_ref, far_ref, sent_ref)


def total_sums(ref, *members):
    rows = [jnp.sum(m.astype(jnp.float32), axis=0, keepdims=True) for m in members]
    ref[...] = jnp.concatenate(rows, axis=0)


def open_back_kernel(grad_ref, branch_ref, modulation_ref, d_branch_ref, sums_ref):
    grad = grad_ref[...].astype(jnp.float32)
    d_branch = (modulation_ref[5:6] * grad).astype(jnp.bfloat16)
    d_branch_ref[...] = d_branch
    total_sums(sums_ref, grad * branch_ref[...], d_branch)


def natural(total, order):
    high = total.astype(jnp.bfloat16)
    low = (total - high.astype(jnp.float32)).astype(jnp.bfloat16)
    both = right_dot(jnp.concatenate([high, low], axis=0), order)
    return both[: total.shape[0]] + both[total.shape[0] :]


def norm_back(d_hidden, x, scale):
    normal, inverse = normal_parts(x)
    entry = d_hidden * (1.0 + scale)
    average = jnp.mean(entry, axis=-1, keepdims=True)
    along = jnp.mean(entry * normal, axis=-1, keepdims=True)
    return (entry - average - normal * along) * inverse, d_hidden * normal


def middle_back_kernel(
    own_ref, got_ref, far_ref, grad_ref, x_ref, branch_ref, modulation_ref, order_ref, d_branch_ref, grad_mid_ref, sums_ref
):
    d_hidden = natural(summed(own_ref, got_ref, far_ref), order_ref[...])
    modulation = modulation_ref[...]
    d_x, d_scale = norm_back(d_hidden, x_ref[...], modulation[4:5])
    grad_mid = grad_ref[...].astype(jnp.float32) + d_x
    grad_mid_ref[...] = grad_mid
    d_branch = (modulation[2:3] * grad_mid).astype(jnp.bfloat16)
    d_branch_ref[...] = d_branch
    total_sums(sums_ref, d_hidden, d_scale, grad_mid * branch_ref[...], d_branch)


def close_back_kernel(own_ref, got_ref, far_ref, grad_ref, x_ref, modulation_ref, order_ref, d_x_ref, sums_ref):
    d_hidden = natural(summed(own_ref, got_ref, far_ref), order_ref[...])
    d_x, d_scale = norm_back(d_hidden, x_ref[...].astype(jnp.float32), modulation_ref[1:2])
    d_x_ref[...] = (grad_ref[...] + d_x).astype(d_x_ref.dtype)
    total_sums(sums_ref, d_hidden, d_scale)


def factor(groups):
    pairs = [pair for members, _ in groups for pair in members]
    ins, scratch, flops = [], [], 0
    for left, right, height in pairs:
        ins += left + right
        count = sum(piece.shape[0] for piece in left)
        scratch.append(pltpu.VMEM((left[0].shape[1], count), jnp.bfloat16))
        if len(right) > 1:
            scratch.append(pltpu.VMEM((count, right[0].shape[1]), jnp.bfloat16))
        flops += 2 * count * left[0].shape[1] * right[0].shape[1]
    outs = []
    for members, side in groups:
        height, width = sum(m[2] for m in members), members[0][1][0].shape[1]
        outs += [bf16(height, width) for _ in range(8)] if side else [bf16(8 * height, width)]

    def kernel(*refs):
        refs = iter(refs)
        taken = [
            ([next(refs) for _ in left], [next(refs) for _ in right], height)
            for left, right, height in pairs
        ]
        results = [next(refs) for _ in outs]
        ready = []
        for left, right, height in taken:
            flip = next(refs)
            at = 0
            for piece in left:
                flip[:, at : at + piece.shape[0]] = piece[...].T
                at += piece.shape[0]
            lay = right[0]
            if len(right) > 1:
                lay = next(refs)
                at = 0
                for piece in right:
                    lay[at : at + piece.shape[0], :] = piece[...]
                    at += piece.shape[0]
            ready.append((flip, lay, height))
        for members, side in groups:
            mine, ready = ready[: len(members)], ready[len(members) :]
            total = sum(member[2] for member in mine)
            for number in range(8):
                at = 0 if side else number * total
                result = results[number] if side else results[0]
                target = target_of(number, side) if side else number
                for flip, lay, height in mine:
                    rows = pl.ds(pl.multiple_of(target * height, 16), height)
                    product = plain_dot(flip[rows, :], lay[...])
                    result[at : at + height, :] = product.astype(jnp.bfloat16)
                    at += height
            results = results[8:] if side else results[1:]

    results = list(run(kernel, ins, outs, scratch=scratch, flops=flops))
    given = []
    for _, side in groups:
        if side:
            given.append((results[:4], results[4:8]))
        else:
            given.append(results[0])
        results = results[8:] if side else results[1:]
    return given


def placed_blocks(half, n_seq):
    for owner in range(4 * n_seq):
        y, core, z, x = owner // (2 * n_seq), (owner // n_seq) % 2, (owner % n_seq) // 2, owner % 2
        yield owner * half, 2 * x + core, (2 * z + y) * half


def part_kernel(half, n_seq, rows_ref, parts_ref):
    rows = rows_ref.shape[1]
    for layer in range(2):
        for at, part, place in placed_blocks(half, n_seq):
            parts_ref[part, layer, 0:rows, place : place + half] = rows_ref[layer, :, at : at + half]


def join_kernel(half, n_seq, room, parts_ref, rows_ref):
    rows = rows_ref.shape[1]
    for layer in range(2):
        for at, part, place in placed_blocks(half, n_seq):
            block = parts_ref[part, layer * room : layer * room + rows, place : place + half]
            rows_ref[layer, :, at : at + half] = block.astype(jnp.float32)


def vector_kernel(
    n_seq, rows, sums_one_ref, sums_mid_ref, sums_two_ref, qkv_ref, one_ref, vector_ref, modulation_ref
):
    y, core, x = lax.axis_index("y"), lax.axis_index("core"), lax.axis_index("x")
    here = 2 * y + core
    room = padded(rows, 16)
    wide, width, half = n_seq * room, n_seq * rows, one_ref.shape[1] // n_seq
    for number in range(4):
        mine = here == number
        query = qkv_ref[:, wide : wide + width]
        vector_ref[:, number * width : (number + 1) * width] = jnp.where(mine, query, 0.0)
        for block in range(n_seq):
            at = D + number * width + block * rows
            value = qkv_ref[:, block * room : block * room + rows]
            vector_ref[:, at : at + rows] = jnp.where(mine, value, 0.0)
    for owner in range(4 * n_seq):
        mine = ((owner // n_seq) % 2 == core) & (owner % 2 == x)
        block = 2 * ((owner % n_seq) // 2) + owner // (2 * n_seq)
        at = 3 * D + owner * half
        vector_ref[:, at : at + half] = jnp.where(mine, one_ref[:, block * half : (block + 1) * half], 0.0)
    vector_ref[:, 2 * D : 3 * D] = sums_mid_ref[3:4]
    vector_ref[:, 3 * D + FF : 4 * D + FF] = sums_two_ref[1:2]
    members = (
        (sums_one_ref, 0),
        (sums_one_ref, 1),
        (sums_mid_ref, 2),
        (sums_mid_ref, 0),
        (sums_mid_ref, 1),
        (sums_two_ref, 0),
    )
    for number, (ref, row) in enumerate(members):
        at = (4 + number) * D + FF
        vector_ref[:, at : at + D] = ref[row : row + 1]
        modulation_ref[number : number + 1, :] = ref[row : row + 1]


def order_matrix(n_dp, n_seq, rows, room, crossed):
    place = lax.broadcasted_iota(jnp.int32, (D, n_dp * n_seq * room), 1)
    feature = lax.broadcasted_iota(jnp.int32, (D, n_dp * n_seq * room), 0)
    block, inner = place // room, place % room
    outer, local = block // n_dp, block % n_dp
    z, side, across, core = outer // 2, outer % 2, local // 2, local % 2
    x, y = (across, side) if crossed else (side, across)
    owner = (2 * y + core) * n_seq + 2 * z + x
    return ((feature == owner * rows + inner) & (inner < rows)).astype(jnp.bfloat16)


def grow(x, axis, size):
    pads = [(0, 0)] * x.ndim
    pads[axis] = (0, size - x.shape[axis])
    return jnp.pad(x, pads)


def exchange(parts, axis):
    return lax.all_to_all(parts, (axis, "core"), split_axis=0, concat_axis=0, tiled=True)


def spread(values, n_seq, rows, room):
    lead = values.shape[:-1]
    return grow(values.reshape(lead + (n_seq, rows)), len(lead) + 1, room).reshape(lead + (-1,))


def ordered_vectors(everyone, n_dp, n_seq, count):
    chosen = owner_rows(n_dp, n_seq, -1)
    ordered = left_dot(chosen.astype(jnp.bfloat16), everyone)
    return ordered.reshape(n_dp * n_seq, 2, count).transpose(1, 0, 2).reshape(2, -1)


def owner_rows(n_dp, n_seq, sign):
    count = n_dp * n_seq
    relative = lax.broadcasted_iota(jnp.int32, (count, count), 0)
    owner = lax.broadcasted_iota(jnp.int32, (count, count), 1)
    n_z = n_seq // 2
    z = (lax.axis_index("z") + sign * (relative // (2 * n_dp)) + n_z) % n_z
    x = lax.axis_index("x") ^ ((relative // n_dp) % 2)
    y = lax.axis_index("y") ^ ((relative // 2) % 2)
    core = lax.axis_index("core") ^ (relative % 2)
    source = (2 * y + core) * n_seq + 2 * z + x
    return (owner == source).astype(jnp.float32)


def scatter_vectors(sums, n_dp, n_seq, finish):
    count = sums.shape[1] // (n_dp * n_seq)
    rows = sums.reshape(2, n_dp * n_seq, count).transpose(1, 0, 2).reshape(n_dp * n_seq, -1)
    chosen = owner_rows(n_dp, n_seq, 1)
    rows = jnp.dot(chosen, rows, precision=lax.Precision.HIGHEST)
    quarters = jnp.split(rows, n_seq // 2)
    got = yield (quarters[0], [shift_z(quarters[k], k) for k in SHIFTS])
    total = got[0] + sum(got[1])
    got = yield (total, swap(total[n_dp:], "x"))
    total = got[0][:n_dp] + got[1]
    got = yield (total, swap(total[2:], "y"))
    total = got[0][:2] + got[1]
    got = yield (total, swap(total[1:], "core"))
    finish((got[0][:1] + got[1]).reshape(2, count))
    yield None


def sum_seq(x, finish):
    got = yield (x, swap(x, "x"))
    total = got[0] + got[1]
    got = yield (total, [shift_z(total, k) for k in SHIFTS])
    finish(got[0] + sum(got[1]))
    yield None


def slice_of(vector, n_dp):
    width = vector.shape[0] // n_dp
    here = 2 * lax.axis_index("y") + lax.axis_index("core")
    return lax.dynamic_slice(vector, (here * width,), (width,))


def crossed_slice(vector, n_z):
    blocks = vector.reshape(2, 2, n_z, 2, -1)
    blocks = lax.dynamic_index_in_dim(blocks, lax.axis_index("x"), 3, keepdims=False)
    blocks = lax.dynamic_index_in_dim(blocks, lax.axis_index("core"), 1, keepdims=False)
    return blocks.transpose(1, 0, 2).reshape(-1)


class Gather:
    def __init__(self, pieces, side, wait):
        self.side, self.wait = side, wait
        self.column, self.across, self.sent, self.waiting = [pieces], [], 0, False

    def wants_x(self):
        return self.sent < len(self.column)

    def send_x(self):
        self.sent += 1
        return [swap(piece, self.side) for piece in self.column[self.sent - 1]]

    def got_x(self, pieces):
        self.across.append(pieces)

    def wants_z(self):
        return len(self.column) < 4 and not self.waiting

    def send_z(self):
        self.waiting = True
        return [shift_z(piece, 1) for piece in self.column[-1]]

    def got_z(self, pieces):
        self.waiting = False
        self.column.append(pieces)

    def finished(self):
        return len(self.across) == 4

    def pieces(self, index):
        return [piece[index] for piece in self.column + self.across]


class Reduce:
    def __init__(self, mine, other, side, wait, finish):
        self.side, self.wait = side, wait
        self.mine, self.other, self.finish = mine, other, finish
        self.sent, self.got, self.hops, self.carried, self.result = 3, {}, 3, None, None

    def wants_x(self):
        return self.sent >= 0

    def send_x(self):
        self.sent -= 1
        return [swap(piece, self.side) for piece in self.other[self.sent + 1]]

    def got_x(self, pieces):
        self.got[3 - len(self.got)] = pieces

    def added(self, k):
        total = [m.astype(jnp.float32) + g.astype(jnp.float32) for m, g in zip(self.mine[k], self.got[k])]
        if k < 3:
            total = [t + c.astype(jnp.float32) for t, c in zip(total, self.carried)]
        return total

    def wants_z(self):
        ready = self.hops == 3 or self.carried is not None
        return self.hops > 0 and self.hops in self.got and ready

    def send_z(self):
        total = self.added(self.hops)
        self.hops -= 1
        self.carried = None
        return [shift_z(t.astype(jnp.bfloat16), 1) for t in total]

    def got_z(self, pieces):
        self.carried = pieces

    def finished(self):
        return self.hops == 0 and self.carried is not None and 0 in self.got


class Lane:
    def __init__(self):
        self.jobs, self.flight, self.extra, self.scripts = [], [], [], []

    def issue(self):
        for job in [job for job in self.jobs if isinstance(job, Reduce)]:
            if job.wants_x():
                self.flight.append((job.wait[0], job, "x", job.send_x()))
            if job.wants_z():
                self.flight.append((job.wait[1], job, "z", job.send_z()))
        for job in [job for job in self.jobs if isinstance(job, Gather)]:
            for kind, link in (("x", job.side), ("z", "z")):
                if getattr(job, "wants_" + kind)():
                    self.flight.append((job.wait, job, kind, getattr(job, "send_" + kind)()))
        for script in self.scripts:
            script[1] = script[0].send(script[1])
        self.scripts = [script for script in self.scripts if script[1] is not None]

    def add(self, mine, other, side, wait, finish):
        job = Reduce([[m] for m in mine], [[m] for m in other], side, wait, finish)
        self.jobs.append(job)
        self.flight.append((wait[0], job, "x", job.send_x()))

    def close(self):
        for job in [job for job in self.jobs if job.finished()]:
            self.jobs.remove(job)
            if isinstance(job, Reduce):
                job.finish(job.added(0))

    def tick(self, values):
        due = [f for f in self.flight if f[0] == 1]
        values, arrived, _, steps = lax.optimization_barrier(
            (values, [f[3] for f in due], self.extra, [script[1] for script in self.scripts])
        )
        for script, step in zip(self.scripts, steps):
            script[1] = step
        self.flight = [(f[0] - 1,) + f[1:] for f in self.flight if f[0] > 1]
        self.extra = []
        for (_, job, kind, _), pieces in zip(due, arrived):
            getattr(job, "got_" + kind)(pieces)
        self.close()
        self.issue()
        return values

    def until(self, job, values):
        while not job.finished():
            values = self.tick(values)
        return values


def on_device_split(tokens, cond, d_out, attn_in, attn_out, mlp_in, mlp_out, vectors):
    n_dp, n_seq = 4, 2 * lax.axis_size("z")
    heads = HEADS // n_dp
    width = heads * HEAD_DIM
    frames, places = tokens.shape[1] * n_seq, tokens.shape[2]
    periods = (0, places // n_seq)
    count = tokens.shape[1] * places
    group = n_dp * count
    rows = D // (n_dp * n_seq)
    room = rows
    out_room = padded(rows, 16)
    deep, wide = n_dp * n_seq * room, n_seq * out_room
    narrow = padded(width, 128)
    packed_width = wide + 2 * narrow
    inner = FF // n_dp
    split = n_dp * room
    half = inner // n_seq
    order = order_matrix(n_dp, n_seq, rows, room, False)
    order_mlp = order_matrix(n_dp, n_seq, rows, room, True)

    parts = attn_in.reshape(2, rows, 3, n_dp, width).transpose(2, 3, 0, 1, 4)
    qkv_parts = jnp.concatenate(
        [spread(parts[2], n_seq, rows, out_room), grow(parts[0], 3, narrow), grow(parts[1], 3, narrow)],
        axis=3,
    )
    qkv_parts = exchange(grow(qkv_parts, 2, room).reshape(n_dp, 2 * room, -1), "y")
    qkv_parts = qkv_parts.reshape(n_dp, 2, room, -1)
    out_parts = grow(attn_out.reshape(2, rows, D), 1, out_room)
    two_parts = mlp_out.reshape(2, half, D)

    def attention_piece(index):
        return jnp.concatenate([qkv_parts[:, index].reshape(split, -1), out_parts[index]])

    def regroup(x):
        x = x.reshape(n_seq, count // n_seq, D)
        return lax.all_to_all(x, ("z", "x"), split_axis=0, concat_axis=0, tiled=True).reshape(-1, D)

    lane = Lane()
    mine = vectors.reshape(1, -1)
    near = jnp.concatenate([mine, swap(mine, "core")])
    clips = jnp.concatenate([near, swap(near, "y")])
    pair = jnp.concatenate([clips, swap(clips, "x")])
    everyone = jnp.concatenate([pair] + [shift_z(pair, k) for k in SHIFTS])
    first = attention_piece(0)
    everyone, first, mlp_in, qkv_parts, out_parts, two_parts = lax.optimization_barrier(
        (everyone, first, mlp_in, qkv_parts, out_parts, two_parts)
    )
    mlp_in = mlp_in.reshape(2, rows, FF)
    attention_job = Gather([first], "x", 1)
    lane.jobs.append(attention_job)
    lane.issue()
    (one_parts,) = run(
        functools.partial(part_kernel, half, n_seq), [mlp_in], [bf16(n_dp, 2, room, inner)]
    )
    vector = ordered_vectors(everyone, n_dp, n_seq, vectors.shape[1])
    biases, modulations = [], []
    for index in range(2):
        v = vector[index]
        bias_q, bias_v = slice_of(v[0:D], n_dp), slice_of(v[D : 2 * D], n_dp)
        bias_q = grow(bias_q, 0, narrow)
        bias_v = spread(bias_v, n_seq, rows, out_room)
        biases.append(
            (
                jnp.concatenate([bias_v, bias_q, jnp.zeros_like(bias_q)])[None],
                v[None, 2 * D : 3 * D],
                crossed_slice(v[3 * D : 3 * D + FF], n_seq // 2)[None],
                v[None, 3 * D + FF : 4 * D + FF],
            )
        )
        modulations.append(v[4 * D + FF :].reshape(6, D) + cond[0])

    def scratch(left_width, *shapes):
        return [
            pltpu.VMEM((group, left_width), jnp.bfloat16),
            *[pltpu.VMEM(shape, jnp.bfloat16) for shape in shapes],
            pltpu.SemaphoreType.DMA((20,)),
        ]

    attention_rooms = ((deep, packed_width), (wide, D))
    mlp_rooms = ((deep, inner), (inner, D))
    attention_flops = 4 * group * (deep * packed_width + wide * D)
    mlp_flops = 2 * group * (deep + D) * inner
    own_shapes = [f32(count, D), f32(count, D), bf16(2, count, D)]
    deep_shapes = [f32(count, deep), f32(count, deep), bf16(2, count, deep)]

    def opened(x, index):
        return run(enter_kernel, [x, modulations[index], order], [bf16(count, deep)])[0]

    def attention(index, hidden, pieces):
        return run(
            functools.partial(attention_kernel, periods[index], heads, split, len(pieces)),
            hidden + pieces + [biases[index][0]],
            [bf16(group, packed_width), bf16(group, wide), f32(group * heads, count)] + own_shapes,
            specs=[anywhere()] * (4 + len(pieces)) + [whole()],
            scratch=scratch(deep, *attention_rooms),
            flops=attention_flops,
        )

    def attention_back(index, d_branch, pieces, packed, probs):
        return run(
            functools.partial(attention_back_kernel, heads, split, len(pieces)),
            d_branch + pieces + [packed, probs],
            [bf16(group, packed_width), f32(1, packed_width)] + deep_shapes,
            specs=[anywhere()] * (4 + len(pieces)) + [whole()] * 2,
            scratch=scratch(D, *attention_rooms),
            flops=attention_flops,
        )

    def middle(index, own, x):
        return run(
            middle_kernel,
            list(own) + [biases[index][1], x, modulations[index], order_mlp],
            [f32(count, D), f32(count, D), bf16(count, deep)],
        )

    def mlp(index, hidden, pieces, pieces_two, at):
        return run(
            functools.partial(mlp_kernel, split, at, len(pieces), len(pieces_two)),
            hidden + pieces + pieces_two + [biases[index][2]],
            [bf16(group, inner), bf16(group, inner)] + own_shapes,
            specs=[anywhere()] * (4 + len(pieces) + len(pieces_two)) + [whole()],
            scratch=scratch(deep, *mlp_rooms),
            flops=mlp_flops,
        )

    def mlp_back(d_branch, pieces, pieces_two, at, slope):
        return run(
            functools.partial(mlp_back_kernel, split, at, len(pieces), len(pieces_two)),
            d_branch + pieces + pieces_two + [slope],
            [bf16(group, inner), f32(1, inner)] + deep_shapes,
            specs=[anywhere()] * (4 + len(pieces) + len(pieces_two)) + [whole()],
            scratch=scratch(D, *mlp_rooms),
            flops=mlp_flops,
        )

    def left(index, own, x):
        return run(
            leave_kernel,
            list(own) + [biases[index][3], x, modulations[index]],
            [f32(count, D), bf16(count, D)],
        )

    def opened_back(index, grad, branch):
        return run(
            open_back_kernel, [grad, branch, modulations[index]], [bf16(count, D), f32(2, D)]
        )

    def middle_back(index, own, grad, x, branch):
        return run(
            middle_back_kernel,
            list(own) + [grad, x, branch, modulations[index], order_mlp],
            [bf16(count, D), f32(count, D), f32(4, D)],
        )

    def closed_back(index, own, grad, x, out_type):
        return run(
            close_back_kernel,
            list(own) + [grad, x, modulations[index], order],
            [jax.ShapeDtypeStruct((count, D), out_type), f32(2, D)],
        )

    def vector_sums(sums_one, sums_mid, sums_two, d_bias_qkv, d_bias_one):
        return run(
            functools.partial(vector_kernel, n_seq, rows),
            [sums_one, sums_mid, sums_two, d_bias_qkv, d_bias_one],
            [f32(1, 10 * D + FF), f32(6, D)],
        )

    x_zero = tokens.reshape(-1, D)
    hidden, one_parts, two_parts = lane.tick((opened(x_zero, 0), one_parts, two_parts))
    one_parts = exchange(one_parts.reshape(n_dp, 2 * room, inner), "x").reshape(n_dp, 2, room, inner)
    hidden_zero, one_parts, two_parts, qkv_parts, out_parts = lane.tick(
        (gather_four(hidden, "y"), one_parts, two_parts, qkv_parts, out_parts)
    )
    two_zero = [lax.all_gather(two_parts[0], ("z", "y"))]
    piece = one_parts[:, 0].reshape(split, inner)
    later = jnp.concatenate([one_parts[:, 1].reshape(split, inner), two_parts[1]])
    hidden_zero, piece, later, second = lane.tick((hidden_zero, piece, later, attention_piece(1)))
    mlp_job = Gather([piece], "y", 1)
    lane.jobs.append(mlp_job)
    lane.issue()
    hidden_zero = lane.until(attention_job, hidden_zero)
    attention_zero = attention_job.pieces(0)
    packed_zero, mixed_zero, probs_zero, *partial = attention(0, hidden_zero, attention_zero)
    next_job = Gather([second], "x", 1)
    lane.jobs.append(next_job)
    partial = lane.tick(partial)
    own = lane.tick(scatter_four(partial, "y"))
    branch_zero, middle_zero, hidden = middle(0, own, x_zero)
    inside_zero, later = lane.until(mlp_job, lane.tick((gather_four(hidden, "x"), later)))
    mlp_one = [lax.all_gather(later, ("z", "y"))]
    mlp_zero = mlp_job.pieces(0)
    active_zero, slope_zero, *partial = mlp(0, inside_zero, mlp_zero, two_zero, 0)
    own = lane.tick(scatter_four(lane.tick(partial), "x"))
    end_zero, result = left(0, own, middle_zero)

    x_one = lane.tick(regroup(result))
    hidden_one = lane.until(next_job, lane.tick(gather_four(opened(x_one, 1), "y")))
    attention_one = next_job.pieces(0)
    packed_one, mixed_one, probs_one, *partial = attention(1, hidden_one, attention_one)
    partial, d_out = lax.optimization_barrier((partial, d_out))
    grad_places = regroup(d_out.reshape(-1, D))
    branch_one, middle_one, hidden = middle(1, scatter_four(partial, "y"), x_one)
    inside_one, grad_places = lax.optimization_barrier((gather_four(hidden, "x"), grad_places))
    active_one, slope_one, *partial = mlp(1, inside_one, mlp_one, mlp_one, split)
    end_one, result = left(1, scatter_four(partial, "x"), middle_one)
    output = regroup(result).astype(jnp.float32)

    d_end, sums_two = opened_back(1, grad_places, end_one)
    d_end = gather_four(d_end, "x")
    d_inner, d_bias_one, *partial = mlp_back(d_end, mlp_one, mlp_one, split, slope_one)
    partial, output = lax.optimization_barrier((partial, output))
    owned = {}

    def keep(name):
        return functools.partial(owned.__setitem__, name)

    (d_mlp,) = factor(
        [([(inside_one, [d_inner], split), ([active_one], d_end, half)], None)]
    )
    own, d_mlp = lax.optimization_barrier((scatter_four(partial, "x"), d_mlp))
    d_mlp_one = lax.psum_scatter(d_mlp, ("z", "y"), scatter_dimension=0, tiled=True)
    d_branch, grad_mid, sums_mid = middle_back(1, own, grad_places, middle_one, branch_one)
    d_branch_one = gather_four(d_branch, "y")
    d_packed, d_bias_qkv, *partial = attention_back(
        1, d_branch_one, attention_one, packed_one, probs_one
    )
    (ring,) = factor(
        [([(hidden_one, [d_packed], split), ([mixed_one], d_branch_one, out_room)], "x")]
    )
    own, ring = lax.optimization_barrier((scatter_four(partial, "y"), ring))
    grad, sums_one = closed_back(1, own, grad_mid, x_one, jnp.bfloat16)
    vector_one, modulation_one = vector_sums(sums_one, sums_mid, sums_two, d_bias_qkv, d_bias_one)

    def finish_mlp(totals):
        total = totals[0]
        ones = jnp.concatenate(
            [x[:split].astype(jnp.bfloat16).reshape(n_dp, room, -1) for x in (total, d_mlp_one)],
            axis=1,
        )
        (joined,) = run(
            functools.partial(join_kernel, half, n_seq, room),
            [exchange(ones, "x")],
            [f32(2, rows, FF)],
        )
        owned["one"] = joined.reshape(2, -1)
        owned["two"] = jnp.stack([total[split:], d_mlp_one[split:].astype(jnp.float32)]).reshape(2, -1)

    def finish_attention(totals):
        pair = (totals[0], owned["attention later"][0])
        both = jnp.concatenate(
            [x[:split].astype(jnp.bfloat16).reshape(n_dp, room, -1) for x in pair], axis=1
        )
        both = exchange(both, "y").reshape(n_dp, 2, room, packed_width)[:, :, :rows]
        values = both[..., :wide].reshape(n_dp, 2, rows, n_seq, out_room)[..., :rows]
        joined = jnp.stack(
            [
                both[..., wide : wide + width],
                both[..., wide + narrow : wide + narrow + width],
                values.reshape(n_dp, 2, rows, width),
            ]
        )
        owned["qkv"] = joined.transpose(2, 3, 0, 1, 4).astype(jnp.float32).reshape(2, -1)
        owned["out"] = jnp.stack(
            [x[split : split + rows].astype(jnp.float32) for x in pair]
        ).reshape(2, -1)

    grad_frames, ring = lax.optimization_barrier((regroup(grad), ring))
    lane.add(*ring, "x", (2, 2), keep("attention later"))
    d_end, sums_two = opened_back(0, grad_frames, end_zero)
    d_end = lane.tick(gather_four(d_end, "x"))
    d_inner, d_bias_one, *partial = mlp_back(d_end, mlp_zero, two_zero, 0, slope_zero)
    partial = lane.tick(partial)
    (ring,) = factor(
        [([(inside_zero, [d_inner], split), ([active_zero], d_end, half)], "y")]
    )
    lane.add(*ring, "y", (1, 1), finish_mlp)
    own = lane.tick(scatter_four(partial, "x"))
    d_branch, grad_mid, sums_mid = middle_back(0, own, grad_frames, middle_zero, branch_zero)
    d_branch = lane.tick(gather_four(d_branch, "y"))
    d_packed, d_bias_qkv, *partial = attention_back(
        0, d_branch, attention_zero, packed_zero, probs_zero
    )
    partial = lane.tick(partial)
    (ring,) = factor(
        [([(hidden_zero, [d_packed], split), ([mixed_zero], d_branch, out_room)], "x")]
    )
    lane.add(*ring, "x", (1, 1), finish_attention)
    lane.extra.append((ring, d_mlp_one))
    own = scatter_four(partial, "y")
    lane.tick(())
    own = lane.tick(own)
    d_tokens, sums_one = closed_back(0, own, grad_mid, x_zero, jnp.float32)
    vector_zero, modulation_zero = vector_sums(sums_one, sums_mid, sums_two, d_bias_qkv, d_bias_one)

    lane.scripts += [
        [scatter_vectors(jnp.concatenate([vector_zero, vector_one]), n_dp, n_seq, keep("vectors")), None],
        [sum_seq(modulation_zero + modulation_one, keep("cond")), None],
    ]
    while lane.jobs or lane.scripts:
        lane.tick(())
    return (
        output.reshape(tokens.shape),
        d_tokens.reshape(tokens.shape),
        owned["cond"][None],
        *[owned[name] for name in ("qkv", "out", "one", "two")],
        owned["vectors"],
    )


def on_device(tokens, cond, d_out, attn_in, attn_out, mlp_in, mlp_out, vectors):
    shards = (attn_in, attn_out, mlp_in, mlp_out, vectors)
    widths = (
        attn_in.shape[1],
        attn_out.shape[1],
        mlp_in.shape[1],
        mlp_out.shape[1],
        vectors.shape[1],
    )
    layer_zero = unpack(fetch_forward(shards, 0))
    spatial_out, stored_zero = layer_forward(tokens.astype(jnp.float32), cond, layer_zero, False)
    by_place = lax.all_to_all(
        spatial_out.astype(jnp.bfloat16), "seq", split_axis=2, concat_axis=1, tiled=True
    ).astype(spatial_out.dtype)
    layer_one = unpack(fetch_forward(shards, 1))
    temporal_out, stored_one = layer_forward(by_place, cond, layer_one, True)
    output = lax.all_to_all(
        temporal_out.astype(jnp.bfloat16), "seq", split_axis=1, concat_axis=2, tiled=True
    ).astype(temporal_out.dtype)
    grad_places = lax.all_to_all(d_out, "seq", split_axis=2, concat_axis=1, tiled=True).astype(
        jnp.float32
    )
    grad_mid, factors_one, modul_one = layer_backward(grad_places, stored_one, layer_one, True)
    owned_one = reduce_grads(factors_one, widths)
    grad_frames = lax.all_to_all(
        grad_mid.astype(jnp.bfloat16), "seq", split_axis=1, concat_axis=2, tiled=True
    ).astype(grad_mid.dtype)
    d_tokens, factors_zero, modul_zero = layer_backward(grad_frames, stored_zero, layer_zero, False)
    owned_zero = reduce_grads(factors_zero, widths)
    d_cond = lax.psum(modul_zero + modul_one, "seq")
    stacked = tuple((jnp.stack([former, latter]) for former, latter in zip(owned_zero, owned_one)))
    return (output, d_tokens, d_cond, stacked[0], stacked[1], stacked[2], stacked[3], stacked[4])


def solution(mesh):
    n_dp, n_seq = mesh.shape["dp"], mesh.shape["seq"]
    split = n_dp == 4 and n_seq == 8
    clips, frames = "dp", "seq"
    if split:
        devices = mesh.devices.reshape(n_dp // 2, 2, n_seq // 2, 2)
        mesh = jax.sharding.Mesh(devices, ("y", "core", "z", "x"))
        clips, frames = ("y", "core"), ("z", "x")
    everyone = P(None, ("y", "core", "z", "x") if split else ("dp", "seq"))
    tokens, cond = P(clips, frames, None, None), P(clips, None, None)
    return jax.shard_map(
        on_device_split if split else on_device,
        mesh=mesh,
        in_specs=(tokens, cond, tokens) + (everyone,) * 5,
        out_specs=(tokens, tokens, cond) + (everyone,) * 5,
        check_vma=False,
    )
```
